32 devices in a mesh: dp: 8 (over y, x, core), seq: 4 (over z).
Axes of the slice: x: 2, y: 2, z: 4, core: 2. Of those that a mesh axis runs over, the one named last changes fastest.
Arguments:
- char_ids: int32 [8, 512, 50], P('dp', 'seq'), may hold values from 0 to 261
- segment_ids: int32 [8, 512], P('dp'), may hold values from 0 to 3, never falling along the last dimension, each value on 1 to 256 neighbouring positions
- pad_mask: int32 [8, 512], P('dp'), may hold values 0 or 1
- cotangent: bfloat16 [8, 512, 768], P('dp', 'seq'), may hold values from -6 to 6
- char_table: bfloat16 [262, 16], replicated, may hold values from -6 to 6
- conv_weight: bfloat16 [7, 16, 2048], replicated, may hold values from -0.5 to 0.5
- conv_bias: bfloat16 [2048], replicated, may hold values from -2 to 2
- hw_weight: bfloat16 [2, 2048, 4096], P(None, 'dp'), may hold values from -0.125 to 0.125
- hw_bias: bfloat16 [2, 4096], P(None, 'dp'), may hold values from -3 to 3
- proj_weight: bfloat16 [2048, 768], P('dp'), may hold values from -0.125 to 0.125
- pos_table: bfloat16 [512, 768], P(None, 'dp'), may hold values from -6 to 6
- qkv_weight: bfloat16 [768, 2304], P('dp'), may hold values from -0.3125 to 0.3125
- out_weight: bfloat16 [768, 768], P('dp'), may hold values from -0.875 to 0.875
- ff_in_weight: bfloat16 [768, 3072], P('dp'), may hold values from -0.21875 to 0.21875
- ff_out_weight: bfloat16 [3072, 768], P('dp'), may hold values from -0.109375 to 0.109375
- ff_in_bias: bfloat16 [3072], P('dp'), may hold values from -2 to 2
- d_biases: bfloat16 [5, 768], P(None, 'dp'), may hold values from -2 to 2
- norm_gain: bfloat16 [3, 768], P(None, 'dp'), may hold values from 0.5 to 1.5
- norm_shift: bfloat16 [3, 768], P(None, 'dp'), may hold values from -2 to 2
Outputs:
- output: bfloat16 [8, 512, 768], P('dp', 'seq')
- char_table_grad: float32 [262, 16], replicated
- conv_weight_grad: float32 [7, 16, 2048], replicated
- conv_bias_grad: float32 [2048], replicated
- hw_weight_grad: float32 [2, 2048, 4096], P(None, 'dp')
- hw_bias_grad: float32 [2, 4096], P(None, 'dp')
- proj_weight_grad: float32 [2048, 768], P('dp')
- pos_table_grad: float32 [512, 768], P(None, 'dp')
- qkv_weight_grad: float32 [768, 2304], P('dp')
- out_weight_grad: float32 [768, 768], P('dp')
- ff_in_weight_grad: float32 [768, 3072], P('dp')
- ff_out_weight_grad: float32 [3072, 768], P('dp')
- ff_in_bias_grad: float32 [3072], P('dp')
- d_biases_grad: float32 [5, 768], P(None, 'dp')
- norm_gain_grad: float32 [3, 768], P(None, 'dp')
- norm_shift_grad: float32 [3, 768], P(None, 'dp')
The draws below stay inside these ranges and needn't reach their ends.
Inputs may be any that keep to these rules, and one draw needn't show every extreme that they name: `segment_ids`: segment numbers never fall along a row; one segment spans 1 to 256 words.
All inputs are finite; a program needn't handle non-finite values. No bound on the sum of `pad_mask` on one device may be relied on, other than what follows from the above.
Results may differ from the reference program's by a relative error of at most 0.028.
The reference program's roundings to bfloat16 on the way count: a program that leaves them out, or rounds other values in their place, can miss the bound.
Values may be sent and summed in bfloat16 or wider, within the bound.
No kernel may reach another device: no remote copies, remote signals or barrier semaphores. Data moves between devices by JAX's collectives and lax.ppermute only.
A program may use at most 448 MiB of HBM per device.

```python
import math
import jax
import jax.numpy as jnp
import numpy as np
from jax import lax

CHARS = 262
CDIM = 16
NF = 2048
HWL = 2
D = 768
HEADS = 12
HDIM = 64
FF = 3072
CLEN = 50
KMAX = 7
L = 512
ROWS = 8


def with_ends(drawn, stream_key, smallest, top_value):
    index_at = [jax.random.randint(jax.random.fold_in(stream_key, axis), (), 0, length) for axis, length in enumerate(drawn.shape)]
    widest = drawn.shape.index(max(drawn.shape))
    beside = index_at[:widest] + [(index_at[widest] + 1) % drawn.shape[widest]] + index_at[widest + 1:]
    return drawn.at[tuple(index_at)].set(smallest).at[tuple(beside)].set(top_value)


def block_levels(key, dims, pieces, least, high):
    def one(axis_at, blocks):
        draws = jax.random.uniform(jax.random.fold_in(jax.random.fold_in(key, 6), axis_at), (blocks,), jnp.float32, least / len(pieces), high / len(pieces))
        return jnp.repeat(jnp.exp(draws), dims[axis_at] // blocks).reshape((-1,) + (1,) * (len(dims) - axis_at - 1))

    gain = one(*pieces[0])
    for cut in pieces[1:]:
        gain = gain * one(*cut)
    return gain


def profile(count, total, bound, lean):
    portions = [(1 << 20) // math.isqrt(grade ** lean) + 1 for grade in range(2, count + 1)]
    rest, holding = total - bound - (count - 1), [1] * (count - 1)
    while rest > 0:
        candidates = [i for i in range(count - 1) if holding[i] < bound]
        pool, budget = sum([portions[i] for i in candidates]), rest
        for i in candidates:
            extra = min(bound - holding[i], max(1, budget * portions[i] // pool), rest)
            holding[i] = holding[i] + extra
            rest = rest - extra
    return np.array([bound] + holding)


def ragged_sizes(stream_key, amount, total, most, lean):
    if amount == 2:
        one = jax.random.randint(stream_key, (), max(1, total - most), min(most, total - 1) + 1)
        return jnp.stack([one, total - one])
    lengths = jnp.asarray(profile(amount, total, most, lean), jnp.int32)
    couples = (amount - 1) // 2
    source_of, receiver = lengths[1:1 + 2 * couples:2], lengths[2:2 + 2 * couples:2]
    margin = jnp.minimum(source_of - 1, most - receiver)
    passed = jax.random.randint(jax.random.fold_in(stream_key, 1), (couples,), 0, 1 << 20) % (margin + 1)
    lengths = lengths.at[1:1 + 2 * couples:2].set(source_of - passed).at[2:2 + 2 * couples:2].set(receiver + passed)
    return lengths[jax.random.permutation(jax.random.fold_in(stream_key, 2), amount)]


def noise(rng, dims, scale, limit, pieces=(), dtype=jnp.bfloat16):
    drawn = jax.random.normal(rng, dims, jnp.float32) * scale
    if len(pieces) > 0:
        drawn = block_levels(rng, dims, pieces, -0.22, 0.18) * drawn
    return jnp.clip(drawn, min=-limit, max=limit).astype(dtype)


def setup_inputs(seed: int = 0) -> dict:
    streams_of = jax.random.split(jax.random.key(seed), 20)
    char_ids = with_ends(jax.random.randint(streams_of[0], (ROWS, L, CLEN), 0, CHARS), jax.random.fold_in(streams_of[0], 1), 0, CHARS - 1).astype(jnp.int32)
    segment_ids = jax.vmap(lambda own: jnp.searchsorted(jnp.cumsum(ragged_sizes(own, 4, L, L // 2, 0)), jnp.arange(L), side="right"))(jax.random.split(streams_of[1], ROWS)).reshape((ROWS, L)).astype(jnp.int32)
    pad_mask = with_ends((jax.random.randint(streams_of[2], (ROWS, L), 0, 8) < 1).astype(jnp.int32), jax.random.fold_in(streams_of[2], 1), 0, 1)
    cotangent = noise(streams_of[3], (ROWS, L, D), 1.0, 6.0, ((0, 8), (1, 4)))
    char_table = noise(streams_of[4], (CHARS, CDIM), 1.0, 6.0)
    conv_weight = noise(streams_of[5], (KMAX, CDIM, NF), (KMAX * CDIM) ** -0.5, 0.5)
    conv_bias = noise(streams_of[6], (NF,), 0.3, 2.0)
    hw_weight = noise(streams_of[7], (HWL, NF, 2 * NF), NF ** -0.5, 0.125, ((1, 8),))
    hw_bias = noise(streams_of[8], (HWL, 2 * NF), 0.5, 3.0, ((1, 8),))
    proj_weight = noise(streams_of[9], (NF, D), NF ** -0.5, 0.125, ((0, 8),))
    pos_table = noise(streams_of[10], (L, D), 1.0, 6.0, ((1, 8),))
    qkv_weight = noise(streams_of[11], (D, 3 * D), (D // 2) ** -0.5, 0.3125, ((0, 8),))
    out_weight = noise(streams_of[12], (D, D), (D // 16) ** -0.5, 0.875, ((0, 8),))
    ff_in_weight = noise(streams_of[13], (D, FF), D ** -0.5, 0.21875, ((0, 8),))
    ff_out_weight = noise(streams_of[14], (FF, D), FF ** -0.5, 0.109375, ((0, 8),))
    ff_in_bias = noise(streams_of[15], (FF,), 0.3, 2.0, ((0, 8),))
    d_biases = noise(streams_of[16], (5, D), 0.3, 2.0, ((1, 8),))
    norm_gain = jnp.clip(1.0 + 0.1 * jax.random.normal(streams_of[17], (3, D), jnp.float32), 0.5, 1.5).astype(jnp.bfloat16)
    norm_shift = noise(streams_of[18], (3, D), 0.3, 2.0, ((1, 8),))
    return {"char_ids": char_ids, "segment_ids": segment_ids, "pad_mask": pad_mask, "cotangent": cotangent, "char_table": char_table, "conv_weight": conv_weight, "conv_bias": conv_bias, "hw_weight": hw_weight, "hw_bias": hw_bias, "proj_weight": proj_weight, "pos_table": pos_table, "qkv_weight": qkv_weight, "out_weight": out_weight, "ff_in_weight": ff_in_weight, "ff_out_weight": ff_out_weight, "ff_in_bias": ff_in_bias, "d_biases": d_biases, "norm_gain": norm_gain, "norm_shift": norm_shift}


@jax.custom_vjp
def low(v):
    return lax.optimization_barrier(v.astype(jnp.bfloat16)).astype(jnp.float32)

@jax.custom_vjp
def low_back(v):
    return v

def low_keep(v):
    return (low(v), None)

def low_pass(kept, grad):
    return (grad,)

def back_keep(v):
    return (v, None)

def back_low(kept, grad):
    return (low(grad),)
low.defvjp(low_keep, low_pass)
low_back.defvjp(back_keep, back_low)
eps_norm = 1e-12
masked_score = -1e+30
width_shares = (1, 1, 2, 4, 8, 16, 32)

def filter_widths(filters):
    per_share = filters // 64
    return np.repeat(np.arange(1, len(width_shares) + 1), [per_share * share_count for share_count in width_shares])

def layer_norm(inputs, gain_row, shift_row):
    centred = inputs - lax.optimization_barrier(jnp.mean(inputs, axis=-1, keepdims=True))
    spread = lax.optimization_barrier(jnp.mean(centred * centred, axis=-1, keepdims=True))
    return centred * lax.rsqrt(spread + eps_norm) * gain_row + shift_row

def highway_mix(gate_values, carried):
    filters = carried.shape[-1]
    opened = jax.nn.sigmoid(gate_values[:, filters:])
    return opened * carried + (1.0 - opened) * jax.nn.relu(gate_values[:, :filters])

def gelu_exact(inputs):
    return jax.nn.gelu(inputs, approximate=False)

def matmul_high(left_side, right_side):
    return jnp.dot(left_side, right_side, precision=lax.Precision.HIGHEST)

def reference(char_ids, segment_ids, pad_mask, cotangent, char_table, conv_weight, conv_bias, hw_weight, hw_bias, proj_weight, pos_table, qkv_weight, out_weight, ff_in_weight, ff_out_weight, ff_in_bias, d_biases, norm_gain, norm_shift):
    params = tuple((array.astype(jnp.float32) for array in (char_table, conv_weight, conv_bias, hw_weight, hw_bias, proj_weight, pos_table, qkv_weight, out_weight, ff_in_weight, ff_out_weight, ff_in_bias, d_biases, norm_gain, norm_shift)))
    widths = filter_widths(NF)
    tap_mask = jnp.asarray(np.arange(KMAX)[:, None] < widths[None, :], jnp.float32)[:, None, :]
    valid_place = jnp.asarray(np.arange(CLEN)[:, None] <= CLEN - widths[None, :])
    group_size = math.gcd(ROWS, max(1, 4096 // L))
    word_block = math.gcd(group_size * L, 256)
    group_count = ROWS // group_size
    score_scale = HDIM ** (-0.5)

    def forward(param_set, group_ids, group_segs, group_pads):
        char_rows, conv_kernel, conv_shift, hw_kernel, hw_shift, proj_kernel, pos_rows, qkv_kernel, out_kernel, inner_kernel, outer_kernel, inner_shift, bias_rows, gain_rows, shift_rows = param_set
        masked_kernel = conv_kernel * tap_mask

        def embed_block(block_ids):
            vectors = low_back(char_rows[block_ids])
            padded = jnp.pad(vectors, ((0, 0), (0, KMAX - 1), (0, 0)))
            char_taps = jnp.stack([padded[:, tap_index:tap_index + CLEN, :] for tap_index in range(KMAX)], axis=2)
            conv_out = low_back(jnp.einsum('btkc,kcf->btf', char_taps, masked_kernel, precision=lax.Precision.HIGHEST) + conv_shift)
            conv_out = jnp.where(valid_place[None], conv_out, masked_score)
            return jax.nn.relu(lax.optimization_barrier(jnp.max(conv_out, axis=1)))
        seq_count = group_ids.shape[0]
        word_count = seq_count * L
        hidden = lax.map(jax.checkpoint(embed_block), group_ids.reshape(word_count // word_block, word_block, CLEN)).reshape(word_count, NF)
        for highway_layer in range(HWL):
            gate_values = low_back(matmul_high(low(hidden), hw_kernel[highway_layer]) + hw_shift[highway_layer])
            hidden = highway_mix(gate_values, hidden)
        projected = low_back(matmul_high(low(hidden), proj_kernel) + bias_rows[0])
        summed = (projected.reshape(seq_count, L, D) + pos_rows[None]).reshape(word_count, D)
        embedded = layer_norm(summed, gain_rows[0], shift_rows[0])
        qkv_shift = jnp.concatenate([bias_rows[1], jnp.zeros_like(bias_rows[1]), bias_rows[2]])
        qkv = low(low_back(matmul_high(low(embedded), qkv_kernel) + qkv_shift))
        queries = qkv[:, :D].reshape(seq_count, L, HEADS, HDIM)
        keys = qkv[:, D:2 * D].reshape(seq_count, L, HEADS, HDIM)
        values = qkv[:, 2 * D:].reshape(seq_count, L, HEADS, HDIM)
        positions = jnp.arange(L)
        allowed = (group_segs[:, :, None] == group_segs[:, None, :]) & ((group_pads[:, None, :] == 0) | (positions[:, None] == positions[None, :])[None])
        scores = low_back(jnp.einsum('sqhd,skhd->shqk', queries, keys, precision=lax.Precision.HIGHEST) * score_scale)
        scores = jnp.where(allowed[:, None], scores, masked_score)
        attn_probs = low(jax.nn.softmax(scores, axis=-1))
        attended = low(low_back(jnp.einsum('shqk,skhd->sqhd', attn_probs, values, precision=lax.Precision.HIGHEST).reshape(word_count, D)))
        attn_out = low_back(matmul_high(attended, out_kernel) + bias_rows[3])
        first_norm = layer_norm(embedded + attn_out, gain_rows[1], shift_rows[1])
        ffn_up = low_back(matmul_high(low(first_norm), inner_kernel) + inner_shift)
        ffn_down = low_back(matmul_high(low(gelu_exact(ffn_up)), outer_kernel) + bias_rows[4])
        return layer_norm(first_norm + ffn_down, gain_rows[2], shift_rows[2])

    def one_group(running, inputs):
        group_ids, group_segs, group_pads, group_cot = inputs
        group_out, pullback = jax.vjp(lambda param_set: forward(param_set, group_ids, group_segs, group_pads), params)
        group_grads = pullback(group_cot.reshape(-1, D))[0]
        return (jax.tree.map(jnp.add, running, group_grads), group_out)
    zero_grads = jax.tree.map(jnp.zeros_like, params)
    inputs = (char_ids.reshape(group_count, group_size, L, CLEN), segment_ids.reshape(group_count, group_size, L), pad_mask.reshape(group_count, group_size, L), cotangent.astype(jnp.float32).reshape(group_count, group_size, L, D))
    totals, outputs = lax.scan(one_group, zero_grads, inputs)
    output = outputs.reshape(ROWS, L, D).astype(jnp.bfloat16)
    return (output, totals[0], totals[1], totals[2], totals[3], totals[4], totals[5], totals[6], totals[7], totals[8], totals[9], totals[10], totals[11], totals[12], totals[13], totals[14])
```

```python
import functools
import math

import jax
import jax.numpy as jnp
import numpy as np
from jax import lax
from jax.experimental import pallas as pl
from jax.experimental.pallas import tpu as pltpu
from jax.sharding import PartitionSpec as P

HDIM = 64


eps_norm = 1e-12
masked_score = -1e30
width_shares = (1, 1, 2, 4, 8, 16, 32)


def filter_widths(filters):
    per_share = filters // 64
    return np.repeat(
        np.arange(1, len(width_shares) + 1),
        [per_share * share_count for share_count in width_shares],
    )


def layer_norm(inputs, gain_row, shift_row):
    centred = inputs - jnp.mean(inputs, axis=-1, keepdims=True)
    spread = jnp.mean(centred * centred, axis=-1, keepdims=True)
    return centred * lax.rsqrt(spread + eps_norm) * gain_row + shift_row


def highway_mix(gate_values, carried):
    filters = carried.shape[-1]
    opened = jax.nn.sigmoid(gate_values[:, filters:])
    return opened * carried + (1.0 - opened) * jax.nn.relu(gate_values[:, :filters])


def gelu_exact(inputs):
    return jax.nn.gelu(inputs, approximate=False)


def product(left_side, right_side):
    return jnp.dot(left_side, right_side, preferred_element_type=jnp.float32)


def product_tn(left_side, right_side):
    return lax.dot_general(
        left_side, right_side, (((0,), (0,)), ((), ())), preferred_element_type=jnp.float32
    )


def product_nt(left_side, right_side):
    return lax.dot_general(
        left_side, right_side, (((1,), (1,)), ((), ())), preferred_element_type=jnp.float32
    )


def char_windows(word_ids, char_rows, tap_count):
    word_count, char_len = word_ids.shape
    char_count = char_rows.shape[0]
    onehot = (
        word_ids.reshape(-1)[:, None] == jnp.arange(char_count, dtype=jnp.int32)[None, :]
    ).astype(jnp.bfloat16)
    vectors = product(onehot, char_rows).astype(jnp.bfloat16).reshape(word_count, char_len, -1)
    padded = jnp.pad(vectors, ((0, 0), (0, tap_count - 1), (0, 0)))
    char_taps = jnp.stack(
        [padded[:, tap_index : tap_index + char_len, :] for tap_index in range(tap_count)], axis=2
    )
    return (onehot, char_taps.reshape(word_count * char_len, -1))


def shards(
    char_ids,
    segment_ids,
    pad_mask,
    cotangent,
    char_table,
    conv_weight,
    conv_bias,
    hw_weight,
    hw_bias,
    proj_weight,
    pos_table,
    qkv_weight,
    out_weight,
    ff_in_weight,
    ff_out_weight,
    ff_in_bias,
    d_biases,
    norm_gain,
    norm_shift,
):
    (
        highway_full,
        highway_bias,
        proj_full,
        pos_full,
        qkv_full,
        out_full,
        inner_full,
        outer_full,
        inner_bias,
        bias_full,
        gain_full,
        shift_full,
    ) = (
        lax.all_gather(hw_weight, "dp", axis=1, tiled=True),
        lax.all_gather(hw_bias, "dp", axis=1, tiled=True),
        lax.all_gather(proj_weight, "dp", axis=0, tiled=True),
        lax.all_gather(pos_table, "dp", axis=1, tiled=True),
        lax.all_gather(qkv_weight, "dp", axis=0, tiled=True),
        lax.all_gather(out_weight, "dp", axis=0, tiled=True),
        lax.all_gather(ff_in_weight, "dp", axis=0, tiled=True),
        lax.all_gather(ff_out_weight, "dp", axis=0, tiled=True),
        lax.all_gather(ff_in_bias, "dp", axis=0, tiled=True),
        lax.all_gather(d_biases, "dp", axis=1, tiled=True),
        lax.all_gather(norm_gain, "dp", axis=1, tiled=True),
        lax.all_gather(norm_shift, "dp", axis=1, tiled=True),
    )
    seqs_here, local_len, char_len = char_ids.shape
    tap_count, char_dim, filters = conv_weight.shape
    model_dim = cotangent.shape[2]
    seq_len = segment_ids.shape[1]
    head_count = model_dim // HDIM
    highway_depth = highway_full.shape[0]
    word_count = seqs_here * local_len
    score_scale = HDIM ** (-0.5)
    bias_rows = bias_full.astype(jnp.float32)
    gain_rows = gain_full.astype(jnp.float32)
    shift_rows = shift_full.astype(jnp.float32)
    widths = filter_widths(filters)
    tap_mask = np.arange(tap_count)[:, None] < widths[None, :]
    masked_kernel = (conv_weight * jnp.asarray(tap_mask, jnp.bfloat16)[:, None, :]).reshape(
        tap_count * char_dim, filters
    )
    valid_place = jnp.asarray(np.arange(char_len)[:, None] <= char_len - widths[None, :])
    word_block = math.gcd(word_count, 32)
    block_count = word_count // word_block
    id_blocks = char_ids.reshape(block_count, word_block, char_len)

    def embed_forward(block_ids):
        unused, char_taps = char_windows(block_ids, char_table, tap_count)
        conv_out = (product(char_taps, masked_kernel) + conv_bias.astype(jnp.float32)).reshape(
            word_block, char_len, filters
        )
        conv_out = jnp.where(valid_place[None], conv_out, masked_score)
        return (jnp.max(conv_out, axis=1), jnp.argmax(conv_out, axis=1))

    pooled, top_place = lax.map(embed_forward, id_blocks)
    pooled = pooled.reshape(word_count, filters)
    hidden = jax.nn.relu(pooled)
    carried_list = []
    gates_list = []
    for highway_layer in range(highway_depth):
        carried_list.append(hidden)
        gate_values = product(
            hidden.astype(jnp.bfloat16), highway_full[highway_layer]
        ) + highway_bias[highway_layer].astype(jnp.float32)
        gates_list.append(gate_values)
        hidden = highway_mix(gate_values, hidden)
    top_hidden = hidden.astype(jnp.bfloat16)
    projected = product(top_hidden, proj_full) + bias_rows[0]
    row_start = lax.axis_index("seq") * local_len
    pos_rows = lax.dynamic_slice_in_dim(pos_full, row_start, local_len, 0).astype(jnp.float32)
    summed = (projected.reshape(seqs_here, local_len, model_dim) + pos_rows[None]).reshape(
        word_count, model_dim
    )
    embedded = layer_norm(summed, gain_rows[0], shift_rows[0])
    embedded_b = embedded.astype(jnp.bfloat16)
    qkv_shift = jnp.concatenate([bias_rows[1], jnp.zeros_like(bias_rows[1]), bias_rows[2]])
    qkv = (product(embedded_b, qkv_full) + qkv_shift).astype(jnp.bfloat16)
    queries = qkv[:, :model_dim].reshape(seqs_here, local_len, head_count, HDIM)
    keys_local = qkv[:, model_dim : 2 * model_dim].reshape(seqs_here, local_len, model_dim)
    values_local = qkv[:, 2 * model_dim :].reshape(seqs_here, local_len, model_dim)
    keys_full, values_full = (
        lax.all_gather(keys_local, "seq", axis=1, tiled=True),
        lax.all_gather(values_local, "seq", axis=1, tiled=True),
    )
    query_segs = lax.dynamic_slice_in_dim(segment_ids, row_start, local_len, 1)
    query_pos = row_start + jnp.arange(local_len, dtype=jnp.int32)
    same_segment = query_segs[:, :, None] == segment_ids[:, None, :]
    open_key = (pad_mask[:, None, :] == 0) | (
        query_pos[:, None] == jnp.arange(seq_len, dtype=jnp.int32)[None, :]
    )[None]
    allowed = (same_segment & open_key)[:, None]

    def score_of(key_rows):
        raw_scores = (
            jnp.einsum(
                "sqhd,skhd->shqk",
                queries,
                key_rows.reshape(seqs_here, seq_len, head_count, HDIM),
                preferred_element_type=jnp.float32,
            )
            * score_scale
        )
        return jnp.where(allowed, raw_scores, masked_score)

    scores = score_of(keys_full)
    row_top = jnp.max(scores, axis=-1, keepdims=True)
    exp_scores = jnp.exp(scores - row_top)
    denominator = jnp.sum(exp_scores, axis=-1, keepdims=True)
    attn_probs = (exp_scores / denominator).astype(jnp.bfloat16)
    log_total = row_top + jnp.log(denominator)
    attended = (
        jnp.einsum(
            "shqk,skhd->sqhd",
            attn_probs,
            values_full.reshape(seqs_here, seq_len, head_count, HDIM),
            preferred_element_type=jnp.float32,
        )
        .reshape(word_count, model_dim)
        .astype(jnp.bfloat16)
    )
    attn_out = product(attended, out_full) + bias_rows[3]
    first_input = embedded + attn_out
    first_norm = layer_norm(first_input, gain_rows[1], shift_rows[1])
    first_b = first_norm.astype(jnp.bfloat16)
    ffn_up = product(first_b, inner_full) + inner_bias.astype(jnp.float32)
    ffn_act = gelu_exact(ffn_up).astype(jnp.bfloat16)
    ffn_down = product(ffn_act, outer_full) + bias_rows[4]
    second = first_norm + ffn_down
    result = layer_norm(second, gain_rows[2], shift_rows[2])
    grad_out = cotangent.reshape(word_count, model_dim).astype(jnp.float32)
    unused, norm_back = jax.vjp(layer_norm, second, gain_rows[2], shift_rows[2])
    d_second, gain_grad2, shift_grad2 = norm_back(grad_out)
    grad_down = d_second.astype(jnp.bfloat16)
    outer_grad = product_tn(ffn_act, grad_down)
    bias_grad4 = jnp.sum(grad_down.astype(jnp.float32), axis=0)
    unused, gelu_back = jax.vjp(gelu_exact, ffn_up)
    grad_up = gelu_back(product_nt(grad_down, outer_full))[0].astype(jnp.bfloat16)
    inner_grad = product_tn(first_b, grad_up)
    inner_bias_grad = jnp.sum(grad_up.astype(jnp.float32), axis=0)
    d_first = d_second + product_nt(grad_up, inner_full)
    unused, norm_back = jax.vjp(layer_norm, first_input, gain_rows[1], shift_rows[1])
    d_res, gain_grad1, shift_grad1 = norm_back(d_first)
    grad_attn = d_res.astype(jnp.bfloat16)
    out_grad = product_tn(attended, grad_attn)
    bias_grad3 = jnp.sum(grad_attn.astype(jnp.float32), axis=0)
    grad_attended = (
        product_nt(grad_attn, out_full)
        .astype(jnp.bfloat16)
        .reshape(seqs_here, local_len, head_count, HDIM)
    )
    keys_back, values_back = (keys_full, values_full)
    probs_again = jnp.exp(score_of(keys_back) - log_total)
    probs_again_b = probs_again.astype(jnp.bfloat16)
    key_heads = keys_back.reshape(seqs_here, seq_len, head_count, HDIM)
    value_heads = values_back.reshape(seqs_here, seq_len, head_count, HDIM)
    d_probs = jnp.einsum(
        "sqhd,skhd->shqk", grad_attended, value_heads, preferred_element_type=jnp.float32
    )
    grad_scores = (
        probs_again * (d_probs - jnp.sum(probs_again * d_probs, axis=-1, keepdims=True))
    ).astype(jnp.bfloat16)
    d_queries = (
        jnp.einsum("shqk,skhd->sqhd", grad_scores, key_heads, preferred_element_type=jnp.float32)
        * score_scale
    )
    d_keys_all = (
        jnp.einsum("shqk,sqhd->skhd", grad_scores, queries, preferred_element_type=jnp.float32)
        * score_scale
    )
    d_values_all = jnp.einsum(
        "shqk,sqhd->skhd", probs_again_b, grad_attended, preferred_element_type=jnp.float32
    )
    d_keys, d_values = (
        lax.psum_scatter(
            d_keys_all.reshape(seqs_here, seq_len, model_dim).astype(jnp.bfloat16),
            "seq",
            scatter_dimension=1,
            tiled=True,
        ).astype(jnp.float32),
        lax.psum_scatter(
            d_values_all.reshape(seqs_here, seq_len, model_dim).astype(jnp.bfloat16),
            "seq",
            scatter_dimension=1,
            tiled=True,
        ).astype(jnp.float32),
    )
    grad_qkv = jnp.concatenate(
        [
            d_queries.reshape(word_count, model_dim),
            d_keys.reshape(word_count, model_dim),
            d_values.reshape(word_count, model_dim),
        ],
        axis=1,
    ).astype(jnp.bfloat16)
    qkv_grad = product_tn(embedded_b, grad_qkv)
    bias_grad1 = jnp.sum(grad_qkv[:, :model_dim].astype(jnp.float32), axis=0)
    bias_grad2 = jnp.sum(grad_qkv[:, 2 * model_dim :].astype(jnp.float32), axis=0)
    d_embedded = d_res + product_nt(grad_qkv, qkv_full)
    unused, norm_back = jax.vjp(layer_norm, summed, gain_rows[0], shift_rows[0])
    d_summed, gain_grad0, shift_grad0 = norm_back(d_embedded)
    pos_local = jnp.sum(d_summed.reshape(seqs_here, local_len, model_dim), axis=0)
    pos_grad = lax.dynamic_update_slice_in_dim(
        jnp.zeros((seq_len, model_dim), jnp.float32), pos_local, row_start, 0
    )
    grad_proj = d_summed.astype(jnp.bfloat16)
    proj_grad = product_tn(top_hidden, grad_proj)
    bias_grad0 = jnp.sum(grad_proj.astype(jnp.float32), axis=0)
    d_hidden = product_nt(grad_proj, proj_full)
    kernel_grads = [None] * highway_depth
    shift_grads = [None] * highway_depth
    for highway_layer in reversed(range(highway_depth)):
        carried = carried_list[highway_layer]
        unused, mix_back = jax.vjp(highway_mix, gates_list[highway_layer], carried)
        d_gates, d_carried = mix_back(d_hidden)
        grad_gates = d_gates.astype(jnp.bfloat16)
        kernel_grads[highway_layer] = product_tn(carried.astype(jnp.bfloat16), grad_gates)
        shift_grads[highway_layer] = jnp.sum(grad_gates.astype(jnp.float32), axis=0)
        d_hidden = d_carried + product_nt(grad_gates, highway_full[highway_layer])
    grad_pooled = jnp.where(pooled > 0, d_hidden, 0.0).astype(jnp.bfloat16)

    def embed_backward(running, inputs):
        weight_sum, bias_sum, table_sum = running
        block_ids, place_block, grad_block = inputs
        onehot, char_taps = char_windows(block_ids, char_table, tap_count)
        grad_conv = jnp.where(
            jnp.arange(char_len, dtype=jnp.int32)[None, :, None] == place_block[:, None, :],
            grad_block[:, None, :],
            jnp.zeros((), jnp.bfloat16),
        ).reshape(word_block * char_len, filters)
        weight_sum = weight_sum + product_tn(char_taps, grad_conv)
        bias_sum = bias_sum + jnp.sum(grad_block.astype(jnp.float32), axis=0)
        d_taps = product_nt(grad_conv, masked_kernel).reshape(
            word_block, char_len, tap_count, char_dim
        )
        spread = jnp.zeros((word_block, char_len + tap_count - 1, char_dim), jnp.float32)
        for tap_index in range(tap_count):
            spread = spread.at[:, tap_index : tap_index + char_len].add(d_taps[:, :, tap_index])
        grad_chars = (
            spread[:, :char_len].reshape(word_block * char_len, char_dim).astype(jnp.bfloat16)
        )
        table_sum = table_sum + product_tn(onehot, grad_chars)
        return ((weight_sum, bias_sum, table_sum), None)

    start_sums = (
        jnp.zeros((tap_count * char_dim, filters), jnp.float32),
        jnp.zeros((filters,), jnp.float32),
        jnp.zeros(char_table.shape, jnp.float32),
    )
    conv_sums, unused = lax.scan(
        embed_backward,
        start_sums,
        (id_blocks, top_place, grad_pooled.reshape(block_count, word_block, filters)),
    )
    conv_weight_grad = (
        conv_sums[0] * jnp.asarray(np.repeat(tap_mask, char_dim, axis=0), jnp.float32)
    ).reshape(tap_count, char_dim, filters)
    table_total, conv_total, conv_bias_total = lax.psum(
        (conv_sums[2], conv_weight_grad, conv_sums[1]), ("dp", "seq")
    )
    weight_grads = (
        jnp.stack(kernel_grads),
        jnp.stack(shift_grads),
        proj_grad,
        pos_grad,
        qkv_grad,
        out_grad,
        inner_grad,
        outer_grad,
        inner_bias_grad,
        jnp.stack([bias_grad0, bias_grad1, bias_grad2, bias_grad3, bias_grad4]),
        jnp.stack([gain_grad0, gain_grad1, gain_grad2]),
        jnp.stack([shift_grad0, shift_grad1, shift_grad2]),
    )
    sliced = (
        lax.psum_scatter(weight_grads[0], "dp", scatter_dimension=1, tiled=True),
        lax.psum_scatter(weight_grads[1], "dp", scatter_dimension=1, tiled=True),
        lax.psum_scatter(weight_grads[2], "dp", scatter_dimension=0, tiled=True),
        lax.psum_scatter(weight_grads[3], "dp", scatter_dimension=1, tiled=True),
        lax.psum_scatter(weight_grads[4], "dp", scatter_dimension=0, tiled=True),
        lax.psum_scatter(weight_grads[5], "dp", scatter_dimension=0, tiled=True),
        lax.psum_scatter(weight_grads[6], "dp", scatter_dimension=0, tiled=True),
        lax.psum_scatter(weight_grads[7], "dp", scatter_dimension=0, tiled=True),
        lax.psum_scatter(weight_grads[8], "dp", scatter_dimension=0, tiled=True),
        lax.psum_scatter(weight_grads[9], "dp", scatter_dimension=1, tiled=True),
        lax.psum_scatter(weight_grads[10], "dp", scatter_dimension=1, tiled=True),
        lax.psum_scatter(weight_grads[11], "dp", scatter_dimension=1, tiled=True),
    )
    summed_grads = (
        lax.psum(sliced[0].astype(jnp.bfloat16), "seq").astype(jnp.float32),
        lax.psum(sliced[1].astype(jnp.bfloat16), "seq").astype(jnp.float32),
        lax.psum(sliced[2].astype(jnp.bfloat16), "seq").astype(jnp.float32),
        lax.psum(sliced[3].astype(jnp.bfloat16), "seq").astype(jnp.float32),
        lax.psum(sliced[4].astype(jnp.bfloat16), "seq").astype(jnp.float32),
        lax.psum(sliced[5].astype(jnp.bfloat16), "seq").astype(jnp.float32),
        lax.psum(sliced[6].astype(jnp.bfloat16), "seq").astype(jnp.float32),
        lax.psum(sliced[7].astype(jnp.bfloat16), "seq").astype(jnp.float32),
        lax.psum(sliced[8].astype(jnp.bfloat16), "seq").astype(jnp.float32),
        lax.psum(sliced[9].astype(jnp.bfloat16), "seq").astype(jnp.float32),
        lax.psum(sliced[10].astype(jnp.bfloat16), "seq").astype(jnp.float32),
        lax.psum(sliced[11].astype(jnp.bfloat16), "seq").astype(jnp.float32),
    )
    output = result.astype(jnp.bfloat16).reshape(seqs_here, local_len, model_dim)
    return (output, table_total, conv_total, conv_bias_total) + tuple(summed_grads)


PLANE = 8
DEPTH = 4
CORE_PARTNER = 1
GROUP = 8

f32 = jnp.float32
bf16 = jnp.bfloat16


def swap(value, axis_name, size, offset):
    return lax.ppermute(value, axis_name, [(at, at ^ offset) for at in range(size)])


def plane_swap(value, offset):
    return swap(value, "dp", PLANE, offset)


def plane_gather(block):
    even = [block] + [plane_swap(block, offset) for offset in (2, 4, 6)]
    odd = [plane_swap(piece, CORE_PARTNER) for piece in even]
    return [piece for pair in zip(even, odd) for piece in pair]


def plane_reduce(keep, send):
    arrived = plane_swap(send, CORE_PARTNER)
    total = keep[0].astype(f32) + arrived[0].astype(f32)
    others = [
        plane_swap((keep[i].astype(f32) + arrived[i].astype(f32)).astype(bf16), 2 * i)
        for i in range(1, PLANE // 2)
    ]
    for piece in others:
        total = total + piece.astype(f32)
    return total


def line_total(block):
    first = lax.ppermute(block, "seq", [(0, 1), (3, 2)])
    paired = block + first
    second = lax.ppermute(paired, "seq", [(1, 2), (2, 1)])
    whole = paired + second
    return whole, lax.ppermute(whole, "seq", [(1, 0), (2, 3)])


def line_sum(block):
    whole, third = line_total(block)
    place = lax.axis_index("seq")
    return jnp.where((place == 1) | (place == 2), whole, third)


def nn(left_side, right_side):
    return jnp.dot(left_side, right_side, preferred_element_type=f32)


def nt(left_side, right_side):
    return lax.dot_general(
        left_side, right_side, (((1,), (1,)), ((), ())), preferred_element_type=f32
    )


def tn(left_side, right_side):
    return lax.dot_general(
        left_side, right_side, (((0,), (0,)), ((), ())), preferred_element_type=f32
    )


VMEM = pltpu.VMEM
SMEM_SPEC = pl.BlockSpec(memory_space=pltpu.SMEM)


def whole(count):
    return [pl.BlockSpec(memory_space=pltpu.VMEM)] * count


def call(body, out_shapes, scalar, operands, scratch=(), name=None):
    return pl.pallas_call(
        body,
        out_shape=[jax.ShapeDtypeStruct(s, t) for s, t in out_shapes],
        in_specs=[SMEM_SPEC] + whole(len(operands)),
        out_specs=whole(len(out_shapes)),
        scratch_shapes=list(scratch),
        name=name,
        compiler_params=pltpu.CompilerParams(vmem_limit_bytes=58 * 1024 * 1024),
    )(scalar, *operands)


def lookup_body(char_len, d_ref, ids_ref, table_ref, extra_ref, x_ref):
    words = ids_ref.shape[0]
    rows, lanes = table_ref.shape
    width = lanes // GROUP
    groups = x_ref.shape[1] // lanes
    lane = lax.broadcasted_iota(jnp.int32, (rows, lanes), 1) // width
    entry = lax.broadcasted_iota(jnp.int32, (words, rows), 1)
    total = jnp.zeros((groups * words, lanes), f32)
    for place in range(GROUP):
        pieces = []
        for group in range(groups):
            at = GROUP * group + place
            if at < char_len:
                hit = ids_ref[:, at : at + 1] == entry
                pieces.append(jnp.where(hit, 1.0, 0.0).astype(bf16))
            else:
                pieces.append(jnp.zeros((words, rows), bf16))
        own = jnp.where(lane == place, table_ref[...].astype(f32), 0.0).astype(bf16)
        total = total + nn(jnp.concatenate(pieces, axis=0), own)
    for group in range(groups):
        x_ref[:words, group * lanes : (group + 1) * lanes] = total[
            group * words : (group + 1) * words
        ].astype(bf16)
    x_ref[words:, :] = extra_ref[...]


def fill_taps(taps_ref, weight_ref):
    depth, filters = weight_ref.shape
    char_dim = taps_ref.shape[0] // (2 * GROUP)
    taps_ref[...] = jnp.zeros_like(taps_ref)
    for place in range(GROUP):
        taps_ref[
            place * char_dim : place * char_dim + depth, place * filters : (place + 1) * filters
        ] = weight_ref[...]


def conv_body(char_len, first_masked, words, d_ref, *refs):
    blocks = refs[:PLANE]
    (weight_ref, last_ref, bias_ref, h_ref, hb_ref, at_ref, x_ref, ba_ref, bb_ref) = refs[
        PLANE : PLANE + 9
    ]
    taps_ref, extra_ref = refs[PLANE + 9 :]
    d = d_ref[0]
    filters = weight_ref.shape[1]
    held = blocks[0].shape[1]
    lanes = taps_ref.shape[0] // 2
    fill_taps(taps_ref, weight_ref)
    for k in range(PLANE):
        rows = pl.ds(pl.multiple_of((d ^ k) * words, words), words)
        x_ref[rows, :held] = blocks[k][:words, :]
        x_ref[rows, held:] = jnp.zeros((words, x_ref.shape[1] - held), bf16)
        extra_ref[d ^ k] = blocks[k][words:, : 2 * filters].astype(f32)
    for half, out in ((0, ba_ref), (PLANE // 2, bb_ref)):
        source = extra_ref[half + d // 2]
        out[...] = jnp.where(d % 2 == 0, source[:, :filters], source[:, filters:])
    last = last_ref[...]

    def one(step, carry):
        rows = pl.ds(pl.multiple_of(step * words, words), words)
        best = None
        for group in range(-(-char_len // GROUP)):
            count = min(GROUP, char_len - GROUP * group)
            values = nn(
                x_ref[rows, group * lanes : (group + 2) * lanes], taps_ref[:, : count * filters]
            )
            for place in range(count):
                at = GROUP * group + place
                value = values[:, place * filters : (place + 1) * filters]
                if at >= first_masked:
                    value = jnp.where(at <= last, value, masked_score)
                if best is None:
                    best, where = value, jnp.zeros(value.shape, jnp.int32)
                else:
                    where = jnp.where(value > best, at, where)
                    best = jnp.maximum(value, best)
        pooled = jnp.maximum(best + bias_ref[...], 0.0)
        h_ref[rows, :] = pooled
        hb_ref[rows, :] = pooled.astype(bf16)
        at_ref[rows, :] = where
        return carry

    lax.fori_loop(0, PLANE, one, 0)


def highway_body(layer, d_ref, *refs):
    blocks = refs[:PLANE]
    w_ref, ba_ref, bb_ref, h_ref, open_ref, ra_ref, hn_ref, hb_ref = refs[PLANE:]
    d = d_ref[0]
    a = ba_ref[layer : layer + 1, :]
    b = bb_ref[layer : layer + 1, :]
    for k in range(PLANE):
        a = a + nn(blocks[k][...], w_ref[d ^ k, 0, 0])
        b = b + nn(blocks[k][...], w_ref[d ^ k, 0, 1])
    opened = jax.nn.sigmoid(b)
    ra = jnp.maximum(a, 0.0)
    mixed = opened * h_ref[...] + (1.0 - opened) * ra
    open_ref[...] = opened
    ra_ref[...] = ra
    hn_ref[...] = mixed
    hb_ref[...] = mixed.astype(bf16)


def highway(layer, dvec, blocks, weights, bias_a, bias_b, hidden):
    words, filters = hidden.shape
    part = words // 4
    row = pl.BlockSpec((part, filters), lambda i: (i, 0))
    depth, parts = weights.shape[1:3]
    return pl.pallas_call(
        functools.partial(highway_body, layer),
        grid=(4,),
        out_shape=[jax.ShapeDtypeStruct((words, filters), t) for t in (f32, f32, f32, bf16)],
        in_specs=[SMEM_SPEC]
        + [row] * PLANE
        + [
            pl.BlockSpec((PLANE, 1, parts, filters, filters), lambda i: (0, layer, 0, 0, 0)),
            pl.BlockSpec(bias_a.shape, lambda i: (0, 0)),
            pl.BlockSpec(bias_b.shape, lambda i: (0, 0)),
            row,
        ],
        out_specs=[row] * 4,
        name=f"highway{layer}",
        compiler_params=pltpu.CompilerParams(vmem_limit_bytes=58 * 1024 * 1024),
    )(dvec, *blocks, weights, bias_a, bias_b, hidden)


def project_body(d_ref, h_ref, w_ref, keep_ref, send_ref):
    d = d_ref[0]
    words = keep_ref.shape[1]
    for i in range(PLANE // 2):
        for odd, out in ((0, keep_ref), (1, send_ref)):
            rows = pl.ds(pl.multiple_of((d ^ odd ^ (2 * i)) * words, words), words)
            out[i] = nn(h_ref[rows, :], w_ref[...]).astype(out.dtype)


def unproject_body(words, d_ref, *refs):
    blocks = refs[:PLANE]
    w_ref, h_ref, dh_ref, dw_ref, sum_ref = refs[PLANE:]
    d = d_ref[0]
    total, rest = None, None
    for k in range(PLANE):
        rows = pl.ds(pl.multiple_of((d ^ k) * words, words), words)
        grad = blocks[k][:words, :]
        dh_ref[rows, :] = nt(grad, w_ref[...])
        piece = tn(h_ref[rows, :], grad)
        total = piece if total is None else total + piece
        block = blocks[k][...].astype(f32)
        rest = block if rest is None else rest + block
    dw_ref[...] = total.astype(dw_ref.dtype)
    sum_ref[: words + 16, :] = rest
    sum_ref[words + 16 :, :] = jnp.broadcast_to(over_words(rest[:words]), (16, rest.shape[1]))


def highway_back_body(
    d_ref, dh_ref, open_ref, ra_ref, h_ref, w_ref, ga_ref, gb_ref, dc_ref, sum_ref, keep_ref, send_ref
):
    d = d_ref[0]
    dh = dh_ref[...]
    opened = open_ref[...]
    ra = ra_ref[...]
    closed = 1.0 - opened
    ga = jnp.where(ra > 0.0, dh * closed, 0.0).astype(bf16)
    gb = (dh * (h_ref[...] - ra) * (opened * closed)).astype(bf16)
    ga_ref[...] = ga
    gb_ref[...] = gb
    dc_ref[...] = dh * opened
    filters = ga.shape[1]

    @pl.when(pl.program_id(0) == 0)
    def first():
        sum_ref[...] = jnp.zeros_like(sum_ref)

    sum_ref[:, :filters] += jnp.sum(
        ga.astype(f32).reshape(-1, 8, filters), axis=0
    )
    sum_ref[:, filters:] += jnp.sum(
        gb.astype(f32).reshape(-1, 8, filters), axis=0
    )
    for i in range(PLANE // 2):
        for odd, out in ((1, send_ref), (0, keep_ref)):
            j = d ^ odd ^ (2 * i)
            out[i] = (nt(ga, w_ref[j, 0, 0]) + nt(gb, w_ref[j, 0, 1])).astype(out.dtype)


def highway_back(layer, dvec, d_hidden, opened, ra, hidden, weights):
    words, filters = hidden.shape
    part = words // 4
    row = pl.BlockSpec((part, filters), lambda i: (i, 0))
    half = PLANE // 2
    blocks = pl.BlockSpec((half, part, filters), lambda i: (0, i, 0))
    parts = weights.shape[2]
    return pl.pallas_call(
        highway_back_body,
        grid=(4,),
        out_shape=[
            jax.ShapeDtypeStruct((words, filters), bf16),
            jax.ShapeDtypeStruct((words, filters), bf16),
            jax.ShapeDtypeStruct((words, filters), f32),
            jax.ShapeDtypeStruct((8, 2 * filters), f32),
            jax.ShapeDtypeStruct((half, words, filters), f32),
            jax.ShapeDtypeStruct((half, words, filters), bf16),
        ],
        in_specs=[SMEM_SPEC]
        + [row] * 4
        + [pl.BlockSpec((PLANE, 1, parts, filters, filters), lambda i: (0, layer, 0, 0, 0))],
        out_specs=[row, row, row, pl.BlockSpec((8, 2 * filters), lambda i: (0, 0)), blocks, blocks],
        name=f"highway_back{layer}",
        compiler_params=pltpu.CompilerParams(vmem_limit_bytes=58 * 1024 * 1024),
    )(dvec, d_hidden, opened, ra, hidden, weights)


def highway_grad_body(d_ref, *refs):
    blocks = refs[:PLANE]
    ga_ref, gb_ref, sum_ref, out_ref = refs[PLANE:]
    d = d_ref[0]
    filters = ga_ref.shape[1]
    row = jnp.sum(sum_ref[...], axis=0, keepdims=True)
    pad = out_ref.shape[1] - filters
    tail = jnp.where(
        lax.broadcasted_iota(jnp.int32, (pad, 2 * filters), 0) == 0, row, 0.0
    ).astype(bf16)
    for k in range(PLANE):
        out_ref[d ^ k, :filters, :filters] = tn(blocks[k][...], ga_ref[...]).astype(bf16)
        out_ref[d ^ k, :filters, filters:] = tn(blocks[k][...], gb_ref[...]).astype(bf16)
        out_ref[d ^ k, filters:, :] = tail


def spread_groups(char_len, filters, grad, at, spread_ref, group):
    count = min(GROUP, char_len - GROUP * group)
    for place in range(count):
        hit = at == GROUP * group + place
        spread_ref[:, place * filters : (place + 1) * filters] = jnp.where(hit, grad, 0.0).astype(
            bf16
        )
    return count


def char_back_body(char_len, words, d_ref, h_ref, at_ref, dh_ref, weight_ref, gp_ref, keep_ref, send_ref, taps_ref, spread_ref, chars_ref):
    d = d_ref[0]
    filters = h_ref.shape[1]
    lanes = taps_ref.shape[0] // 2
    held = keep_ref.shape[2]
    fill_taps(taps_ref, weight_ref)
    chars_ref[...] = jnp.zeros_like(chars_ref)

    def one(step, carry):
        rows = pl.ds(pl.multiple_of(step * 2 * words, 2 * words), 2 * words)
        grad = jnp.where(h_ref[rows, :] > 0.0, dh_ref[rows, :], 0.0).astype(bf16)
        gp_ref[rows, :] = grad
        grad = grad.astype(f32)
        at = at_ref[rows, :]
        for group in range(-(-char_len // GROUP)):
            count = spread_groups(char_len, filters, grad, at, spread_ref, group)
            piece = nt(spread_ref[:, : count * filters], taps_ref[:, : count * filters])
            chars_ref[rows, group * lanes : (group + 2) * lanes] += piece
        return carry

    lax.fori_loop(0, PLANE // 2, one, 0)
    for i in range(PLANE // 2):
        for odd, out in ((1, send_ref), (0, keep_ref)):
            rows = pl.ds(pl.multiple_of((d ^ odd ^ (2 * i)) * words, words), words)
            out[i] = chars_ref[rows, :held].astype(out.dtype)


def conv_grad_body(char_len, d_ref, x_ref, at_ref, gp_ref, dw_ref, spread_ref, xt_ref):
    filters = gp_ref.shape[1]
    lanes = 128
    depth = dw_ref.shape[0] - 8
    char_dim = lanes // GROUP
    grad = gp_ref[...].astype(f32)
    at = at_ref[...]
    groups = -(-char_len // GROUP)
    dw_ref[...] = jnp.zeros_like(dw_ref)
    for group in range(groups):
        count = spread_groups(char_len, filters, grad, at, spread_ref, group)
        piece = tn(x_ref[:, group * lanes : (group + 2) * lanes], spread_ref[:, : count * filters])
        for place in range(count):
            dw_ref[:depth, :] += piece[
                place * char_dim : place * char_dim + depth,
                place * filters : (place + 1) * filters,
            ]
    total = jnp.sum(grad.reshape(-1, 8, filters), axis=0)
    dw_ref[depth:, :] = jnp.broadcast_to(jnp.sum(total, axis=0, keepdims=True), (8, filters))


def table_grad_body(char_len, d_ref, ids_ref, chars_ref, out_ref):
    words = ids_ref.shape[1]
    lanes = 128
    width = lanes // GROUP
    rows = out_ref.shape[0] * GROUP
    groups = -(-char_len // GROUP)
    entry = lax.broadcasted_iota(jnp.int32, (rows, words), 0)
    lane = lax.broadcasted_iota(jnp.int32, (rows, lanes), 1) // width
    stacked = jnp.concatenate(
        [chars_ref[:, group * lanes : (group + 1) * lanes] for group in range(groups)], axis=0
    ).astype(bf16)
    total = jnp.zeros((rows, lanes), f32)
    for place in range(GROUP):
        pieces = []
        for group in range(groups):
            at = GROUP * group + place
            if at < char_len:
                pieces.append(jnp.where(ids_ref[at : at + 1, :] == entry, 1.0, 0.0).astype(bf16))
            else:
                pieces.append(jnp.zeros((rows, words), bf16))
        found = nn(jnp.concatenate(pieces, axis=1), stacked)
        total = total + jnp.where(lane == place, found, 0.0)
    step = width
    while step < lanes:
        total = total + pltpu.roll(total, step, 1)
        step *= 2
    part = out_ref.shape[0]
    fold = jnp.zeros(out_ref.shape, f32)
    lane = lax.broadcasted_iota(jnp.int32, out_ref.shape, 1) // width
    for place in range(GROUP):
        fold = fold + jnp.where(lane == place, total[place * part : (place + 1) * part], 0.0)
    out_ref[...] = fold


def pack_highway_body(carry_ref, gate_ref, out_ref):
    out_ref[0, :, 0] = carry_ref[...]
    out_ref[0, :, 1] = gate_ref[...]


def pack_highway(weights):
    layers, rows, columns = weights.shape
    own = columns // (2 * PLANE)
    block = (layers, rows, own)
    return pl.pallas_call(
        pack_highway_body,
        grid=(PLANE,),
        out_shape=jax.ShapeDtypeStruct((PLANE, layers, 2, rows, own), bf16),
        in_specs=[
            pl.BlockSpec(block, lambda j: (0, 0, j)),
            pl.BlockSpec(block, lambda j: (0, 0, PLANE + j)),
        ],
        out_specs=pl.BlockSpec((1, layers, 2, rows, own), lambda j: (j, 0, 0, 0, 0)),
        name="pack_highway",
    )(weights, weights)


def pack_encoder_body(qkv_ref, out_ref, inner_ref, outer_ref, small_ref, packed_ref):
    dim = packed_ref.shape[1]
    at = 0
    for ref in (qkv_ref, out_ref, inner_ref, outer_ref, small_ref):
        rows = ref.shape[0]
        for start in range(0, ref.shape[1], dim):
            packed_ref[at : at + rows, :] = ref[:, start : start + dim]
            at += rows


def finish_highway_body(flag_ref, whole_ref, third_ref, *refs):
    mid = flag_ref[0] == 1
    refs[-1][0] = jnp.where(mid, whole_ref[0].astype(f32), third_ref[0].astype(f32))


def finish_highway(layer, layers, flag, total, third, previous):
    own = total.shape[2] // 2
    block = pl.BlockSpec((1, own, own), lambda half, j: (j, 0, half))
    shape = jax.ShapeDtypeStruct((layers, own, 2 * PLANE * own), f32)
    operands = [flag, total, third]
    specs = [SMEM_SPEC, block, block]
    aliases = {}
    if previous is not None:
        operands.append(previous)
        specs.append(pl.BlockSpec(memory_space=pl.ANY))
        aliases = {3: 0}
    return pl.pallas_call(
        finish_highway_body,
        grid=(2, PLANE),
        out_shape=shape,
        in_specs=specs,
        out_specs=pl.BlockSpec((1, own, own), lambda half, j: (layer, 0, half * PLANE + j)),
        input_output_aliases=aliases,
        name=f"finish_highway{layer}",
    )(*operands)


def normalize(value):
    mean = jnp.mean(value, axis=-1, keepdims=True)
    centred = value - mean
    spread = jnp.mean(centred * centred, axis=-1, keepdims=True)
    scale = lax.rsqrt(spread + eps_norm)
    return centred * scale, scale


def normalize_back(grad, normal, scale, gain):
    moved = grad * gain
    return (
        moved
        - jnp.mean(moved, axis=-1, keepdims=True)
        - normal * jnp.mean(moved * normal, axis=-1, keepdims=True)
    ) * scale


def over_words(value):
    return jnp.sum(value, axis=0, keepdims=True)


def encoder_body(
    head_count,
    in_parts,
    flag_ref,
    emb_ref,
    e1_ref,
    e2_ref,
    e3_ref,
    small_ref,
    qseg_ref,
    kseg_ref,
    kpad_ref,
    cot_ref,
    w_hbm,
    result_ref,
    d_own_ref,
    d_send_ref,
    embs_ref,
    gq_ref,
    gk_ref,
    gv_ref,
    att_ref,
    gattn_ref,
    first_ref,
    act_ref,
    gup_ref,
    gdown_ref,
    stats_ref,
    w_ref,
    q_ref,
    k_ref,
    v_ref,
    p_ref,
    up_ref,
    gatt_ref,
    sems,
):
    words, dim = emb_ref.shape
    part = dim // PLANE
    wide = act_ref.shape[1] // PLANE
    cuts = [0, 3 * part, 4 * part, (4 + in_parts) * part, (4 + in_parts) * part + wide]
    copies = [
        pltpu.make_async_copy(
            w_hbm.at[:, low:high, :], w_ref.at[:, low:high, :], sems.at[i]
        )
        for i, (low, high) in enumerate(zip(cuts, cuts[1:]))
    ]
    for copy in copies:
        copy.start()
    pair = 2 * HDIM
    scale = HDIM ** (-0.5)

    def square(i):
        return w_ref[:, i * part : (i + 1) * part, :].reshape(dim, dim)

    def small(i):
        return small_ref[i : i + 1, :]

    emb = emb_ref[...]
    emb_b = emb.astype(bf16)
    embs_ref[:words] = emb_b
    for i, ref in enumerate((e1_ref, e2_ref, e3_ref)):
        embs_ref[(i + 1) * words : (i + 2) * words] = ref[...]
    copies[0].wait()
    q_ref[...] = (nn(emb_b, square(0)) + small(1)).astype(bf16)
    k_ref[...] = nn(embs_ref[...], square(1)).astype(bf16)
    v_ref[...] = (nn(embs_ref[...], square(2)) + small(2)).astype(bf16)
    keys = k_ref.shape[0]
    row = lax.broadcasted_iota(jnp.int32, (words, keys), 0)
    column = lax.broadcasted_iota(jnp.int32, (words, keys), 1)
    allowed = (qseg_ref[...] == kseg_ref[...]) & ((kpad_ref[...] == 0) | (row == column))
    low_lane = lax.broadcasted_iota(jnp.int32, (1, pair), 1) < HDIM

    def of_head(value, side):
        keep = low_lane if side == 0 else jnp.logical_not(low_lane)
        return jnp.where(keep, value.astype(f32), 0.0).astype(bf16)

    for at in range(head_count // 2):
        cols = slice(at * pair, (at + 1) * pair)
        outs = []
        for side in range(2):
            scores = nt(of_head(q_ref[:, cols], side), k_ref[:, cols]) * scale
            scores = jnp.where(allowed, scores, masked_score)
            top = jnp.max(scores, axis=-1, keepdims=True)
            raised = jnp.exp(scores - top)
            probs = raised / jnp.sum(raised, axis=-1, keepdims=True)
            p_ref[2 * at + side] = probs
            outs.append(nn(probs.astype(bf16), v_ref[:, cols]))
        att_ref[:, cols] = jnp.where(low_lane, outs[0], outs[1]).astype(bf16)
    copies[1].wait()
    attn_out = nn(att_ref[...], square(3)) + small(3)
    normal1, scale1 = normalize(emb + attn_out)
    first = normal1 * small(6) + small(9)
    first_b = first.astype(bf16)
    first_ref[...] = first_b
    copies[2].wait()
    half_root = math.sqrt(0.5)
    for i in range(in_parts):
        cols = slice(i * dim, (i + 1) * dim)
        up = nn(first_b, square(4 + i)) + small(11 + i)
        up_ref[:, cols] = up
        act_ref[:, cols] = (0.5 * up * (1.0 + lax.erf(up * half_root))).astype(bf16)
    copies[3].wait()
    low = cuts[3]
    outer = w_ref[:, low : low + wide, :].reshape(PLANE * wide, dim)
    second = first + (nn(act_ref[...], outer) + small(4))
    normal2, scale2 = normalize(second)
    result_ref[...] = (normal2 * small(7) + small(10)).astype(bf16)

    grad = cot_ref[...].astype(f32)
    d_second = normalize_back(grad, normal2, scale2, small(7))
    stats_ref[...] = jnp.zeros_like(stats_ref)
    stats_ref[7:8] = over_words(grad * normal2)
    stats_ref[10:11] = over_words(grad)
    gdown = d_second.astype(bf16)
    gdown_ref[...] = gdown
    stats_ref[4:5] = over_words(gdown.astype(f32))
    d_first = d_second
    density = 1.0 / math.sqrt(2.0 * math.pi)
    per = dim // wide
    for i in range(in_parts):
        cols = slice(i * dim, (i + 1) * dim)
        block = w_ref[i * per : (i + 1) * per, low : low + wide, :].reshape(dim, dim)
        up = up_ref[:, cols]
        slope = 0.5 * (1.0 + lax.erf(up * half_root)) + up * (
            density * jnp.exp(-0.5 * up * up)
        )
        gup = (nt(gdown, block) * slope).astype(bf16)
        gup_ref[:, cols] = gup
        stats_ref[11 + i : 12 + i] = over_words(gup.astype(f32))
        d_first = d_first + nt(gup, square(4 + i))
    stats_ref[6:7] = over_words(d_first * normal1)
    stats_ref[9:10] = over_words(d_first)
    d_res = normalize_back(d_first, normal1, scale1, small(6))
    gattn = d_res.astype(bf16)
    gattn_ref[...] = gattn
    stats_ref[3:4] = over_words(gattn.astype(f32))
    gatt_ref[...] = nt(gattn, square(3)).astype(bf16)
    for at in range(head_count // 2):
        cols = slice(at * pair, (at + 1) * pair)
        dq, dk, dv = [], None, None
        for side in range(2):
            gatt = of_head(gatt_ref[:, cols], side)
            probs = p_ref[2 * at + side]
            d_probs = nt(gatt, v_ref[:, cols])
            inner = jnp.sum(probs * d_probs, axis=-1, keepdims=True)
            gscore = (probs * (d_probs - inner)).astype(bf16)
            dq.append(nn(gscore, k_ref[:, cols]))
            more_k = tn(gscore, of_head(q_ref[:, cols], side))
            more_v = tn(probs.astype(bf16), gatt)
            dk = more_k if dk is None else dk + more_k
            dv = more_v if dv is None else dv + more_v
        gq_ref[:, cols] = (jnp.where(low_lane, dq[0], dq[1]) * scale).astype(bf16)
        gk_ref[:, cols] = (dk * scale).astype(bf16)
        gv_ref[:, cols] = dv.astype(bf16)
    stats_ref[1:2] = over_words(gq_ref[...].astype(f32))
    stats_ref[2:3] = over_words(gv_ref[...].astype(f32))
    for i in range(DEPTH):
        rows = slice(i * words, (i + 1) * words)
        piece = nt(gk_ref[rows, :], square(1)) + nt(gv_ref[rows, :], square(2))
        if i == 0:
            d_own_ref[...] = d_res + nt(gq_ref[...], square(0)) + piece
        else:
            d_send_ref[i - 1] = piece.astype(bf16)


def encoder_grad_body(
    flag_ref,
    embs_ref,
    gq_ref,
    gk_ref,
    gv_ref,
    att_ref,
    gattn_ref,
    first_ref,
    act_ref,
    gup_ref,
    gdown_ref,
    stats_ref,
    out_hbm,
    out_ref,
    sems,
):
    words, dim = gq_ref.shape
    part = dim // PLANE
    wide = act_ref.shape[1] // PLANE
    in_parts = gup_ref.shape[1] // dim
    pieces = []

    def put(low, high, value):
        out_ref[:, low:high, :] = value.reshape(PLANE, high - low, dim)

    def send(low, high):
        copy = pltpu.make_async_copy(
            out_ref.at[:, low:high, :], out_hbm.at[:, low:high, :], sems.at[len(pieces)]
        )
        copy.start()
        pieces.append(copy)

    low = (4 + in_parts) * part
    per = dim // wide
    for i in range(in_parts):
        cols = slice(i * dim, (i + 1) * dim)
        out_ref[i * per : (i + 1) * per, low : low + wide, :] = (
            tn(act_ref[:, cols], gdown_ref[...]).astype(bf16).reshape(per, wide, dim)
        )
    tail = jnp.broadcast_to(stats_ref[...].astype(bf16)[None], (PLANE,) + stats_ref.shape)
    out_ref[:, low + wide :, :] = tail
    send(low, out_ref.shape[1])
    for i in range(in_parts):
        cols = slice(i * dim, (i + 1) * dim)
        put((4 + i) * part, (5 + i) * part, tn(first_ref[...], gup_ref[:, cols]).astype(bf16))
    send(4 * part, low)
    put(3 * part, 4 * part, tn(att_ref[...], gattn_ref[...]).astype(bf16))
    put(0, part, tn(embs_ref[:words, :], gq_ref[...]).astype(bf16))
    put(part, 2 * part, tn(embs_ref[...], gk_ref[...]).astype(bf16))
    put(2 * part, 3 * part, tn(embs_ref[...], gv_ref[...]).astype(bf16))
    send(0, 4 * part)
    for copy in pieces:
        copy.wait()


def encoder(flag, embedded, others, small, query_segs, key_segs, key_pads, cotangent, weights):
    words, dim = embedded.shape
    keys = DEPTH * words
    head_count = dim // HDIM
    part = dim // PLANE
    in_parts = 4
    ff_dim = in_parts * dim
    vmem = pl.BlockSpec(memory_space=pltpu.VMEM)
    hbm = pl.BlockSpec(memory_space=pl.ANY)
    shapes = [
        ((words, dim), bf16),
        ((words, dim), f32),
        ((DEPTH - 1, words, dim), bf16),
        ((keys, dim), bf16),
        ((words, dim), bf16),
        ((keys, dim), bf16),
        ((keys, dim), bf16),
        ((words, dim), bf16),
        ((words, dim), bf16),
        ((words, dim), bf16),
        ((words, ff_dim), bf16),
        ((words, ff_dim), bf16),
        ((words, dim), bf16),
        ((16, dim), f32),
    ]
    outs = pl.pallas_call(
        functools.partial(encoder_body, head_count, in_parts),
        out_shape=[jax.ShapeDtypeStruct(s, t) for s, t in shapes],
        in_specs=[SMEM_SPEC] + [vmem] * 9 + [hbm],
        out_specs=[vmem] * len(shapes),
        scratch_shapes=[
            VMEM(weights.shape, bf16),
            VMEM((words, dim), bf16),
            VMEM((keys, dim), bf16),
            VMEM((keys, dim), bf16),
            VMEM((head_count, words, keys), f32),
            VMEM((words, ff_dim), f32),
            VMEM((words, dim), bf16),
            pltpu.SemaphoreType.DMA((4,)),
        ],
        name="encoder",
        compiler_params=pltpu.CompilerParams(vmem_limit_bytes=58 * 1024 * 1024),
    )(flag, embedded, *others, small, query_segs, key_segs, key_pads, cotangent, weights)
    result, d_own, d_send = outs[:3]
    rows = (4 + in_parts) * part + ff_dim // PLANE + 16
    grads = pl.pallas_call(
        encoder_grad_body,
        out_shape=jax.ShapeDtypeStruct((PLANE, rows, dim), bf16),
        in_specs=[SMEM_SPEC] + [vmem] * 11,
        out_specs=hbm,
        scratch_shapes=[VMEM((PLANE, rows, dim), bf16), pltpu.SemaphoreType.DMA((3,))],
        name="encoder_grad",
        compiler_params=pltpu.CompilerParams(vmem_limit_bytes=58 * 1024 * 1024),
    )(flag, *outs[3:])
    return result, d_own, d_send, grads


def round_up(value, multiple):
    return -(-value // multiple) * multiple


def plane_shards(
    char_ids,
    segment_ids,
    pad_mask,
    cotangent,
    char_table,
    conv_weight,
    conv_bias,
    hw_weight,
    hw_bias,
    proj_weight,
    pos_table,
    qkv_weight,
    out_weight,
    ff_in_weight,
    ff_out_weight,
    ff_in_bias,
    d_biases,
    norm_gain,
    norm_shift,
):
    d = lax.axis_index("dp")
    z = lax.axis_index("seq")
    dvec = d.astype(jnp.int32)[None]
    words, char_len = char_ids.shape[1:]
    all_words = PLANE * words
    tap_count, char_dim, filters = conv_weight.shape
    chars = char_table.shape[0]
    own = filters // PLANE
    depth = hw_weight.shape[0]
    model_dim = cotangent.shape[2]
    seq_len = segment_ids.shape[1]
    head_count = model_dim // HDIM
    part = model_dim // PLANE
    ff_dim = ff_out_weight.shape[0] * PLANE
    lanes = GROUP * char_dim
    held = round_up(char_len * char_dim, lanes)
    score_scale = HDIM ** (-0.5)

    ids = char_ids.reshape(words, char_len)
    table_rows = round_up(chars, 128)
    table = jnp.pad(jnp.tile(char_table, (1, GROUP)), ((0, table_rows - chars), (0, 0)))
    extra = jnp.pad(hw_bias, ((0, 16 - depth), (0, held - hw_bias.shape[1])))
    (own_x,) = call(
        functools.partial(lookup_body, char_len),
        [((words + 16, held), bf16)],
        dvec,
        (ids, table, extra),
        name="lookup",
    )
    x_blocks = plane_gather(own_x)

    hw_cols = lax.all_to_all(pack_highway(hw_weight), "dp", 0, 0)

    small = jnp.concatenate(
        [d_biases.reshape(-1), norm_gain.reshape(-1), norm_shift.reshape(-1), ff_in_bias]
    )
    small_rows = round_up(small.shape[0], model_dim) // model_dim
    small = jnp.pad(small, (0, small_rows * model_dim - small.shape[0])).reshape(-1, model_dim)
    pos_here = lax.dynamic_slice_in_dim(pos_table, z * words, words, 0).reshape(-1, model_dim)
    pos_rows = pos_here.shape[0]
    tail_rows = round_up(small_rows + pos_rows, 16)
    tail = jnp.pad(
        jnp.concatenate([small, pos_here], axis=0), ((0, tail_rows - small_rows - pos_rows), (0, 0))
    )
    in_parts = ff_in_weight.shape[1] // model_dim
    weight_rows = (4 + in_parts) * part + ff_dim // PLANE
    packed = pl.pallas_call(
        pack_encoder_body,
        out_shape=jax.ShapeDtypeStruct((weight_rows + tail_rows, model_dim), bf16),
        name="pack_encoder",
    )(qkv_weight, out_weight, ff_in_weight, ff_out_weight, tail)
    gathered = lax.all_gather(packed, "dp", axis=0, tiled=False)
    at = weight_rows
    small = gathered[:, at : at + small_rows].reshape(PLANE, -1)
    at += small_rows
    pos_full = (
        gathered[:, at : at + pos_rows]
        .reshape(PLANE, words, part)
        .transpose(1, 0, 2)
        .reshape(words, model_dim)
    )

    def rows_of(start, count):
        piece = small[:, start : start + count * part].reshape(PLANE, count, part)
        return piece.transpose(1, 0, 2).reshape(count, model_dim).astype(f32)

    inner_bias = small[:, 11 * part : 11 * part + ff_dim // PLANE].reshape(in_parts, model_dim)
    small_full = jnp.concatenate(
        [
            rows_of(0, 5),
            rows_of(5 * part, 3),
            rows_of(8 * part, 3),
            inner_bias.astype(f32),
            jnp.zeros((16 - 11 - in_parts, model_dim), f32),
        ],
        axis=0,
    )

    widths = filter_widths(filters)
    tap_mask = jnp.asarray(np.arange(tap_count)[:, None] < widths[None, :])
    masked_kernel = jnp.where(tap_mask[:, None, :], conv_weight, 0).reshape(
        tap_count * char_dim, filters
    )
    own_kernel = lax.dynamic_slice_in_dim(masked_kernel, d * own, own, 1)
    last_place = jnp.asarray((char_len - widths)[None, :], jnp.int32)
    own_last = lax.dynamic_slice_in_dim(last_place, d * own, own, 1)
    own_bias = lax.dynamic_slice_in_dim(conv_bias.astype(f32)[None, :], d * own, own, 1)
    taps_shape = VMEM((2 * lanes, GROUP * own), bf16)
    hidden0, hidden0_b, top_at, x_all, bias_a, bias_b = call(
        functools.partial(conv_body, char_len, char_len - tap_count + 1, words),
        [
            ((all_words, own), f32),
            ((all_words, own), bf16),
            ((all_words, own), jnp.int32),
            ((all_words, held + lanes), bf16),
            ((16, own), f32),
            ((16, own), f32),
        ],
        dvec,
        (*x_blocks, own_kernel, own_last, own_bias),
        [taps_shape, VMEM((PLANE, 16, 2 * own), f32)],
        name="conv",
    )

    hidden, hidden_b = hidden0, hidden0_b
    saved = []
    for layer in range(depth):
        blocks = plane_gather(hidden_b)
        opened, ra, following, following_b = highway(
            layer, dvec, blocks, hw_cols, bias_a, bias_b, hidden
        )
        saved.append((blocks, opened, ra, hidden))
        hidden, hidden_b = following, following_b
    half = PLANE // 2
    keep, send = call(
        project_body,
        [((half, words, model_dim), f32), ((half, words, model_dim), bf16)],
        dvec,
        (hidden_b, proj_weight),
        name="project",
    )
    projected = plane_reduce(keep, send) + small_full[0]

    summed = projected + pos_full.astype(f32)
    normal0, scale0 = normalize(summed)
    embedded = normal0 * small_full[5] + small_full[8]
    embedded_b = embedded.astype(bf16)
    others = [swap(embedded_b, "seq", DEPTH, offset) for offset in range(1, DEPTH)]

    def by_offset(row):
        pieces = row.reshape(DEPTH, words)
        return jnp.concatenate(
            [lax.dynamic_index_in_dim(pieces, z ^ offset, 0) for offset in range(DEPTH)], axis=1
        )

    key_segs, key_pads = by_offset(segment_ids), by_offset(pad_mask)
    result, d_own, d_send, enc_grads = encoder(
        dvec,
        embedded,
        others,
        small_full,
        key_segs[0, :words, None],
        key_segs,
        key_pads,
        cotangent.reshape(words, model_dim),
        gathered,
    )
    d_embedded = d_own
    for offset in range(1, DEPTH):
        d_embedded = d_embedded + swap(d_send[offset - 1], "seq", DEPTH, offset).astype(f32)
    enc_slice = lax.psum_scatter(enc_grads, "dp", scatter_dimension=0, tiled=True)[0]
    d_summed = normalize_back(d_embedded, normal0, scale0, small_full[5])
    grad_proj = jnp.concatenate(
        [
            d_summed.astype(bf16),
            over_words(d_embedded * normal0).astype(bf16),
            over_words(d_embedded).astype(bf16),
            jnp.zeros((14, model_dim), bf16),
        ],
        axis=0,
    )

    gp_blocks = plane_gather(grad_proj)
    d_hidden, proj_grad, top_sums = call(
        functools.partial(unproject_body, words),
        [((all_words, own), f32), ((own, model_dim), bf16), ((words + 32, model_dim), f32)],
        dvec,
        (*gp_blocks, proj_weight, hidden_b),
        name="unproject",
    )
    hw_slices = [None] * depth
    for layer in reversed(range(depth)):
        blocks, opened, ra, hidden = saved[layer]
        ga, gb, d_carry, sums, keep, send = highway_back(
            layer, dvec, d_hidden, opened, ra, hidden, hw_cols
        )
        d_hidden = d_carry + plane_reduce(keep, send)
        (cols_grad,) = call(
            highway_grad_body,
            [((PLANE, own + 16, 2 * own), bf16)],
            dvec,
            (*blocks, ga, gb, sums),
            name=f"highway_grad{layer}",
        )
        hw_slices[layer] = lax.all_to_all(cols_grad, "dp", 0, 0)

    grad_pooled, keep, send = call(
        functools.partial(char_back_body, char_len, words),
        [
            ((all_words, own), bf16),
            ((half, words, held), f32),
            ((half, words, held), bf16),
        ],
        dvec,
        (hidden0, top_at, d_hidden, own_kernel),
        [
            taps_shape,
            VMEM((2 * words, GROUP * own), bf16),
            VMEM((all_words, held + lanes), f32),
        ],
        name="char_back",
    )
    char_grads = plane_reduce(keep, send)
    (conv_part,) = call(
        functools.partial(conv_grad_body, char_len),
        [((tap_count * char_dim + 8, own), f32)],
        dvec,
        (x_all, top_at, grad_pooled),
        [VMEM((all_words, GROUP * own), bf16), VMEM((2 * lanes, all_words), bf16)],
        name="conv_grad",
    )
    fold_rows = round_up(-(-chars // GROUP), 8)
    (table_part,) = call(
        functools.partial(table_grad_body, char_len),
        [((fold_rows, lanes), f32)],
        dvec,
        (ids.T, char_grads),
        name="table_grad",
    )
    ends = jnp.concatenate(
        [conv_part, jnp.pad(table_part, ((0, 0), (0, own - lanes)))], axis=0
    )
    ends = ends + swap(ends, "seq", DEPTH, 1)
    ends = ends + swap(ends, "seq", DEPTH, 2)
    end_blocks = jnp.stack(plane_gather(ends))
    ordered = [lax.dynamic_index_in_dim(end_blocks, d ^ j, 0, False) for j in range(PLANE)]
    conv_rows = tap_count * char_dim
    conv_total = jnp.concatenate([piece[:conv_rows] for piece in ordered], axis=1)
    conv_total = jnp.where(
        tap_mask[:, None, :], conv_total.reshape(tap_count, char_dim, filters), 0.0
    )
    conv_bias_total = jnp.concatenate([piece[conv_rows] for piece in ordered])
    table_total = sum(piece[conv_rows + 8 :, :lanes] for piece in ordered)
    table_total = (
        table_total.reshape(fold_rows, GROUP, char_dim)
        .transpose(1, 0, 2)
        .reshape(GROUP * fold_rows, char_dim)[:chars]
    )

    top_own = lax.dynamic_slice_in_dim(top_sums, d * part, part, 1).astype(bf16)
    top_own = jnp.pad(top_own, ((0, 0), (0, 128 - part)))
    top_all = lax.dynamic_update_slice_in_dim(
        jnp.zeros((seq_len, 128), bf16), top_own[:words], z * words, 0
    )
    top_total = line_sum(jnp.concatenate([top_all, top_own[words:]], axis=0))[:, :part].astype(f32)
    pos_total = top_total[:seq_len]
    gain0, shift0, bias0 = top_total[seq_len], top_total[seq_len + 1], top_total[seq_len + 16]
    proj_total = line_sum(proj_grad).astype(f32)
    enc_total = line_sum(enc_slice).astype(f32)
    qkv_total = jnp.concatenate([enc_total[i * part : (i + 1) * part] for i in range(3)], axis=1)
    out_total = enc_total[3 * part : 4 * part]
    at = 4 * part
    inner_total = jnp.concatenate(
        [enc_total[at + i * part : at + (i + 1) * part] for i in range(in_parts)], axis=1
    )
    at += in_parts * part
    outer_total = enc_total[at : at + ff_dim // PLANE]
    small_total = enc_total[weight_rows:]
    own_small = lax.dynamic_slice_in_dim(small_total, d * part, part, 1)
    bias_total = jnp.concatenate([bias0[None], own_small[1:5]], axis=0)
    gain_total = jnp.concatenate([gain0[None], own_small[6:8]], axis=0)
    shift_total = jnp.concatenate([shift0[None], own_small[9:11]], axis=0)
    inner_bias_total = lax.dynamic_slice_in_dim(
        small_total[11 : 11 + in_parts].reshape(-1), d * (ff_dim // PLANE), ff_dim // PLANE, 0
    )

    flag = ((z == 1) | (z == 2)).astype(jnp.int32)[None]
    hw_total, hw_bias_totals = None, [None] * depth
    for layer in reversed(range(depth)):
        whole_sum, third = line_total(hw_slices[layer])
        hw_total = finish_highway(layer, depth, flag, whole_sum, third, hw_total)
        row = jnp.where(flag[0] == 1, whole_sum[:, own], third[:, own])
        row = row.reshape(PLANE, 2, own).transpose(1, 0, 2).reshape(-1)
        hw_bias_totals[layer] = lax.dynamic_slice_in_dim(row, d * 2 * own, 2 * own, 0).astype(f32)

    output = result.reshape(1, words, model_dim)
    return (
        output,
        table_total,
        conv_total,
        conv_bias_total,
        hw_total,
        jnp.stack(hw_bias_totals),
        proj_total,
        pos_total,
        qkv_total,
        out_total,
        inner_total,
        outer_total,
        inner_bias_total,
        bias_total,
        gain_total,
        shift_total,
    )


def solution(mesh):
    placed = (
        P("dp", "seq", None),
        P("dp", None),
        P("dp", None),
        P("dp", "seq", None),
        P(),
        P(),
        P(),
        P(None, "dp", None),
        P(None, "dp"),
        P("dp", None),
        P(None, "dp"),
        P("dp", None),
        P("dp", None),
        P("dp", None),
        P("dp", None),
        P("dp"),
        P(None, "dp"),
        P(None, "dp"),
        P(None, "dp"),
    )
    plane, depth = mesh.shape["dp"], mesh.shape["seq"]
    step = plane_shards if (plane, depth) == (PLANE, DEPTH) else shards
    return jax.shard_map(
        step,
        mesh=mesh,
        in_specs=placed,
        out_specs=(
            P("dp", "seq", None),
            P(),
            P(),
            P(),
            P(None, "dp", None),
            P(None, "dp"),
            P("dp", None),
            P(None, "dp"),
            P("dp", None),
            P("dp", None),
            P("dp", None),
            P("dp", None),
            P("dp"),
            P(None, "dp"),
            P(None, "dp"),
            P(None, "dp"),
        ),
        check_vma=False,
    )
```

```python
import functools
import math

import jax
import jax.numpy as jnp
import numpy as np
from jax import lax
from jax.experimental import pallas as pl
from jax.experimental.pallas import tpu as pltpu
from jax.sharding import PartitionSpec as P

HDIM = 64


eps_norm = 1e-12
masked_score = -1e30
width_shares = (1, 1, 2, 4, 8, 16, 32)


def filter_widths(filters):
    per_share = filters // 64
    return np.repeat(
        np.arange(1, len(width_shares) + 1),
        [per_share * share_count for share_count in width_shares],
    )


def layer_norm(inputs, gain_row, shift_row):
    centred = inputs - jnp.mean(inputs, axis=-1, keepdims=True)
    spread = jnp.mean(centred * centred, axis=-1, keepdims=True)
    return centred * lax.rsqrt(spread + eps_norm) * gain_row + shift_row


def highway_mix(gate_values, carried):
    filters = carried.shape[-1]
    opened = jax.nn.sigmoid(gate_values[:, filters:])
    return opened * carried + (1.0 - opened) * jax.nn.relu(gate_values[:, :filters])


def gelu_exact(inputs):
    return jax.nn.gelu(inputs, approximate=False)


def product(left_side, right_side):
    return jnp.dot(left_side, right_side, preferred_element_type=jnp.float32)


def product_tn(left_side, right_side):
    return lax.dot_general(
        left_side, right_side, (((0,), (0,)), ((), ())), preferred_element_type=jnp.float32
    )


def product_nt(left_side, right_side):
    return lax.dot_general(
        left_side, right_side, (((1,), (1,)), ((), ())), preferred_element_type=jnp.float32
    )


def char_windows(word_ids, char_rows, tap_count):
    word_count, char_len = word_ids.shape
    char_count = char_rows.shape[0]
    onehot = (
        word_ids.reshape(-1)[:, None] == jnp.arange(char_count, dtype=jnp.int32)[None, :]
    ).astype(jnp.bfloat16)
    vectors = product(onehot, char_rows).astype(jnp.bfloat16).reshape(word_count, char_len, -1)
    padded = jnp.pad(vectors, ((0, 0), (0, tap_count - 1), (0, 0)))
    char_taps = jnp.stack(
        [padded[:, tap_index : tap_index + char_len, :] for tap_index in range(tap_count)], axis=2
    )
    return (onehot, char_taps.reshape(word_count * char_len, -1))


def shards(
    char_ids,
    segment_ids,
    pad_mask,
    cotangent,
    char_table,
    conv_weight,
    conv_bias,
    hw_weight,
    hw_bias,
    proj_weight,
    pos_table,
    qkv_weight,
    out_weight,
    ff_in_weight,
    ff_out_weight,
    ff_in_bias,
    d_biases,
    norm_gain,
    norm_shift,
):
    (
        highway_full,
        highway_bias,
        proj_full,
        pos_full,
        qkv_full,
        out_full,
        inner_full,
        outer_full,
        inner_bias,
        bias_full,
        gain_full,
        shift_full,
    ) = (
        lax.all_gather(hw_weight, "dp", axis=1, tiled=True),
        lax.all_gather(hw_bias, "dp", axis=1, tiled=True),
        lax.all_gather(proj_weight, "dp", axis=0, tiled=True),
        lax.all_gather(pos_table, "dp", axis=1, tiled=True),
        lax.all_gather(qkv_weight, "dp", axis=0, tiled=True),
        lax.all_gather(out_weight, "dp", axis=0, tiled=True),
        lax.all_gather(ff_in_weight, "dp", axis=0, tiled=True),
        lax.all_gather(ff_out_weight, "dp", axis=0, tiled=True),
        lax.all_gather(ff_in_bias, "dp", axis=0, tiled=True),
        lax.all_gather(d_biases, "dp", axis=1, tiled=True),
        lax.all_gather(norm_gain, "dp", axis=1, tiled=True),
        lax.all_gather(norm_shift, "dp", axis=1, tiled=True),
    )
    seqs_here, local_len, char_len = char_ids.shape
    tap_count, char_dim, filters = conv_weight.shape
    model_dim = cotangent.shape[2]
    seq_len = segment_ids.shape[1]
    head_count = model_dim // HDIM
    highway_depth = highway_full.shape[0]
    word_count = seqs_here * local_len
    score_scale = HDIM ** (-0.5)
    bias_rows = bias_full.astype(jnp.float32)
    gain_rows = gain_full.astype(jnp.float32)
    shift_rows = shift_full.astype(jnp.float32)
    widths = filter_widths(filters)
    tap_mask = np.arange(tap_count)[:, None] < widths[None, :]
    masked_kernel = (conv_weight * jnp.asarray(tap_mask, jnp.bfloat16)[:, None, :]).reshape(
        tap_count * char_dim, filters
    )
    valid_place = jnp.asarray(np.arange(char_len)[:, None] <= char_len - widths[None, :])
    word_block = math.gcd(word_count, 32)
    block_count = word_count // word_block
    id_blocks = char_ids.reshape(block_count, word_block, char_len)

    def embed_forward(block_ids):
        unused, char_taps = char_windows(block_ids, char_table, tap_count)
        conv_out = (product(char_taps, masked_kernel) + conv_bias.astype(jnp.float32)).reshape(
            word_block, char_len, filters
        )
        conv_out = jnp.where(valid_place[None], conv_out, masked_score)
        return (jnp.max(conv_out, axis=1), jnp.argmax(conv_out, axis=1))

    pooled, top_place = lax.map(embed_forward, id_blocks)
    pooled = pooled.reshape(word_count, filters)
    hidden = jax.nn.relu(pooled)
    carried_list = []
    gates_list = []
    for highway_layer in range(highway_depth):
        carried_list.append(hidden)
        gate_values = product(
            hidden.astype(jnp.bfloat16), highway_full[highway_layer]
        ) + highway_bias[highway_layer].astype(jnp.float32)
        gates_list.append(gate_values)
        hidden = highway_mix(gate_values, hidden)
    top_hidden = hidden.astype(jnp.bfloat16)
    projected = product(top_hidden, proj_full) + bias_rows[0]
    row_start = lax.axis_index("seq") * local_len
    pos_rows = lax.dynamic_slice_in_dim(pos_full, row_start, local_len, 0).astype(jnp.float32)
    summed = (projected.reshape(seqs_here, local_len, model_dim) + pos_rows[None]).reshape(
        word_count, model_dim
    )
    embedded = layer_norm(summed, gain_rows[0], shift_rows[0])
    embedded_b = embedded.astype(jnp.bfloat16)
    qkv_shift = jnp.concatenate([bias_rows[1], jnp.zeros_like(bias_rows[1]), bias_rows[2]])
    qkv = (product(embedded_b, qkv_full) + qkv_shift).astype(jnp.bfloat16)
    queries = qkv[:, :model_dim].reshape(seqs_here, local_len, head_count, HDIM)
    keys_local = qkv[:, model_dim : 2 * model_dim].reshape(seqs_here, local_len, model_dim)
    values_local = qkv[:, 2 * model_dim :].reshape(seqs_here, local_len, model_dim)
    keys_full, values_full = (
        lax.all_gather(keys_local, "seq", axis=1, tiled=True),
        lax.all_gather(values_local, "seq", axis=1, tiled=True),
    )
    query_segs = lax.dynamic_slice_in_dim(segment_ids, row_start, local_len, 1)
    query_pos = row_start + jnp.arange(local_len, dtype=jnp.int32)
    same_segment = query_segs[:, :, None] == segment_ids[:, None, :]
    open_key = (pad_mask[:, None, :] == 0) | (
        query_pos[:, None] == jnp.arange(seq_len, dtype=jnp.int32)[None, :]
    )[None]
    allowed = (same_segment & open_key)[:, None]

    def score_of(key_rows):
        raw_scores = (
            jnp.einsum(
                "sqhd,skhd->shqk",
                queries,
                key_rows.reshape(seqs_here, seq_len, head_count, HDIM),
                preferred_element_type=jnp.float32,
            )
            * score_scale
        )
        return jnp.where(allowed, raw_scores, masked_score)

    scores = score_of(keys_full)
    row_top = jnp.max(scores, axis=-1, keepdims=True)
    exp_scores = jnp.exp(scores - row_top)
    denominator = jnp.sum(exp_scores, axis=-1, keepdims=True)
    attn_probs = (exp_scores / denominator).astype(jnp.bfloat16)
    log_total = row_top + jnp.log(denominator)
    attended = (
        jnp.einsum(
            "shqk,skhd->sqhd",
            attn_probs,
            values_full.reshape(seqs_here, seq_len, head_count, HDIM),
            preferred_element_type=jnp.float32,
        )
        .reshape(word_count, model_dim)
        .astype(jnp.bfloat16)
    )
    attn_out = product(attended, out_full) + bias_rows[3]
    first_input = embedded + attn_out
    first_norm = layer_norm(first_input, gain_rows[1], shift_rows[1])
    first_b = first_norm.astype(jnp.bfloat16)
    ffn_up = product(first_b, inner_full) + inner_bias.astype(jnp.float32)
    ffn_act = gelu_exact(ffn_up).astype(jnp.bfloat16)
    ffn_down = product(ffn_act, outer_full) + bias_rows[4]
    second = first_norm + ffn_down
    result = layer_norm(second, gain_rows[2], shift_rows[2])
    grad_out = cotangent.reshape(word_count, model_dim).astype(jnp.float32)
    unused, norm_back = jax.vjp(layer_norm, second, gain_rows[2], shift_rows[2])
    d_second, gain_grad2, shift_grad2 = norm_back(grad_out)
    grad_down = d_second.astype(jnp.bfloat16)
    outer_grad = product_tn(ffn_act, grad_down)
    bias_grad4 = jnp.sum(grad_down.astype(jnp.float32), axis=0)
    unused, gelu_back = jax.vjp(gelu_exact, ffn_up)
    grad_up = gelu_back(product_nt(grad_down, outer_full))[0].astype(jnp.bfloat16)
    inner_grad = product_tn(first_b, grad_up)
    inner_bias_grad = jnp.sum(grad_up.astype(jnp.float32), axis=0)
    d_first = d_second + product_nt(grad_up, inner_full)
    unused, norm_back = jax.vjp(layer_norm, first_input, gain_rows[1], shift_rows[1])
    d_res, gain_grad1, shift_grad1 = norm_back(d_first)
    grad_attn = d_res.astype(jnp.bfloat16)
    out_grad = product_tn(attended, grad_attn)
    bias_grad3 = jnp.sum(grad_attn.astype(jnp.float32), axis=0)
    grad_attended = (
        product_nt(grad_attn, out_full)
        .astype(jnp.bfloat16)
        .reshape(seqs_here, local_len, head_count, HDIM)
    )
    keys_back, values_back = (keys_full, values_full)
    probs_again = jnp.exp(score_of(keys_back) - log_total)
    probs_again_b = probs_again.astype(jnp.bfloat16)
    key_heads = keys_back.reshape(seqs_here, seq_len, head_count, HDIM)
    value_heads = values_back.reshape(seqs_here, seq_len, head_count, HDIM)
    d_probs = jnp.einsum(
        "sqhd,skhd->shqk", grad_attended, value_heads, preferred_element_type=jnp.float32
    )
    grad_scores = (
        probs_again * (d_probs - jnp.sum(probs_again * d_probs, axis=-1, keepdims=True))
    ).astype(jnp.bfloat16)
    d_queries = (
        jnp.einsum("shqk,skhd->sqhd", grad_scores, key_heads, preferred_element_type=jnp.float32)
        * score_scale
    )
    d_keys_all = (
        jnp.einsum("shqk,sqhd->skhd", grad_scores, queries, preferred_element_type=jnp.float32)
        * score_scale
    )
    d_values_all = jnp.einsum(
        "shqk,sqhd->skhd", probs_again_b, grad_attended, preferred_element_type=jnp.float32
    )
    d_keys, d_values = (
        lax.psum_scatter(
            d_keys_all.reshape(seqs_here, seq_len, model_dim).astype(jnp.bfloat16),
            "seq",
            scatter_dimension=1,
            tiled=True,
        ).astype(jnp.float32),
        lax.psum_scatter(
            d_values_all.reshape(seqs_here, seq_len, model_dim).astype(jnp.bfloat16),
            "seq",
            scatter_dimension=1,
            tiled=True,
        ).astype(jnp.float32),
    )
    grad_qkv = jnp.concatenate(
        [
            d_queries.reshape(word_count, model_dim),
            d_keys.reshape(word_count, model_dim),
            d_values.reshape(word_count, model_dim),
        ],
        axis=1,
    ).astype(jnp.bfloat16)
    qkv_grad = product_tn(embedded_b, grad_qkv)
    bias_grad1 = jnp.sum(grad_qkv[:, :model_dim].astype(jnp.float32), axis=0)
    bias_grad2 = jnp.sum(grad_qkv[:, 2 * model_dim :].astype(jnp.float32), axis=0)
    d_embedded = d_res + product_nt(grad_qkv, qkv_full)
    unused, norm_back = jax.vjp(layer_norm, summed, gain_rows[0], shift_rows[0])
    d_summed, gain_grad0, shift_grad0 = norm_back(d_embedded)
    pos_local = jnp.sum(d_summed.reshape(seqs_here, local_len, model_dim), axis=0)
    pos_grad = lax.dynamic_update_slice_in_dim(
        jnp.zeros((seq_len, model_dim), jnp.float32), pos_local, row_start, 0
    )
    grad_proj = d_summed.astype(jnp.bfloat16)
    proj_grad = product_tn(top_hidden, grad_proj)
    bias_grad0 = jnp.sum(grad_proj.astype(jnp.float32), axis=0)
    d_hidden = product_nt(grad_proj, proj_full)
    kernel_grads = [None] * highway_depth
    shift_grads = [None] * highway_depth
    for highway_layer in reversed(range(highway_depth)):
        carried = carried_list[highway_layer]
        unused, mix_back = jax.vjp(highway_mix, gates_list[highway_layer], carried)
        d_gates, d_carried = mix_back(d_hidden)
        grad_gates = d_gates.astype(jnp.bfloat16)
        kernel_grads[highway_layer] = product_tn(carried.astype(jnp.bfloat16), grad_gates)
        shift_grads[highway_layer] = jnp.sum(grad_gates.astype(jnp.float32), axis=0)
        d_hidden = d_carried + product_nt(grad_gates, highway_full[highway_layer])
    grad_pooled = jnp.where(pooled > 0, d_hidden, 0.0).astype(jnp.bfloat16)

    def embed_backward(running, inputs):
        weight_sum, bias_sum, table_sum = running
        block_ids, place_block, grad_block = inputs
        onehot, char_taps = char_windows(block_ids, char_table, tap_count)
        grad_conv = jnp.where(
            jnp.arange(char_len, dtype=jnp.int32)[None, :, None] == place_block[:, None, :],
            grad_block[:, None, :],
            jnp.zeros((), jnp.bfloat16),
        ).reshape(word_block * char_len, filters)
        weight_sum = weight_sum + product_tn(char_taps, grad_conv)
        bias_sum = bias_sum + jnp.sum(grad_block.astype(jnp.float32), axis=0)
        d_taps = product_nt(grad_conv, masked_kernel).reshape(
            word_block, char_len, tap_count, char_dim
        )
        spread = jnp.zeros((word_block, char_len + tap_count - 1, char_dim), jnp.float32)
        for tap_index in range(tap_count):
            spread = spread.at[:, tap_index : tap_index + char_len].add(d_taps[:, :, tap_index])
        grad_chars = (
            spread[:, :char_len].reshape(word_block * char_len, char_dim).astype(jnp.bfloat16)
        )
        table_sum = table_sum + product_tn(onehot, grad_chars)
        return ((weight_sum, bias_sum, table_sum), None)

    start_sums = (
        jnp.zeros((tap_count * char_dim, filters), jnp.float32),
        jnp.zeros((filters,), jnp.float32),
        jnp.zeros(char_table.shape, jnp.float32),
    )
    conv_sums, unused = lax.scan(
        embed_backward,
        start_sums,
        (id_blocks, top_place, grad_pooled.reshape(block_count, word_block, filters)),
    )
    conv_weight_grad = (
        conv_sums[0] * jnp.asarray(np.repeat(tap_mask, char_dim, axis=0), jnp.float32)
    ).reshape(tap_count, char_dim, filters)
    table_total, conv_total, conv_bias_total = lax.psum(
        (conv_sums[2], conv_weight_grad, conv_sums[1]), ("dp", "seq")
    )
    weight_grads = (
        jnp.stack(kernel_grads),
        jnp.stack(shift_grads),
        proj_grad,
        pos_grad,
        qkv_grad,
        out_grad,
        inner_grad,
        outer_grad,
        inner_bias_grad,
        jnp.stack([bias_grad0, bias_grad1, bias_grad2, bias_grad3, bias_grad4]),
        jnp.stack([gain_grad0, gain_grad1, gain_grad2]),
        jnp.stack([shift_grad0, shift_grad1, shift_grad2]),
    )
    sliced = (
        lax.psum_scatter(weight_grads[0], "dp", scatter_dimension=1, tiled=True),
        lax.psum_scatter(weight_grads[1], "dp", scatter_dimension=1, tiled=True),
        lax.psum_scatter(weight_grads[2], "dp", scatter_dimension=0, tiled=True),
        lax.psum_scatter(weight_grads[3], "dp", scatter_dimension=1, tiled=True),
        lax.psum_scatter(weight_grads[4], "dp", scatter_dimension=0, tiled=True),
        lax.psum_scatter(weight_grads[5], "dp", scatter_dimension=0, tiled=True),
        lax.psum_scatter(weight_grads[6], "dp", scatter_dimension=0, tiled=True),
        lax.psum_scatter(weight_grads[7], "dp", scatter_dimension=0, tiled=True),
        lax.psum_scatter(weight_grads[8], "dp", scatter_dimension=0, tiled=True),
        lax.psum_scatter(weight_grads[9], "dp", scatter_dimension=1, tiled=True),
        lax.psum_scatter(weight_grads[10], "dp", scatter_dimension=1, tiled=True),
        lax.psum_scatter(weight_grads[11], "dp", scatter_dimension=1, tiled=True),
    )
    summed_grads = (
        lax.psum(sliced[0].astype(jnp.bfloat16), "seq").astype(jnp.float32),
        lax.psum(sliced[1].astype(jnp.bfloat16), "seq").astype(jnp.float32),
        lax.psum(sliced[2].astype(jnp.bfloat16), "seq").astype(jnp.float32),
        lax.psum(sliced[3].astype(jnp.bfloat16), "seq").astype(jnp.float32),
        lax.psum(sliced[4].astype(jnp.bfloat16), "seq").astype(jnp.float32),
        lax.psum(sliced[5].astype(jnp.bfloat16), "seq").astype(jnp.float32),
        lax.psum(sliced[6].astype(jnp.bfloat16), "seq").astype(jnp.float32),
        lax.psum(sliced[7].astype(jnp.bfloat16), "seq").astype(jnp.float32),
        lax.psum(sliced[8].astype(jnp.bfloat16), "seq").astype(jnp.float32),
        lax.psum(sliced[9].astype(jnp.bfloat16), "seq").astype(jnp.float32),
        lax.psum(sliced[10].astype(jnp.bfloat16), "seq").astype(jnp.float32),
        lax.psum(sliced[11].astype(jnp.bfloat16), "seq").astype(jnp.float32),
    )
    output = result.astype(jnp.bfloat16).reshape(seqs_here, local_len, model_dim)
    return (output, table_total, conv_total, conv_bias_total) + tuple(summed_grads)


PLANE = 8
DEPTH = 4
CORE_PARTNER = 1
GROUP = 8

f32 = jnp.float32
bf16 = jnp.bfloat16


def swap(value, axis_name, size, offset):
    return lax.ppermute(value, axis_name, [(at, at ^ offset) for at in range(size)])


def plane_swap(value, offset):
    return swap(value, "dp", PLANE, offset)


def plane_gather(block, before=()):
    even = [block] + [plane_swap(block, offset) for offset in (2, 4, 6)]
    if before:
        even[1] = tie(even[1], *before)
    odd = [plane_swap(piece, CORE_PARTNER) for piece in even]
    return [piece for pair in zip(even, odd) for piece in pair]


def tie(value, *after):
    return lax.optimization_barrier((value, *after))[0]


def plane_parts(keep, send):
    arrived = plane_swap(send, CORE_PARTNER)
    own = keep[0].astype(f32) + arrived[0].astype(f32)
    return [own] + [
        (keep[i].astype(f32) + arrived[i].astype(f32)).astype(bf16) for i in range(1, PLANE // 2)
    ]


def plane_total(parts, after=()):
    total = tie(parts[0], *after)
    for i, part in enumerate(parts[1:], 1):
        total = total + plane_swap(part, 2 * i).astype(f32)
    return total


def plane_reduce(keep, send):
    return plane_total(plane_parts(keep, send))


LINE_STEPS = ([(0, 1), (3, 2)], [(1, 2), (2, 1)], [(1, 0), (2, 3)])


def line_step(value, step):
    return lax.ppermute(value, "seq", LINE_STEPS[step])


def nn(left_side, right_side):
    return jnp.dot(left_side, right_side, preferred_element_type=f32)


def nt(left_side, right_side):
    return lax.dot_general(
        left_side, right_side, (((1,), (1,)), ((), ())), preferred_element_type=f32
    )


def tn(left_side, right_side):
    return lax.dot_general(
        left_side, right_side, (((0,), (0,)), ((), ())), preferred_element_type=f32
    )


VMEM = pltpu.VMEM
SMEM_SPEC = pl.BlockSpec(memory_space=pltpu.SMEM)


def whole(count):
    return [pl.BlockSpec(memory_space=pltpu.VMEM)] * count


def cost(flops, moved):
    return pl.CostEstimate(flops=int(flops), transcendentals=0, bytes_accessed=int(moved))


def call(body, out_shapes, scalar, operands, scratch=(), name=None, flops=0):
    return pl.pallas_call(
        body,
        out_shape=[jax.ShapeDtypeStruct(s, t) for s, t in out_shapes],
        in_specs=[SMEM_SPEC] + whole(len(operands)),
        out_specs=whole(len(out_shapes)),
        scratch_shapes=list(scratch),
        name=name,
        cost_estimate=cost(
            flops,
            sum(x.size * x.dtype.itemsize for x in operands)
            + sum(math.prod(s) * jnp.dtype(t).itemsize for s, t in out_shapes),
        ),
        compiler_params=pltpu.CompilerParams(vmem_limit_bytes=58 * 1024 * 1024),
    )(scalar, *operands)


EXTRA_ROWS = 32
VECTOR_ROW = 2
POS_ROW = 16


def lookup_body(
    char_len,
    z_ref,
    ids_ref,
    table_ref,
    gate_ref,
    biases_ref,
    gain_ref,
    shift_ref,
    inner_ref,
    pos_ref,
    x_ref,
    extra_ref,
):
    words = ids_ref.shape[0]
    rows, lanes = table_ref.shape
    width = lanes // GROUP
    groups = x_ref.shape[1] // lanes
    lane = lax.broadcasted_iota(jnp.int32, (rows, lanes), 1) // width
    entry = lax.broadcasted_iota(jnp.int32, (words, rows), 1)
    total = jnp.zeros((groups * words, lanes), f32)
    for place in range(GROUP):
        pieces = []
        for group in range(groups):
            at = GROUP * group + place
            if at < char_len:
                hit = ids_ref[:, at : at + 1] == entry
                pieces.append(jnp.where(hit, 1.0, 0.0).astype(bf16))
            else:
                pieces.append(jnp.zeros((words, rows), bf16))
        own = jnp.where(lane == place, table_ref[...].astype(f32), 0.0).astype(bf16)
        total = total + nn(jnp.concatenate(pieces, axis=0), own)
    for group in range(groups):
        x_ref[:words, group * lanes : (group + 1) * lanes] = total[
            group * words : (group + 1) * words
        ].astype(bf16)
    extra_ref[...] = jnp.zeros_like(extra_ref)
    at = 0
    for ref in (gate_ref, biases_ref, gain_ref, shift_ref, inner_ref):
        extra_ref[at : at + ref.shape[0], : ref.shape[1]] = ref[...].astype(f32)
        at += ref.shape[0]
    per = EXTRA_ROWS - POS_ROW
    part = pos_ref.shape[1]
    for i in range(words // per):
        rows = pl.ds(pl.multiple_of(z_ref[0] * words + i * per, per), per)
        extra_ref[POS_ROW:, i * part : (i + 1) * part] = pos_ref[rows, :].astype(f32)
    x_ref[words:, :] = extra_ref[...].astype(bf16)


def fill_taps(d, taps_ref, weight_ref, widths_ref):
    depth = weight_ref.shape[0]
    filters = weight_ref.shape[1] // PLANE
    char_dim = taps_ref.shape[0] // (2 * GROUP)
    cols = pl.ds(pl.multiple_of(d * filters, filters), filters)
    tap = lax.broadcasted_iota(jnp.int32, (depth, filters), 0) // char_dim
    own = jnp.where(tap < widths_ref[:, cols], weight_ref[:, cols].astype(f32), 0.0).astype(bf16)
    taps_ref[...] = jnp.zeros_like(taps_ref)
    for place in range(GROUP):
        taps_ref[
            place * char_dim : place * char_dim + depth, place * filters : (place + 1) * filters
        ] = own


def conv_body(char_len, first_masked, words, d_ref, *refs):
    blocks = refs[:PLANE]
    (weight_ref, widths_ref, bias_ref, h_ref, hb_ref, at_ref, x_ref, ba_ref, bb_ref, all_extra_ref) = refs[
        PLANE : PLANE + 10
    ]
    taps_ref, extra_ref = refs[PLANE + 10 :]
    d = d_ref[0]
    filters = h_ref.shape[1]
    held = blocks[0].shape[1]
    lanes = taps_ref.shape[0] // 2
    fill_taps(d, taps_ref, weight_ref, widths_ref)
    cols = pl.ds(pl.multiple_of(d * filters, filters), filters)
    bias = bias_ref[:, cols].astype(f32)
    for k in range(PLANE):
        rows = pl.ds(pl.multiple_of((d ^ k) * words, words), words)
        x_ref[rows, :held] = blocks[k][:words, :]
        x_ref[rows, held:] = jnp.zeros((words, x_ref.shape[1] - held), bf16)
        extra_ref[d ^ k] = blocks[k][words : words + 16, : 2 * filters].astype(f32)
        all_extra_ref[d ^ k] = blocks[k][words:, :]
    for half, out in ((0, ba_ref), (PLANE // 2, bb_ref)):
        source = extra_ref[half + d // 2]
        out[...] = jnp.where(d % 2 == 0, source[:, :filters], source[:, filters:])
    last = char_len - widths_ref[:, cols]

    def one(step, carry):
        rows = pl.ds(pl.multiple_of(step * words, words), words)
        best = None
        for group in range(-(-char_len // GROUP)):
            count = min(GROUP, char_len - GROUP * group)
            values = nn(
                x_ref[rows, group * lanes : (group + 2) * lanes], taps_ref[:, : count * filters]
            )
            for place in range(count):
                at = GROUP * group + place
                value = values[:, place * filters : (place + 1) * filters]
                if at >= first_masked:
                    value = jnp.where(at <= last, value, masked_score)
                if best is None:
                    best, where = value, jnp.zeros(value.shape, jnp.int32)
                else:
                    where = jnp.where(value > best, at, where)
                    best = jnp.maximum(value, best)
        pooled = jnp.maximum(best + bias, 0.0)
        h_ref[rows, :] = pooled
        hb_ref[rows, :] = pooled.astype(bf16)
        at_ref[rows, :] = where
        return carry

    lax.fori_loop(0, PLANE, one, 0)


def highway_body(layer, d_ref, *refs):
    blocks = refs[:PLANE]
    w_ref, ba_ref, bb_ref, h_ref, open_ref, ra_ref, hn_ref, hb_ref = refs[PLANE:]
    d = d_ref[0]
    a = ba_ref[layer : layer + 1, :]
    b = bb_ref[layer : layer + 1, :]
    for k in range(PLANE):
        a = a + nn(blocks[k][...], w_ref[d ^ k, 0])
        b = b + nn(blocks[k][...], w_ref[d ^ k, 1])
    opened = jax.nn.sigmoid(b)
    ra = jnp.maximum(a, 0.0)
    mixed = opened * h_ref[...] + (1.0 - opened) * ra
    open_ref[...] = opened
    ra_ref[...] = ra
    hn_ref[...] = mixed
    hb_ref[...] = mixed.astype(bf16)


def highway(layer, dvec, blocks, weights, bias_a, bias_b, hidden):
    words, filters = hidden.shape
    part = words // 4
    row = pl.BlockSpec((part, filters), lambda i: (i, 0))
    return pl.pallas_call(
        functools.partial(highway_body, layer),
        grid=(4,),
        out_shape=[jax.ShapeDtypeStruct((words, filters), t) for t in (f32, f32, f32, bf16)],
        in_specs=[SMEM_SPEC]
        + [row] * PLANE
        + [
            pl.BlockSpec(weights.shape, lambda i: (0, 0, 0, 0)),
            pl.BlockSpec(bias_a.shape, lambda i: (0, 0)),
            pl.BlockSpec(bias_b.shape, lambda i: (0, 0)),
            row,
        ],
        out_specs=[row] * 4,
        name=f"highway{layer}",
        cost_estimate=cost(2 * words * filters * PLANE * 2 * filters, 12e6),
        compiler_params=pltpu.CompilerParams(vmem_limit_bytes=58 * 1024 * 1024),
    )(dvec, *blocks, weights, bias_a, bias_b, hidden)


def project_body(d_ref, h_ref, w_ref, keep_ref, send_ref):
    d = d_ref[0]
    words = keep_ref.shape[1]
    for i in range(PLANE // 2):
        for odd, out in ((0, keep_ref), (1, send_ref)):
            rows = pl.ds(pl.multiple_of((d ^ odd ^ (2 * i)) * words, words), words)
            out[i] = nn(h_ref[rows, :], w_ref[...]).astype(out.dtype)


def unproject_body(words, d_ref, *refs):
    blocks = refs[:PLANE]
    w_ref, h_ref, dh_ref, dw_ref, sum_ref = refs[PLANE:]
    d = d_ref[0]
    total, rest = None, None
    for k in range(PLANE):
        rows = pl.ds(pl.multiple_of((d ^ k) * words, words), words)
        grad = blocks[k][:words, :]
        dh_ref[rows, :] = nt(grad, w_ref[...])
        piece = tn(h_ref[rows, :], grad)
        total = piece if total is None else total + piece
        block = blocks[k][...].astype(f32)
        rest = block if rest is None else rest + block
    dw_ref[...] = total.astype(dw_ref.dtype)
    sum_ref[: words + 16, :] = rest
    sum_ref[words + 16 :, :] = jnp.broadcast_to(over_words(rest[:words]), (16, rest.shape[1]))


def highway_back_body(
    d_ref, dh_ref, open_ref, ra_ref, h_ref, w_ref, ga_ref, gb_ref, dc_ref, sum_ref, keep_ref, send_ref
):
    d = d_ref[0]
    dh = dh_ref[...]
    opened = open_ref[...]
    ra = ra_ref[...]
    closed = 1.0 - opened
    ga = jnp.where(ra > 0.0, dh * closed, 0.0).astype(bf16)
    gb = (dh * (h_ref[...] - ra) * (opened * closed)).astype(bf16)
    ga_ref[...] = ga
    gb_ref[...] = gb
    dc_ref[...] = dh * opened
    filters = ga.shape[1]

    @pl.when(pl.program_id(0) == 0)
    def first():
        sum_ref[...] = jnp.zeros_like(sum_ref)

    sum_ref[:, :filters] += jnp.sum(
        ga.astype(f32).reshape(-1, 8, filters), axis=0
    )
    sum_ref[:, filters:] += jnp.sum(
        gb.astype(f32).reshape(-1, 8, filters), axis=0
    )
    for i in range(PLANE // 2):
        for odd, out in ((1, send_ref), (0, keep_ref)):
            j = d ^ odd ^ (2 * i)
            out[i] = (nt(ga, w_ref[j, 0]) + nt(gb, w_ref[j, 1])).astype(out.dtype)


def highway_back(layer, dvec, d_hidden, opened, ra, hidden, weights):
    words, filters = hidden.shape
    part = words // 4
    row = pl.BlockSpec((part, filters), lambda i: (i, 0))
    half = PLANE // 2
    blocks = pl.BlockSpec((half, part, filters), lambda i: (0, i, 0))
    return pl.pallas_call(
        highway_back_body,
        grid=(4,),
        out_shape=[
            jax.ShapeDtypeStruct((words, filters), bf16),
            jax.ShapeDtypeStruct((words, filters), bf16),
            jax.ShapeDtypeStruct((words, filters), f32),
            jax.ShapeDtypeStruct((8, 2 * filters), f32),
            jax.ShapeDtypeStruct((half, words, filters), f32),
            jax.ShapeDtypeStruct((half, words, filters), bf16),
        ],
        in_specs=[SMEM_SPEC]
        + [row] * 4
        + [pl.BlockSpec(weights.shape, lambda i: (0, 0, 0, 0))],
        out_specs=[row, row, row, pl.BlockSpec((8, 2 * filters), lambda i: (0, 0)), blocks, blocks],
        name=f"highway_back{layer}",
        cost_estimate=cost(2 * words * filters * PLANE * 2 * filters, 20e6),
        compiler_params=pltpu.CompilerParams(vmem_limit_bytes=58 * 1024 * 1024),
    )(dvec, d_hidden, opened, ra, hidden, weights)


def highway_grad_body(d_ref, *refs):
    blocks = refs[:PLANE]
    ga_ref, gb_ref, out_ref = refs[PLANE:]
    d = d_ref[0]
    filters = ga_ref.shape[1]
    for k in range(PLANE):
        for side, grad_ref in enumerate((ga_ref, gb_ref)):
            piece = tn(blocks[k][...], grad_ref[...]).astype(bf16)
            out_ref[:, d ^ k, :, side * filters : (side + 1) * filters] = piece.reshape(
                DEPTH, filters // DEPTH, filters
            )


def spread_groups(char_len, filters, grad, at, spread_ref, group):
    count = min(GROUP, char_len - GROUP * group)
    for place in range(count):
        hit = at == GROUP * group + place
        spread_ref[:, place * filters : (place + 1) * filters] = jnp.where(hit, grad, 0.0).astype(
            bf16
        )
    return count


def char_back_body(char_len, words, d_ref, h_ref, at_ref, dh_ref, weight_ref, widths_ref, gp_ref, keep_ref, send_ref, taps_ref, spread_ref, chars_ref):
    d = d_ref[0]
    filters = h_ref.shape[1]
    lanes = taps_ref.shape[0] // 2
    held = keep_ref.shape[2]
    fill_taps(d, taps_ref, weight_ref, widths_ref)
    chars_ref[...] = jnp.zeros_like(chars_ref)

    def one(step, carry):
        rows = pl.ds(pl.multiple_of(step * 2 * words, 2 * words), 2 * words)
        grad = jnp.where(h_ref[rows, :] > 0.0, dh_ref[rows, :], 0.0).astype(bf16)
        gp_ref[rows, :] = grad
        grad = grad.astype(f32)
        at = at_ref[rows, :]
        for group in range(-(-char_len // GROUP)):
            count = spread_groups(char_len, filters, grad, at, spread_ref, group)
            piece = nt(spread_ref[:, : count * filters], taps_ref[:, : count * filters])
            chars_ref[rows, group * lanes : (group + 2) * lanes] += piece
        return carry

    lax.fori_loop(0, PLANE // 2, one, 0)
    for i in range(PLANE // 2):
        for odd, out in ((1, send_ref), (0, keep_ref)):
            rows = pl.ds(pl.multiple_of((d ^ odd ^ (2 * i)) * words, words), words)
            out[i] = chars_ref[rows, :held].astype(out.dtype)


def conv_grad_body(char_len, d_ref, x_ref, at_ref, gp_ref, dw_ref, spread_ref, xt_ref):
    filters = gp_ref.shape[1]
    lanes = 128
    depth = dw_ref.shape[0] - 8
    char_dim = lanes // GROUP
    grad = gp_ref[...].astype(f32)
    at = at_ref[...]
    groups = -(-char_len // GROUP)
    dw_ref[...] = jnp.zeros_like(dw_ref)
    for group in range(groups):
        count = spread_groups(char_len, filters, grad, at, spread_ref, group)
        piece = tn(x_ref[:, group * lanes : (group + 2) * lanes], spread_ref[:, : count * filters])
        for place in range(count):
            dw_ref[:depth, :] += piece[
                place * char_dim : place * char_dim + depth,
                place * filters : (place + 1) * filters,
            ]
    total = jnp.sum(grad.reshape(-1, 8, filters), axis=0)
    dw_ref[depth:, :] = jnp.broadcast_to(jnp.sum(total, axis=0, keepdims=True), (8, filters))


def table_grad_body(char_len, d_ref, ids_ref, chars_ref, out_ref):
    words = ids_ref.shape[1]
    lanes = 128
    width = lanes // GROUP
    rows = out_ref.shape[0] * GROUP
    groups = -(-char_len // GROUP)
    entry = lax.broadcasted_iota(jnp.int32, (rows, words), 0)
    lane = lax.broadcasted_iota(jnp.int32, (rows, lanes), 1) // width
    stacked = jnp.concatenate(
        [chars_ref[:, group * lanes : (group + 1) * lanes] for group in range(groups)], axis=0
    ).astype(bf16)
    total = jnp.zeros((rows, lanes), f32)
    for place in range(GROUP):
        pieces = []
        for group in range(groups):
            at = GROUP * group + place
            if at < char_len:
                pieces.append(jnp.where(ids_ref[at : at + 1, :] == entry, 1.0, 0.0).astype(bf16))
            else:
                pieces.append(jnp.zeros((rows, words), bf16))
        found = nn(jnp.concatenate(pieces, axis=1), stacked)
        total = total + jnp.where(lane == place, found, 0.0)
    step = width
    while step < lanes:
        total = total + pltpu.roll(total, step, 1)
        step *= 2
    part = out_ref.shape[0]
    fold = jnp.zeros(out_ref.shape, f32)
    lane = lax.broadcasted_iota(jnp.int32, out_ref.shape, 1) // width
    for place in range(GROUP):
        fold = fold + jnp.where(lane == place, total[place * part : (place + 1) * part], 0.0)
    out_ref[...] = fold


def pack_highway_body(carry_ref, gate_ref, *outs):
    for layer, out_ref in enumerate(outs):
        out_ref[0, 0] = carry_ref[layer]
        out_ref[0, 1] = gate_ref[layer]


def pack_highway(weights):
    layers, rows, columns = weights.shape
    own = columns // (2 * PLANE)
    block = (layers, rows, own)
    return pl.pallas_call(
        pack_highway_body,
        grid=(PLANE,),
        out_shape=[jax.ShapeDtypeStruct((PLANE, 2, rows, own), bf16)] * layers,
        in_specs=[
            pl.BlockSpec(block, lambda j: (0, 0, j)),
            pl.BlockSpec(block, lambda j: (0, 0, PLANE + j)),
        ],
        out_specs=[pl.BlockSpec((1, 2, rows, own), lambda j: (j, 0, 0, 0))] * layers,
        name="pack_highway",
    )(weights, weights)


def pack_encoder_body(qkv_ref, out_ref, inner_ref, outer_ref, packed_ref):
    dim = packed_ref.shape[1]
    at = 0
    for ref in (qkv_ref, out_ref, inner_ref, outer_ref):
        rows = ref.shape[0]
        for start in range(0, ref.shape[1], dim):
            packed_ref[at : at + rows, :] = ref[:, start : start + dim]
            at += rows


def finish_highway_body(blocks_ref, *refs):
    out_ref = refs[-1]
    own = out_ref.shape[1]
    half = out_ref.shape[2] // 2
    for j in range(PLANE):
        for side in range(2):
            at = slice(j * own + side * half, (j + 1) * own + side * half)
            cols = slice(side * own, (side + 1) * own)
            out_ref[0, :, at] = blocks_ref[:, j, :, cols].reshape(own, own).astype(f32)


def finish_highway(layer, layers, blocks, previous):
    own = blocks.shape[3] // 2
    width = 2 * PLANE * own
    operands = [blocks]
    specs = [pl.BlockSpec(blocks.shape, lambda i: (0, 0, 0, 0))]
    aliases = {}
    if previous is not None:
        operands.append(previous)
        specs.append(pl.BlockSpec(memory_space=pl.ANY))
        aliases = {1: 0}
    return pl.pallas_call(
        finish_highway_body,
        grid=(1,),
        out_shape=jax.ShapeDtypeStruct((layers, own, width), f32),
        in_specs=specs,
        out_specs=pl.BlockSpec((1, own, width), lambda i: (layer, 0, 0)),
        input_output_aliases=aliases,
        name=f"finish_highway{layer}",
        compiler_params=pltpu.CompilerParams(vmem_limit_bytes=58 * 1024 * 1024),
    )(*operands)


def finish_ends_body(d_ref, *refs):
    blocks = refs[:PLANE]
    widths_ref, conv_ref, bias_ref, gates_ref, table_ref, held_ref = refs[PLANE:]
    d = d_ref[0]
    own = blocks[0].shape[1]
    rows = conv_ref.shape[0]
    lanes = table_ref.shape[1]
    char_dim = lanes // GROUP
    tap = lax.broadcasted_iota(jnp.int32, (rows, own), 0) // char_dim
    for k in range(PLANE):
        cols = pl.ds(pl.multiple_of((d ^ k) * own, own), own)
        conv_ref[:, cols] = jnp.where(tap < widths_ref[:, cols], blocks[k][:rows, :], 0.0)
        bias_ref[:, cols] = blocks[k][rows : rows + 8, :]
        gates_ref[:, cols] = blocks[k][rows + 8 : rows + 16, :]
        held_ref[d ^ k] = blocks[k][rows + 16 :, :lanes]
    total = held_ref[0]
    for j in range(1, PLANE):
        total = total + held_ref[j]
    table_ref[...] = total


def finish_encoder_body(d_ref, low_ref, high_ref, *outs):
    dim = low_ref.shape[1]
    at = 0
    for ref in outs:
        count = ref.shape[0]
        for left in range(0, ref.shape[1], dim):
            low = low_ref.shape[0]
            source = low_ref[at : at + count] if at < low else high_ref[at - low : at - low + count]
            ref[:, left : left + dim] = source.astype(f32)
            at += count


def normalize(value):
    mean = jnp.mean(value, axis=-1, keepdims=True)
    centred = value - mean
    spread = jnp.mean(centred * centred, axis=-1, keepdims=True)
    scale = lax.rsqrt(spread + eps_norm)
    return centred * scale, scale


def normalize_back(grad, normal, scale, gain):
    moved = grad * gain
    return (
        moved
        - jnp.mean(moved, axis=-1, keepdims=True)
        - normal * jnp.mean(moved * normal, axis=-1, keepdims=True)
    ) * scale


def over_words(value):
    return jnp.sum(value, axis=0, keepdims=True)


def encoder_body(
    head_count,
    in_parts,
    flag_ref,
    emb_ref,
    e1_ref,
    e2_ref,
    e3_ref,
    small_ref,
    qseg_ref,
    kseg_ref,
    kpad_ref,
    cot_ref,
    w_hbm,
    result_ref,
    d_own_ref,
    send1_ref,
    send2_ref,
    send3_ref,
    embs_ref,
    gq_ref,
    gk_ref,
    gv_ref,
    att_ref,
    gattn_ref,
    first_ref,
    act_ref,
    gup_ref,
    gdown_ref,
    stats_ref,
    w_ref,
    q_ref,
    k_ref,
    v_ref,
    p_ref,
    up_ref,
    gatt_ref,
    sems,
):
    words, dim = emb_ref.shape
    part = dim // PLANE
    wide = act_ref.shape[1] // PLANE
    cuts = [0, 3 * part, 4 * part, (4 + in_parts) * part, (4 + in_parts) * part + wide]
    copies = [
        pltpu.make_async_copy(
            w_hbm.at[:, low:high, :], w_ref.at[:, low:high, :], sems.at[i]
        )
        for i, (low, high) in enumerate(zip(cuts, cuts[1:]))
    ]
    for copy in copies:
        copy.start()
    pair = 2 * HDIM
    scale = HDIM ** (-0.5)

    def square(i):
        return w_ref[:, i * part : (i + 1) * part, :].reshape(dim, dim)

    def small(i):
        return small_ref[i : i + 1, :]

    emb = emb_ref[...]
    emb_b = emb.astype(bf16)
    embs_ref[:words] = emb_b
    for i, ref in enumerate((e1_ref, e2_ref, e3_ref)):
        embs_ref[(i + 1) * words : (i + 2) * words] = ref[...]
    copies[0].wait()
    q_ref[...] = (nn(emb_b, square(0)) + small(1)).astype(bf16)
    k_ref[...] = nn(embs_ref[...], square(1)).astype(bf16)
    v_ref[...] = (nn(embs_ref[...], square(2)) + small(2)).astype(bf16)
    keys = k_ref.shape[0]
    row = lax.broadcasted_iota(jnp.int32, (words, keys), 0)
    column = lax.broadcasted_iota(jnp.int32, (words, keys), 1)
    allowed = (qseg_ref[...] == kseg_ref[...]) & ((kpad_ref[...] == 0) | (row == column))
    low_lane = lax.broadcasted_iota(jnp.int32, (1, pair), 1) < HDIM

    def of_head(value, side):
        keep = low_lane if side == 0 else jnp.logical_not(low_lane)
        return jnp.where(keep, value.astype(f32), 0.0).astype(bf16)

    for at in range(head_count // 2):
        cols = slice(at * pair, (at + 1) * pair)
        outs = []
        for side in range(2):
            scores = nt(of_head(q_ref[:, cols], side), k_ref[:, cols]) * scale
            scores = jnp.where(allowed, scores, masked_score)
            top = jnp.max(scores, axis=-1, keepdims=True)
            raised = jnp.exp(scores - top)
            probs = raised / jnp.sum(raised, axis=-1, keepdims=True)
            p_ref[2 * at + side] = probs
            outs.append(nn(probs.astype(bf16), v_ref[:, cols]))
        att_ref[:, cols] = jnp.where(low_lane, outs[0], outs[1]).astype(bf16)
    copies[1].wait()
    attn_out = nn(att_ref[...], square(3)) + small(3)
    normal1, scale1 = normalize(emb + attn_out)
    first = normal1 * small(6) + small(9)
    first_b = first.astype(bf16)
    first_ref[...] = first_b
    copies[2].wait()
    half_root = math.sqrt(0.5)
    for i in range(in_parts):
        cols = slice(i * dim, (i + 1) * dim)
        up = nn(first_b, square(4 + i)) + small(11 + i)
        up_ref[:, cols] = up
        act_ref[:, cols] = (0.5 * up * (1.0 + lax.erf(up * half_root))).astype(bf16)
    copies[3].wait()
    low = cuts[3]
    outer = w_ref[:, low : low + wide, :].reshape(PLANE * wide, dim)
    second = first + (nn(act_ref[...], outer) + small(4))
    normal2, scale2 = normalize(second)
    result_ref[...] = (normal2 * small(7) + small(10)).astype(bf16)

    grad = cot_ref[...].astype(f32)
    d_second = normalize_back(grad, normal2, scale2, small(7))
    stats_ref[...] = jnp.zeros_like(stats_ref)
    stats_ref[7:8] = over_words(grad * normal2)
    stats_ref[10:11] = over_words(grad)
    gdown = d_second.astype(bf16)
    gdown_ref[...] = gdown
    stats_ref[4:5] = over_words(gdown.astype(f32))
    d_first = d_second
    density = 1.0 / math.sqrt(2.0 * math.pi)
    per = dim // wide
    for i in range(in_parts):
        cols = slice(i * dim, (i + 1) * dim)
        block = w_ref[i * per : (i + 1) * per, low : low + wide, :].reshape(dim, dim)
        up = up_ref[:, cols]
        slope = 0.5 * (1.0 + lax.erf(up * half_root)) + up * (
            density * jnp.exp(-0.5 * up * up)
        )
        gup = (nt(gdown, block) * slope).astype(bf16)
        gup_ref[:, cols] = gup
        stats_ref[11 + i : 12 + i] = over_words(gup.astype(f32))
        d_first = d_first + nt(gup, square(4 + i))
    stats_ref[6:7] = over_words(d_first * normal1)
    stats_ref[9:10] = over_words(d_first)
    d_res = normalize_back(d_first, normal1, scale1, small(6))
    gattn = d_res.astype(bf16)
    gattn_ref[...] = gattn
    stats_ref[3:4] = over_words(gattn.astype(f32))
    gatt_ref[...] = nt(gattn, square(3)).astype(bf16)
    for at in range(head_count // 2):
        cols = slice(at * pair, (at + 1) * pair)
        dq, dk, dv = [], None, None
        for side in range(2):
            gatt = of_head(gatt_ref[:, cols], side)
            probs = p_ref[2 * at + side]
            d_probs = nt(gatt, v_ref[:, cols])
            inner = jnp.sum(probs * d_probs, axis=-1, keepdims=True)
            gscore = (probs * (d_probs - inner)).astype(bf16)
            dq.append(nn(gscore, k_ref[:, cols]))
            more_k = tn(gscore, of_head(q_ref[:, cols], side))
            more_v = tn(probs.astype(bf16), gatt)
            dk = more_k if dk is None else dk + more_k
            dv = more_v if dv is None else dv + more_v
        gq_ref[:, cols] = (jnp.where(low_lane, dq[0], dq[1]) * scale).astype(bf16)
        gk_ref[:, cols] = (dk * scale).astype(bf16)
        gv_ref[:, cols] = dv.astype(bf16)
    stats_ref[1:2] = over_words(gq_ref[...].astype(f32))
    stats_ref[2:3] = over_words(gv_ref[...].astype(f32))
    for i in range(DEPTH):
        rows = slice(i * words, (i + 1) * words)
        piece = nt(gk_ref[rows, :], square(1)) + nt(gv_ref[rows, :], square(2))
        if i == 0:
            d_own_ref[...] = d_res + nt(gq_ref[...], square(0)) + piece
        else:
            (send1_ref, send2_ref, send3_ref)[i - 1][...] = piece.astype(bf16)


def encoder_grad_body(
    flag_ref,
    embs_ref,
    gq_ref,
    gk_ref,
    gv_ref,
    att_ref,
    gattn_ref,
    first_ref,
    act_ref,
    gup_ref,
    gdown_ref,
    stats_ref,
    keep_hbm,
    send_hbm,
    out_ref,
    sems,
):
    d = flag_ref[0]
    words, dim = gq_ref.shape
    part = dim // PLANE
    wide = act_ref.shape[1] // PLANE
    in_parts = gup_ref.shape[1] // dim
    pieces = []

    def put(low, high, value):
        out_ref[:, low:high, :] = value.reshape(PLANE, high - low, dim)

    def send(low, high):
        for i in range(PLANE // 2):
            for odd, hbm in ((1, send_hbm), (0, keep_hbm)):
                copy = pltpu.make_async_copy(
                    out_ref.at[d ^ odd ^ (2 * i), low:high, :],
                    hbm.at[i, low:high, :],
                    sems.at[len(pieces)],
                )
                copy.start()
                pieces.append(copy)

    low = (4 + in_parts) * part
    per = dim // wide
    for i in range(in_parts):
        cols = slice(i * dim, (i + 1) * dim)
        out_ref[i * per : (i + 1) * per, low : low + wide, :] = (
            tn(act_ref[:, cols], gdown_ref[...]).astype(bf16).reshape(per, wide, dim)
        )
    tail = jnp.broadcast_to(stats_ref[...].astype(bf16)[None], (PLANE,) + stats_ref.shape)
    out_ref[:, low + wide :, :] = tail
    send(low, out_ref.shape[1])
    for i in range(in_parts):
        cols = slice(i * dim, (i + 1) * dim)
        put((4 + i) * part, (5 + i) * part, tn(first_ref[...], gup_ref[:, cols]).astype(bf16))
    send(4 * part, low)
    put(3 * part, 4 * part, tn(att_ref[...], gattn_ref[...]).astype(bf16))
    put(0, part, tn(embs_ref[:words, :], gq_ref[...]).astype(bf16))
    put(part, 2 * part, tn(embs_ref[...], gk_ref[...]).astype(bf16))
    put(2 * part, 3 * part, tn(embs_ref[...], gv_ref[...]).astype(bf16))
    send(0, 4 * part)
    for copy in pieces:
        copy.wait()


def encoder(flag, embedded, others, small, query_segs, key_segs, key_pads, cotangent, weights):
    words, dim = embedded.shape
    keys = DEPTH * words
    head_count = dim // HDIM
    part = dim // PLANE
    in_parts = 4
    ff_dim = in_parts * dim
    vmem = pl.BlockSpec(memory_space=pltpu.VMEM)
    hbm = pl.BlockSpec(memory_space=pl.ANY)
    shapes = [
        ((words, dim), bf16),
        ((words, dim), f32),
        ((words, dim), bf16),
        ((words, dim), bf16),
        ((words, dim), bf16),
        ((keys, dim), bf16),
        ((words, dim), bf16),
        ((keys, dim), bf16),
        ((keys, dim), bf16),
        ((words, dim), bf16),
        ((words, dim), bf16),
        ((words, dim), bf16),
        ((words, ff_dim), bf16),
        ((words, ff_dim), bf16),
        ((words, dim), bf16),
        ((16, dim), f32),
    ]
    outs = pl.pallas_call(
        functools.partial(encoder_body, head_count, in_parts),
        out_shape=[jax.ShapeDtypeStruct(s, t) for s, t in shapes],
        in_specs=[SMEM_SPEC] + [vmem] * 9 + [hbm],
        out_specs=[vmem] * len(shapes),
        scratch_shapes=[
            VMEM(weights.shape, bf16),
            VMEM((words, dim), bf16),
            VMEM((keys, dim), bf16),
            VMEM((keys, dim), bf16),
            VMEM((head_count, words, keys), f32),
            VMEM((words, ff_dim), f32),
            VMEM((words, dim), bf16),
            pltpu.SemaphoreType.DMA((4,)),
        ],
        name="encoder",
        cost_estimate=cost(16e9, 30e6),
        compiler_params=pltpu.CompilerParams(vmem_limit_bytes=58 * 1024 * 1024),
    )(flag, embedded, *others, small, query_segs, key_segs, key_pads, cotangent, weights)
    result, d_own = outs[:2]
    d_embedded = d_own
    first = None
    for offset in range(1, DEPTH):
        piece = swap(outs[1 + offset], "seq", DEPTH, offset)
        first = piece if first is None else first
        d_embedded = d_embedded + piece.astype(f32)
    saved = [tie(outs[5], first), *outs[6:]]
    rows = (4 + in_parts) * part + ff_dim // PLANE + 16
    grads = pl.pallas_call(
        encoder_grad_body,
        out_shape=[jax.ShapeDtypeStruct((PLANE // 2, rows, dim), bf16)] * 2,
        in_specs=[SMEM_SPEC] + [vmem] * 11,
        out_specs=[hbm] * 2,
        scratch_shapes=[VMEM((PLANE, rows, dim), bf16), pltpu.SemaphoreType.DMA((3 * PLANE,))],
        name="encoder_grad",
        cost_estimate=cost(6e9, 20e6),
        compiler_params=pltpu.CompilerParams(vmem_limit_bytes=58 * 1024 * 1024),
    )(flag, *saved)
    return result, d_embedded, grads


def round_up(value, multiple):
    return -(-value // multiple) * multiple


def plane_shards(
    char_ids,
    segment_ids,
    pad_mask,
    cotangent,
    char_table,
    conv_weight,
    conv_bias,
    hw_weight,
    hw_bias,
    proj_weight,
    pos_table,
    qkv_weight,
    out_weight,
    ff_in_weight,
    ff_out_weight,
    ff_in_bias,
    d_biases,
    norm_gain,
    norm_shift,
):
    d = lax.axis_index("dp")
    z = lax.axis_index("seq")
    dvec = d.astype(jnp.int32)[None]
    words, char_len = char_ids.shape[1:]
    all_words = PLANE * words
    tap_count, char_dim, filters = conv_weight.shape
    chars = char_table.shape[0]
    own = filters // PLANE
    depth = hw_weight.shape[0]
    model_dim = cotangent.shape[2]
    seq_len = segment_ids.shape[1]
    head_count = model_dim // HDIM
    part = model_dim // PLANE
    ff_dim = ff_out_weight.shape[0] * PLANE
    lanes = GROUP * char_dim
    held = round_up(char_len * char_dim, lanes)
    score_scale = HDIM ** (-0.5)

    ids = char_ids.reshape(words, char_len)
    table_rows = round_up(chars, 128)
    table = jnp.pad(jnp.tile(char_table, (1, GROUP)), ((0, table_rows - chars), (0, 0)))
    (own_x,) = call(
        functools.partial(lookup_body, char_len),
        [((words + EXTRA_ROWS, held), bf16)],
        z.astype(jnp.int32)[None],
        (ids, table, hw_bias, d_biases, norm_gain, norm_shift, ff_in_bias[None, :], pos_table),
        [VMEM((EXTRA_ROWS, held), f32)],
        name="lookup",
    )
    hw_weight, qkv_weight, unused = lax.optimization_barrier((hw_weight, qkv_weight, own_x))
    hw_packed = pack_highway(hw_weight)

    x_blocks = plane_gather(own_x, hw_packed)
    hw_cols = [lax.all_to_all(tie(hw_packed[0], x_blocks[2]), "dp", 0, 0)]

    in_parts = ff_in_weight.shape[1] // model_dim
    weight_rows = (4 + in_parts) * part + ff_dim // PLANE
    packed = pl.pallas_call(
        pack_encoder_body,
        out_shape=jax.ShapeDtypeStruct((weight_rows, model_dim), bf16),
        name="pack_encoder",
    )(qkv_weight, out_weight, ff_in_weight, ff_out_weight)
    widths = filter_widths(filters)
    widths_row = jnp.asarray(widths[None, :], jnp.int32)
    taps = conv_weight.reshape(tap_count * char_dim, filters)
    taps_shape = VMEM((2 * lanes, GROUP * own), bf16)
    hidden0, hidden0_b, top_at, x_all, bias_a, bias_b, extras = call(
        functools.partial(conv_body, char_len, char_len - tap_count + 1, words),
        [
            ((all_words, own), f32),
            ((all_words, own), bf16),
            ((all_words, own), jnp.int32),
            ((all_words, held + lanes), bf16),
            ((16, own), f32),
            ((16, own), f32),
            ((PLANE, EXTRA_ROWS, held), bf16),
        ],
        dvec,
        (*x_blocks, taps, widths_row, conv_bias[None, :]),
        [taps_shape, VMEM((PLANE, 16, 2 * own), f32)],
        name="conv",
        flops=8e9,
    )

    hidden, hidden_b = hidden0, hidden0_b
    saved = []
    for layer in range(depth):
        blocks = plane_gather(hidden_b, (hw_cols[layer],))
        if layer + 1 < depth:
            following, packed = tie((hw_packed[layer + 1], packed), blocks)
            hw_cols.append(lax.all_to_all(following, "dp", 0, 0))
        if layer == 0:
            gathered = lax.all_gather(packed, "dp", axis=0, tiled=False)
        opened, ra, following, following_b = highway(
            layer, dvec, blocks, hw_cols[layer], bias_a, bias_b, hidden
        )
        saved.append((blocks, opened, ra, hidden))
        hidden, hidden_b = following, following_b
    vectors = extras[:, VECTOR_ROW : VECTOR_ROW + 11, :part].astype(f32)
    inner_bias = extras[:, VECTOR_ROW + 11, : ff_dim // PLANE].reshape(in_parts, model_dim)
    small_full = jnp.concatenate(
        [
            vectors.transpose(1, 0, 2).reshape(11, model_dim),
            inner_bias.astype(f32),
            jnp.zeros((16 - 11 - in_parts, model_dim), f32),
        ],
        axis=0,
    )
    per = EXTRA_ROWS - POS_ROW
    pos_full = (
        extras[:, POS_ROW:, : (words // per) * part]
        .reshape(PLANE, per, words // per, part)
        .transpose(2, 1, 0, 3)
        .reshape(words, model_dim)
    )

    half = PLANE // 2
    keep, send = call(
        project_body,
        [((half, words, model_dim), f32), ((half, words, model_dim), bf16)],
        dvec,
        (hidden_b, proj_weight),
        name="project",
    )
    projected = plane_reduce(keep, send) + small_full[0]

    summed = projected + pos_full.astype(f32)
    normal0, scale0 = normalize(summed)
    embedded = normal0 * small_full[5] + small_full[8]
    embedded_b = embedded.astype(bf16)
    others = [swap(embedded_b, "seq", DEPTH, offset) for offset in range(1, DEPTH)]

    def by_offset(row):
        pieces = row.reshape(DEPTH, words)
        return jnp.concatenate(
            [lax.dynamic_index_in_dim(pieces, z ^ offset, 0) for offset in range(DEPTH)], axis=1
        )

    key_segs, key_pads = by_offset(segment_ids), by_offset(pad_mask)
    result, d_embedded, (enc_keep, enc_send) = encoder(
        dvec,
        embedded,
        others,
        small_full,
        key_segs[0, :words, None],
        key_segs,
        key_pads,
        cotangent.reshape(words, model_dim),
        gathered,
    )
    enc_arrived = plane_swap(enc_send, CORE_PARTNER)
    d_summed = normalize_back(d_embedded, normal0, scale0, small_full[5])
    grad_proj = jnp.concatenate(
        [
            d_summed.astype(bf16),
            over_words(d_embedded * normal0).astype(bf16),
            over_words(d_embedded).astype(bf16),
            jnp.zeros((14, model_dim), bf16),
        ],
        axis=0,
    )

    gp_blocks = plane_gather(grad_proj)
    d_hidden, proj_grad, top_sums = call(
        functools.partial(unproject_body, words),
        [((all_words, own), f32), ((own, model_dim), bf16), ((words + 32, model_dim), f32)],
        dvec,
        (*gp_blocks, proj_weight, hidden_b),
        name="unproject",
    )
    hw_sums, gate_parts, quarters = {}, {}, {}
    enc_parts = None
    for layer in reversed(range(depth)):
        blocks, opened, ra, hidden = saved[layer]
        ga, gb, d_carry, sums, keep, send = highway_back(
            layer, dvec, d_hidden, opened, ra, hidden, hw_cols[layer]
        )
        parts = plane_parts(keep, send)
        gate_parts[layer] = jnp.sum(sums, axis=0).reshape(2, own)
        (cols_grad,) = call(
            highway_grad_body,
            [((DEPTH, PLANE, own // DEPTH, 2 * own), bf16)],
            dvec,
            (*blocks, tie(ga, parts[1]), gb),
            name=f"highway_grad{layer}",
            flops=2 * all_words * filters * 2 * own,
        )
        after = [cols_grad]
        quarter = lax.psum_scatter(cols_grad, "seq", scatter_dimension=0, tiled=False)
        quarters[layer] = lax.all_to_all(quarter, "dp", 0, 0)
        hw_sums[layer] = lax.all_gather(quarters[layer], "seq", axis=0, tiled=False)
        if enc_parts is None:
            arrived = tie(enc_arrived, parts[1], cols_grad)
            enc_parts = [enc_keep[0].astype(f32) + arrived[0].astype(f32)] + [
                (enc_keep[i].astype(f32) + arrived[i].astype(f32)).astype(bf16)
                for i in range(1, half)
            ]
            enc_rest = [plane_swap(enc_parts[i], 2 * i) for i in range(1, half)]
            after.append(enc_parts[1])
        d_hidden = d_carry + plane_total(parts, after)
    enc_sum = enc_parts[0]
    for piece in enc_rest[:-1]:
        enc_sum = enc_sum + tie(piece, d_hidden).astype(f32)
    d_hidden = tie(d_hidden, enc_sum, *[quarters[other] for other in range(1, depth)])
    grad_pooled, keep, send = call(
        functools.partial(char_back_body, char_len, words),
        [
            ((all_words, own), bf16),
            ((half, words, held), f32),
            ((half, words, held), bf16),
        ],
        dvec,
        (hidden0, top_at, d_hidden, taps, widths_row),
        [
            taps_shape,
            VMEM((2 * words, GROUP * own), bf16),
            VMEM((all_words, held + lanes), f32),
        ],
        name="char_back",
        flops=8e9,
    )
    parts = plane_parts(keep, send)
    grad_pooled = tie(grad_pooled, parts[1])
    (conv_part,) = call(
        functools.partial(conv_grad_body, char_len),
        [((tap_count * char_dim + 8, own), f32)],
        dvec,
        (x_all, top_at, grad_pooled),
        [VMEM((all_words, GROUP * own), bf16), VMEM((2 * lanes, all_words), bf16)],
        name="conv_grad",
        flops=8e9,
    )
    enc_slice = (tie(enc_sum, conv_part) + enc_rest[-1].astype(f32)).astype(bf16)
    top_own = lax.dynamic_slice_in_dim(top_sums, d * part, part, 1).astype(bf16)
    top_own = jnp.pad(top_own, ((0, 0), (0, 128 - part)))
    top_all = lax.dynamic_update_slice_in_dim(
        jnp.zeros((seq_len, 128), bf16), top_own[:words], z * words, 0
    )
    cut = (4 + in_parts) * part
    lines = [enc_slice[:cut], enc_slice[cut:], proj_grad, jnp.concatenate([top_all, top_own[words:]], axis=0)]
    moved = [line_step(value, 0) for value in lines]
    char_grads = tie(plane_total(parts, (conv_part, enc_slice)), quarters[0])
    fold_rows = round_up(-(-chars // GROUP), 8)
    (table_part,) = call(
        functools.partial(table_grad_body, char_len),
        [((fold_rows, lanes), f32)],
        dvec,
        (ids.T, char_grads),
        name="table_grad",
        flops=2e9,
    )
    gate_rows = jnp.concatenate([gate_parts[layer] for layer in range(depth)], axis=0)
    ends = jnp.concatenate(
        [
            conv_part,
            jnp.pad(gate_rows, ((0, 8 - 2 * depth), (0, 0))),
            jnp.pad(table_part, ((0, 0), (0, own - lanes))),
        ],
        axis=0,
    )
    ends = ends + swap(ends, "seq", DEPTH, 1)
    ends = ends + swap(ends, "seq", DEPTH, 2)
    lines = [value + tie(piece, ends) for value, piece in zip(lines, moved)]
    moved = [line_step(value, 1) for value in lines]
    end_blocks = plane_gather(ends)
    conv_rows = tap_count * char_dim
    conv_total, conv_bias_total, gate_sums, table_total = call(
        finish_ends_body,
        [
            ((conv_rows, filters), f32),
            ((8, filters), f32),
            ((8, filters), f32),
            ((fold_rows, lanes), f32),
        ],
        dvec,
        (*end_blocks, widths_row),
        [VMEM((PLANE, fold_rows, lanes), f32)],
        name="finish_ends",
    )
    conv_total = conv_total.reshape(tap_count, char_dim, filters)
    conv_bias_total = conv_bias_total[0]
    table_total = (
        table_total.reshape(fold_rows, GROUP, char_dim)
        .transpose(1, 0, 2)
        .reshape(GROUP * fold_rows, char_dim)[:chars]
    )

    lines = [value + tie(piece, ends) for value, piece in zip(lines, moved)]
    moved = [line_step(value, 2) for value in lines]
    middle = (z == 1) | (z == 2)
    *enc_total, proj_total, top_total = (
        jnp.where(middle, value, piece) for value, piece in zip(lines, moved)
    )
    top_total = top_total[:, :part].astype(f32)
    pos_total = top_total[:seq_len]
    gain0, shift0, bias0 = top_total[seq_len], top_total[seq_len + 1], top_total[seq_len + 16]
    proj_total = proj_total.astype(f32)
    qkv_total, out_total, inner_total, outer_total, small_total = call(
        finish_encoder_body,
        [
            ((part, 3 * model_dim), f32),
            ((part, model_dim), f32),
            ((part, ff_dim), f32),
            ((ff_dim // PLANE, model_dim), f32),
            ((16, model_dim), f32),
        ],
        dvec,
        enc_total,
        name="finish_encoder",
    )
    own_small = lax.dynamic_slice_in_dim(small_total, d * part, part, 1)
    bias_total = jnp.concatenate([bias0[None], own_small[1:5]], axis=0)
    gain_total = jnp.concatenate([gain0[None], own_small[6:8]], axis=0)
    shift_total = jnp.concatenate([shift0[None], own_small[9:11]], axis=0)
    inner_bias_total = lax.dynamic_slice_in_dim(
        small_total[11 : 11 + in_parts].reshape(-1), d * (ff_dim // PLANE), ff_dim // PLANE, 0
    )

    hw_total, hw_bias_totals = None, [None] * depth
    for layer in reversed(range(depth)):
        hw_total = finish_highway(layer, depth, hw_sums[layer], hw_total)
        row = gate_sums[2 * layer : 2 * layer + 2].reshape(-1)
        hw_bias_totals[layer] = lax.dynamic_slice_in_dim(row, d * 2 * own, 2 * own, 0)

    output = result.reshape(1, words, model_dim)
    return (
        output,
        table_total,
        conv_total,
        conv_bias_total,
        hw_total,
        jnp.stack(hw_bias_totals),
        proj_total,
        pos_total,
        qkv_total,
        out_total,
        inner_total,
        outer_total,
        inner_bias_total,
        bias_total,
        gain_total,
        shift_total,
    )


def solution(mesh):
    placed = (
        P("dp", "seq", None),
        P("dp", None),
        P("dp", None),
        P("dp", "seq", None),
        P(),
        P(),
        P(),
        P(None, "dp", None),
        P(None, "dp"),
        P("dp", None),
        P(None, "dp"),
        P("dp", None),
        P("dp", None),
        P("dp", None),
        P("dp", None),
        P("dp"),
        P(None, "dp"),
        P(None, "dp"),
        P(None, "dp"),
    )
    plane, depth = mesh.shape["dp"], mesh.shape["seq"]
    step = plane_shards if (plane, depth) == (PLANE, DEPTH) else shards
    return jax.shard_map(
        step,
        mesh=mesh,
        in_specs=placed,
        out_specs=(
            P("dp", "seq", None),
            P(),
            P(),
            P(),
            P(None, "dp", None),
            P(None, "dp"),
            P("dp", None),
            P(None, "dp"),
            P("dp", None),
            P("dp", None),
            P("dp", None),
            P("dp", None),
            P("dp"),
            P(None, "dp"),
            P(None, "dp"),
            P(None, "dp"),
        ),
        check_vma=False,
    )
```

```python
import functools
import math

import jax
import jax.numpy as jnp
import numpy as np
from jax import lax
from jax.experimental import pallas as pl
from jax.experimental.pallas import tpu as pltpu
from jax.sharding import PartitionSpec as P

HDIM = 64


eps_norm = 1e-12
masked_score = -1e30
width_shares = (1, 1, 2, 4, 8, 16, 32)


def filter_widths(filters):
    per_share = filters // 64
    return np.repeat(
        np.arange(1, len(width_shares) + 1),
        [per_share * share_count for share_count in width_shares],
    )


def layer_norm(inputs, gain_row, shift_row):
    centred = inputs - jnp.mean(inputs, axis=-1, keepdims=True)
    spread = jnp.mean(centred * centred, axis=-1, keepdims=True)
    return centred * lax.rsqrt(spread + eps_norm) * gain_row + shift_row


def highway_mix(gate_values, carried):
    filters = carried.shape[-1]
    opened = jax.nn.sigmoid(gate_values[:, filters:])
    return opened * carried + (1.0 - opened) * jax.nn.relu(gate_values[:, :filters])


def gelu_exact(inputs):
    return jax.nn.gelu(inputs, approximate=False)


def product(left_side, right_side):
    return jnp.dot(left_side, right_side, preferred_element_type=jnp.float32)


def product_tn(left_side, right_side):
    return lax.dot_general(
        left_side, right_side, (((0,), (0,)), ((), ())), preferred_element_type=jnp.float32
    )


def product_nt(left_side, right_side):
    return lax.dot_general(
        left_side, right_side, (((1,), (1,)), ((), ())), preferred_element_type=jnp.float32
    )


def char_windows(word_ids, char_rows, tap_count):
    word_count, char_len = word_ids.shape
    char_count = char_rows.shape[0]
    onehot = (
        word_ids.reshape(-1)[:, None] == jnp.arange(char_count, dtype=jnp.int32)[None, :]
    ).astype(jnp.bfloat16)
    vectors = product(onehot, char_rows).astype(jnp.bfloat16).reshape(word_count, char_len, -1)
    padded = jnp.pad(vectors, ((0, 0), (0, tap_count - 1), (0, 0)))
    char_taps = jnp.stack(
        [padded[:, tap_index : tap_index + char_len, :] for tap_index in range(tap_count)], axis=2
    )
    return (onehot, char_taps.reshape(word_count * char_len, -1))


def shards(
    char_ids,
    segment_ids,
    pad_mask,
    cotangent,
    char_table,
    conv_weight,
    conv_bias,
    hw_weight,
    hw_bias,
    proj_weight,
    pos_table,
    qkv_weight,
    out_weight,
    ff_in_weight,
    ff_out_weight,
    ff_in_bias,
    d_biases,
    norm_gain,
    norm_shift,
):
    (
        highway_full,
        highway_bias,
        proj_full,
        pos_full,
        qkv_full,
        out_full,
        inner_full,
        outer_full,
        inner_bias,
        bias_full,
        gain_full,
        shift_full,
    ) = (
        lax.all_gather(hw_weight, "dp", axis=1, tiled=True),
        lax.all_gather(hw_bias, "dp", axis=1, tiled=True),
        lax.all_gather(proj_weight, "dp", axis=0, tiled=True),
        lax.all_gather(pos_table, "dp", axis=1, tiled=True),
        lax.all_gather(qkv_weight, "dp", axis=0, tiled=True),
        lax.all_gather(out_weight, "dp", axis=0, tiled=True),
        lax.all_gather(ff_in_weight, "dp", axis=0, tiled=True),
        lax.all_gather(ff_out_weight, "dp", axis=0, tiled=True),
        lax.all_gather(ff_in_bias, "dp", axis=0, tiled=True),
        lax.all_gather(d_biases, "dp", axis=1, tiled=True),
        lax.all_gather(norm_gain, "dp", axis=1, tiled=True),
        lax.all_gather(norm_shift, "dp", axis=1, tiled=True),
    )
    seqs_here, local_len, char_len = char_ids.shape
    tap_count, char_dim, filters = conv_weight.shape
    model_dim = cotangent.shape[2]
    seq_len = segment_ids.shape[1]
    head_count = model_dim // HDIM
    highway_depth = highway_full.shape[0]
    word_count = seqs_here * local_len
    score_scale = HDIM ** (-0.5)
    bias_rows = bias_full.astype(jnp.float32)
    gain_rows = gain_full.astype(jnp.float32)
    shift_rows = shift_full.astype(jnp.float32)
    widths = filter_widths(filters)
    tap_mask = np.arange(tap_count)[:, None] < widths[None, :]
    masked_kernel = (conv_weight * jnp.asarray(tap_mask, jnp.bfloat16)[:, None, :]).reshape(
        tap_count * char_dim, filters
    )
    valid_place = jnp.asarray(np.arange(char_len)[:, None] <= char_len - widths[None, :])
    word_block = math.gcd(word_count, 32)
    block_count = word_count // word_block
    id_blocks = char_ids.reshape(block_count, word_block, char_len)

    def embed_forward(block_ids):
        unused, char_taps = char_windows(block_ids, char_table, tap_count)
        conv_out = (product(char_taps, masked_kernel) + conv_bias.astype(jnp.float32)).reshape(
            word_block, char_len, filters
        )
        conv_out = jnp.where(valid_place[None], conv_out, masked_score)
        return (jnp.max(conv_out, axis=1), jnp.argmax(conv_out, axis=1))

    pooled, top_place = lax.map(embed_forward, id_blocks)
    pooled = pooled.reshape(word_count, filters)
    hidden = jax.nn.relu(pooled)
    carried_list = []
    gates_list = []
    for highway_layer in range(highway_depth):
        carried_list.append(hidden)
        gate_values = product(
            hidden.astype(jnp.bfloat16), highway_full[highway_layer]
        ) + highway_bias[highway_layer].astype(jnp.float32)
        gates_list.append(gate_values)
        hidden = highway_mix(gate_values, hidden)
    top_hidden = hidden.astype(jnp.bfloat16)
    projected = product(top_hidden, proj_full) + bias_rows[0]
    row_start = lax.axis_index("seq") * local_len
    pos_rows = lax.dynamic_slice_in_dim(pos_full, row_start, local_len, 0).astype(jnp.float32)
    summed = (projected.reshape(seqs_here, local_len, model_dim) + pos_rows[None]).reshape(
        word_count, model_dim
    )
    embedded = layer_norm(summed, gain_rows[0], shift_rows[0])
    embedded_b = embedded.astype(jnp.bfloat16)
    qkv_shift = jnp.concatenate([bias_rows[1], jnp.zeros_like(bias_rows[1]), bias_rows[2]])
    qkv = (product(embedded_b, qkv_full) + qkv_shift).astype(jnp.bfloat16)
    queries = qkv[:, :model_dim].reshape(seqs_here, local_len, head_count, HDIM)
    keys_local = qkv[:, model_dim : 2 * model_dim].reshape(seqs_here, local_len, model_dim)
    values_local = qkv[:, 2 * model_dim :].reshape(seqs_here, local_len, model_dim)
    keys_full, values_full = (
        lax.all_gather(keys_local, "seq", axis=1, tiled=True),
        lax.all_gather(values_local, "seq", axis=1, tiled=True),
    )
    query_segs = lax.dynamic_slice_in_dim(segment_ids, row_start, local_len, 1)
    query_pos = row_start + jnp.arange(local_len, dtype=jnp.int32)
    same_segment = query_segs[:, :, None] == segment_ids[:, None, :]
    open_key = (pad_mask[:, None, :] == 0) | (
        query_pos[:, None] == jnp.arange(seq_len, dtype=jnp.int32)[None, :]
    )[None]
    allowed = (same_segment & open_key)[:, None]

    def score_of(key_rows):
        raw_scores = (
            jnp.einsum(
                "sqhd,skhd->shqk",
                queries,
                key_rows.reshape(seqs_here, seq_len, head_count, HDIM),
                preferred_element_type=jnp.float32,
            )
            * score_scale
        )
        return jnp.where(allowed, raw_scores, masked_score)

    scores = score_of(keys_full)
    row_top = jnp.max(scores, axis=-1, keepdims=True)
    exp_scores = jnp.exp(scores - row_top)
    denominator = jnp.sum(exp_scores, axis=-1, keepdims=True)
    attn_probs = (exp_scores / denominator).astype(jnp.bfloat16)
    log_total = row_top + jnp.log(denominator)
    attended = (
        jnp.einsum(
            "shqk,skhd->sqhd",
            attn_probs,
            values_full.reshape(seqs_here, seq_len, head_count, HDIM),
            preferred_element_type=jnp.float32,
        )
        .reshape(word_count, model_dim)
        .astype(jnp.bfloat16)
    )
    attn_out = product(attended, out_full) + bias_rows[3]
    first_input = embedded + attn_out
    first_norm = layer_norm(first_input, gain_rows[1], shift_rows[1])
    first_b = first_norm.astype(jnp.bfloat16)
    ffn_up = product(first_b, inner_full) + inner_bias.astype(jnp.float32)
    ffn_act = gelu_exact(ffn_up).astype(jnp.bfloat16)
    ffn_down = product(ffn_act, outer_full) + bias_rows[4]
    second = first_norm + ffn_down
    result = layer_norm(second, gain_rows[2], shift_rows[2])
    grad_out = cotangent.reshape(word_count, model_dim).astype(jnp.float32)
    unused, norm_back = jax.vjp(layer_norm, second, gain_rows[2], shift_rows[2])
    d_second, gain_grad2, shift_grad2 = norm_back(grad_out)
    grad_down = d_second.astype(jnp.bfloat16)
    outer_grad = product_tn(ffn_act, grad_down)
    bias_grad4 = jnp.sum(grad_down.astype(jnp.float32), axis=0)
    unused, gelu_back = jax.vjp(gelu_exact, ffn_up)
    grad_up = gelu_back(product_nt(grad_down, outer_full))[0].astype(jnp.bfloat16)
    inner_grad = product_tn(first_b, grad_up)
    inner_bias_grad = jnp.sum(grad_up.astype(jnp.float32), axis=0)
    d_first = d_second + product_nt(grad_up, inner_full)
    unused, norm_back = jax.vjp(layer_norm, first_input, gain_rows[1], shift_rows[1])
    d_res, gain_grad1, shift_grad1 = norm_back(d_first)
    grad_attn = d_res.astype(jnp.bfloat16)
    out_grad = product_tn(attended, grad_attn)
    bias_grad3 = jnp.sum(grad_attn.astype(jnp.float32), axis=0)
    grad_attended = (
        product_nt(grad_attn, out_full)
        .astype(jnp.bfloat16)
        .reshape(seqs_here, local_len, head_count, HDIM)
    )
    keys_back, values_back = (keys_full, values_full)
    probs_again = jnp.exp(score_of(keys_back) - log_total)
    probs_again_b = probs_again.astype(jnp.bfloat16)
    key_heads = keys_back.reshape(seqs_here, seq_len, head_count, HDIM)
    value_heads = values_back.reshape(seqs_here, seq_len, head_count, HDIM)
    d_probs = jnp.einsum(
        "sqhd,skhd->shqk", grad_attended, value_heads, preferred_element_type=jnp.float32
    )
    grad_scores = (
        probs_again * (d_probs - jnp.sum(probs_again * d_probs, axis=-1, keepdims=True))
    ).astype(jnp.bfloat16)
    d_queries = (
        jnp.einsum("shqk,skhd->sqhd", grad_scores, key_heads, preferred_element_type=jnp.float32)
        * score_scale
    )
    d_keys_all = (
        jnp.einsum("shqk,sqhd->skhd", grad_scores, queries, preferred_element_type=jnp.float32)
        * score_scale
    )
    d_values_all = jnp.einsum(
        "shqk,sqhd->skhd", probs_again_b, grad_attended, preferred_element_type=jnp.float32
    )
    d_keys, d_values = (
        lax.psum_scatter(
            d_keys_all.reshape(seqs_here, seq_len, model_dim).astype(jnp.bfloat16),
            "seq",
            scatter_dimension=1,
            tiled=True,
        ).astype(jnp.float32),
        lax.psum_scatter(
            d_values_all.reshape(seqs_here, seq_len, model_dim).astype(jnp.bfloat16),
            "seq",
            scatter_dimension=1,
            tiled=True,
        ).astype(jnp.float32),
    )
    grad_qkv = jnp.concatenate(
        [
            d_queries.reshape(word_count, model_dim),
            d_keys.reshape(word_count, model_dim),
            d_values.reshape(word_count, model_dim),
        ],
        axis=1,
    ).astype(jnp.bfloat16)
    qkv_grad = product_tn(embedded_b, grad_qkv)
    bias_grad1 = jnp.sum(grad_qkv[:, :model_dim].astype(jnp.float32), axis=0)
    bias_grad2 = jnp.sum(grad_qkv[:, 2 * model_dim :].astype(jnp.float32), axis=0)
    d_embedded = d_res + product_nt(grad_qkv, qkv_full)
    unused, norm_back = jax.vjp(layer_norm, summed, gain_rows[0], shift_rows[0])
    d_summed, gain_grad0, shift_grad0 = norm_back(d_embedded)
    pos_local = jnp.sum(d_summed.reshape(seqs_here, local_len, model_dim), axis=0)
    pos_grad = lax.dynamic_update_slice_in_dim(
        jnp.zeros((seq_len, model_dim), jnp.float32), pos_local, row_start, 0
    )
    grad_proj = d_summed.astype(jnp.bfloat16)
    proj_grad = product_tn(top_hidden, grad_proj)
    bias_grad0 = jnp.sum(grad_proj.astype(jnp.float32), axis=0)
    d_hidden = product_nt(grad_proj, proj_full)
    kernel_grads = [None] * highway_depth
    shift_grads = [None] * highway_depth
    for highway_layer in reversed(range(highway_depth)):
        carried = carried_list[highway_layer]
        unused, mix_back = jax.vjp(highway_mix, gates_list[highway_layer], carried)
        d_gates, d_carried = mix_back(d_hidden)
        grad_gates = d_gates.astype(jnp.bfloat16)
        kernel_grads[highway_layer] = product_tn(carried.astype(jnp.bfloat16), grad_gates)
        shift_grads[highway_layer] = jnp.sum(grad_gates.astype(jnp.float32), axis=0)
        d_hidden = d_carried + product_nt(grad_gates, highway_full[highway_layer])
    grad_pooled = jnp.where(pooled > 0, d_hidden, 0.0).astype(jnp.bfloat16)

    def embed_backward(running, inputs):
        weight_sum, bias_sum, table_sum = running
        block_ids, place_block, grad_block = inputs
        onehot, char_taps = char_windows(block_ids, char_table, tap_count)
        grad_conv = jnp.where(
            jnp.arange(char_len, dtype=jnp.int32)[None, :, None] == place_block[:, None, :],
            grad_block[:, None, :],
            jnp.zeros((), jnp.bfloat16),
        ).reshape(word_block * char_len, filters)
        weight_sum = weight_sum + product_tn(char_taps, grad_conv)
        bias_sum = bias_sum + jnp.sum(grad_block.astype(jnp.float32), axis=0)
        d_taps = product_nt(grad_conv, masked_kernel).reshape(
            word_block, char_len, tap_count, char_dim
        )
        spread = jnp.zeros((word_block, char_len + tap_count - 1, char_dim), jnp.float32)
        for tap_index in range(tap_count):
            spread = spread.at[:, tap_index : tap_index + char_len].add(d_taps[:, :, tap_index])
        grad_chars = (
            spread[:, :char_len].reshape(word_block * char_len, char_dim).astype(jnp.bfloat16)
        )
        table_sum = table_sum + product_tn(onehot, grad_chars)
        return ((weight_sum, bias_sum, table_sum), None)

    start_sums = (
        jnp.zeros((tap_count * char_dim, filters), jnp.float32),
        jnp.zeros((filters,), jnp.float32),
        jnp.zeros(char_table.shape, jnp.float32),
    )
    conv_sums, unused = lax.scan(
        embed_backward,
        start_sums,
        (id_blocks, top_place, grad_pooled.reshape(block_count, word_block, filters)),
    )
    conv_weight_grad = (
        conv_sums[0] * jnp.asarray(np.repeat(tap_mask, char_dim, axis=0), jnp.float32)
    ).reshape(tap_count, char_dim, filters)
    table_total, conv_total, conv_bias_total = lax.psum(
        (conv_sums[2], conv_weight_grad, conv_sums[1]), ("dp", "seq")
    )
    weight_grads = (
        jnp.stack(kernel_grads),
        jnp.stack(shift_grads),
        proj_grad,
        pos_grad,
        qkv_grad,
        out_grad,
        inner_grad,
        outer_grad,
        inner_bias_grad,
        jnp.stack([bias_grad0, bias_grad1, bias_grad2, bias_grad3, bias_grad4]),
        jnp.stack([gain_grad0, gain_grad1, gain_grad2]),
        jnp.stack([shift_grad0, shift_grad1, shift_grad2]),
    )
    sliced = (
        lax.psum_scatter(weight_grads[0], "dp", scatter_dimension=1, tiled=True),
        lax.psum_scatter(weight_grads[1], "dp", scatter_dimension=1, tiled=True),
        lax.psum_scatter(weight_grads[2], "dp", scatter_dimension=0, tiled=True),
        lax.psum_scatter(weight_grads[3], "dp", scatter_dimension=1, tiled=True),
        lax.psum_scatter(weight_grads[4], "dp", scatter_dimension=0, tiled=True),
        lax.psum_scatter(weight_grads[5], "dp", scatter_dimension=0, tiled=True),
        lax.psum_scatter(weight_grads[6], "dp", scatter_dimension=0, tiled=True),
        lax.psum_scatter(weight_grads[7], "dp", scatter_dimension=0, tiled=True),
        lax.psum_scatter(weight_grads[8], "dp", scatter_dimension=0, tiled=True),
        lax.psum_scatter(weight_grads[9], "dp", scatter_dimension=1, tiled=True),
        lax.psum_scatter(weight_grads[10], "dp", scatter_dimension=1, tiled=True),
        lax.psum_scatter(weight_grads[11], "dp", scatter_dimension=1, tiled=True),
    )
    summed_grads = (
        lax.psum(sliced[0].astype(jnp.bfloat16), "seq").astype(jnp.float32),
        lax.psum(sliced[1].astype(jnp.bfloat16), "seq").astype(jnp.float32),
        lax.psum(sliced[2].astype(jnp.bfloat16), "seq").astype(jnp.float32),
        lax.psum(sliced[3].astype(jnp.bfloat16), "seq").astype(jnp.float32),
        lax.psum(sliced[4].astype(jnp.bfloat16), "seq").astype(jnp.float32),
        lax.psum(sliced[5].astype(jnp.bfloat16), "seq").astype(jnp.float32),
        lax.psum(sliced[6].astype(jnp.bfloat16), "seq").astype(jnp.float32),
        lax.psum(sliced[7].astype(jnp.bfloat16), "seq").astype(jnp.float32),
        lax.psum(sliced[8].astype(jnp.bfloat16), "seq").astype(jnp.float32),
        lax.psum(sliced[9].astype(jnp.bfloat16), "seq").astype(jnp.float32),
        lax.psum(sliced[10].astype(jnp.bfloat16), "seq").astype(jnp.float32),
        lax.psum(sliced[11].astype(jnp.bfloat16), "seq").astype(jnp.float32),
    )
    output = result.astype(jnp.bfloat16).reshape(seqs_here, local_len, model_dim)
    return (output, table_total, conv_total, conv_bias_total) + tuple(summed_grads)


PLANE = 8
DEPTH = 4
CORE_PARTNER = 1
GROUP = 8

f32 = jnp.float32
bf16 = jnp.bfloat16


def swap(value, axis_name, size, offset):
    return lax.ppermute(value, axis_name, [(at, at ^ offset) for at in range(size)])


def plane_swap(value, offset):
    return swap(value, "dp", PLANE, offset)


def plane_gather(block, before=()):
    even = [block] + [plane_swap(block, offset) for offset in (2, 4, 6)]
    if before:
        even[1] = tie(even[1], *before)
    odd = [plane_swap(piece, CORE_PARTNER) for piece in even]
    return [piece for pair in zip(even, odd) for piece in pair]


def tie(value, *after):
    return lax.optimization_barrier((value, *after))[0]


def plane_parts(keep, send):
    arrived = plane_swap(send, CORE_PARTNER)
    own = keep[0].astype(f32) + arrived[0].astype(f32)
    return [own] + [
        (keep[i].astype(f32) + arrived[i].astype(f32)).astype(bf16) for i in range(1, PLANE // 2)
    ]


def plane_total(parts, after=()):
    total = tie(parts[0], *after)
    for i, part in enumerate(parts[1:], 1):
        total = total + plane_swap(part, 2 * i).astype(f32)
    return total


def plane_reduce(keep, send):
    return plane_total(plane_parts(keep, send))


LINE_STEPS = ([(0, 1), (3, 2)], [(1, 2), (2, 1)], [(1, 0), (2, 3)])


def line_step(value, step):
    return lax.ppermute(value, "seq", LINE_STEPS[step])


def nn(left_side, right_side):
    return jnp.dot(left_side, right_side, preferred_element_type=f32)


def nt(left_side, right_side):
    return lax.dot_general(
        left_side, right_side, (((1,), (1,)), ((), ())), preferred_element_type=f32
    )


def tn(left_side, right_side):
    return lax.dot_general(
        left_side, right_side, (((0,), (0,)), ((), ())), preferred_element_type=f32
    )


VMEM = pltpu.VMEM
SMEM_SPEC = pl.BlockSpec(memory_space=pltpu.SMEM)


def whole(count):
    return [pl.BlockSpec(memory_space=pltpu.VMEM)] * count


def cost(flops, moved):
    return pl.CostEstimate(flops=int(flops), transcendentals=0, bytes_accessed=int(moved))


def call(body, out_shapes, scalar, operands, scratch=(), name=None, flops=0):
    return pl.pallas_call(
        body,
        out_shape=[jax.ShapeDtypeStruct(s, t) for s, t in out_shapes],
        in_specs=[SMEM_SPEC] + whole(len(operands)),
        out_specs=whole(len(out_shapes)),
        scratch_shapes=list(scratch),
        name=name,
        cost_estimate=cost(
            flops,
            sum(x.size * x.dtype.itemsize for x in operands)
            + sum(math.prod(s) * jnp.dtype(t).itemsize for s, t in out_shapes),
        ),
        compiler_params=pltpu.CompilerParams(vmem_limit_bytes=58 * 1024 * 1024),
    )(scalar, *operands)


EXTRA_ROWS = 32
VECTOR_ROW = 2
POS_ROW = 16


def lookup_body(
    char_len,
    z_ref,
    ids_ref,
    table_ref,
    gate_ref,
    biases_ref,
    gain_ref,
    shift_ref,
    inner_ref,
    pos_ref,
    x_ref,
    extra_ref,
):
    words = ids_ref.shape[0]
    rows, lanes = table_ref.shape
    width = lanes // GROUP
    groups = x_ref.shape[1] // lanes
    lane = lax.broadcasted_iota(jnp.int32, (rows, lanes), 1) // width
    entry = lax.broadcasted_iota(jnp.int32, (words, rows), 1)
    total = jnp.zeros((groups * words, lanes), f32)
    for place in range(GROUP):
        pieces = []
        for group in range(groups):
            at = GROUP * group + place
            if at < char_len:
                hit = ids_ref[:, at : at + 1] == entry
                pieces.append(jnp.where(hit, 1.0, 0.0).astype(bf16))
            else:
                pieces.append(jnp.zeros((words, rows), bf16))
        own = jnp.where(lane == place, table_ref[...].astype(f32), 0.0).astype(bf16)
        total = total + nn(jnp.concatenate(pieces, axis=0), own)
    for group in range(groups):
        x_ref[:words, group * lanes : (group + 1) * lanes] = total[
            group * words : (group + 1) * words
        ].astype(bf16)
    extra_ref[...] = jnp.zeros_like(extra_ref)
    at = 0
    for ref in (gate_ref, biases_ref, gain_ref, shift_ref, inner_ref):
        extra_ref[at : at + ref.shape[0], : ref.shape[1]] = ref[...].astype(f32)
        at += ref.shape[0]
    per = EXTRA_ROWS - POS_ROW
    part = pos_ref.shape[1]
    for i in range(words // per):
        rows = pl.ds(pl.multiple_of(z_ref[0] * words + i * per, per), per)
        extra_ref[POS_ROW:, i * part : (i + 1) * part] = pos_ref[rows, :].astype(f32)
    x_ref[words:, :] = extra_ref[...].astype(bf16)


def fill_taps(d, taps_ref, weight_ref, widths_ref):
    depth = weight_ref.shape[0]
    filters = weight_ref.shape[1] // PLANE
    char_dim = taps_ref.shape[0] // (2 * GROUP)
    cols = pl.ds(pl.multiple_of(d * filters, filters), filters)
    tap = lax.broadcasted_iota(jnp.int32, (depth, filters), 0) // char_dim
    own = jnp.where(tap < widths_ref[:, cols], weight_ref[:, cols].astype(f32), 0.0).astype(bf16)
    taps_ref[...] = jnp.zeros_like(taps_ref)
    for place in range(GROUP):
        taps_ref[
            place * char_dim : place * char_dim + depth, place * filters : (place + 1) * filters
        ] = own


def conv_body(char_len, first_masked, words, d_ref, *refs):
    blocks = refs[:PLANE]
    (weight_ref, widths_ref, bias_ref, h_ref, hb_ref, at_ref, x_ref, ba_ref, bb_ref, all_extra_ref) = refs[
        PLANE : PLANE + 10
    ]
    taps_ref, extra_ref = refs[PLANE + 10 :]
    d = d_ref[0]
    filters = h_ref.shape[1]
    held = blocks[0].shape[1]
    lanes = taps_ref.shape[0] // 2
    fill_taps(d, taps_ref, weight_ref, widths_ref)
    cols = pl.ds(pl.multiple_of(d * filters, filters), filters)
    bias = bias_ref[:, cols].astype(f32)
    for k in range(PLANE):
        rows = pl.ds(pl.multiple_of((d ^ k) * words, words), words)
        x_ref[rows, :held] = blocks[k][:words, :]
        x_ref[rows, held:] = jnp.zeros((words, x_ref.shape[1] - held), bf16)
        extra_ref[d ^ k] = blocks[k][words : words + 16, : 2 * filters].astype(f32)
        all_extra_ref[d ^ k] = blocks[k][words:, :]
    for half, out in ((0, ba_ref), (PLANE // 2, bb_ref)):
        source = extra_ref[half + d // 2]
        out[...] = jnp.where(d % 2 == 0, source[:, :filters], source[:, filters:])
    last = char_len - widths_ref[:, cols]

    def one(step, carry):
        rows = pl.ds(pl.multiple_of(step * words, words), words)
        best = None
        for group in range(-(-char_len // GROUP)):
            count = min(GROUP, char_len - GROUP * group)
            values = nn(
                x_ref[rows, group * lanes : (group + 2) * lanes], taps_ref[:, : count * filters]
            )
            for place in range(count):
                at = GROUP * group + place
                value = values[:, place * filters : (place + 1) * filters]
                if at >= first_masked:
                    value = jnp.where(at <= last, value, masked_score)
                if best is None:
                    best, where = value, jnp.zeros(value.shape, jnp.int32)
                else:
                    where = jnp.where(value > best, at, where)
                    best = jnp.maximum(value, best)
        pooled = jnp.maximum(best + bias, 0.0)
        h_ref[rows, :] = pooled
        hb_ref[rows, :] = pooled.astype(bf16)
        at_ref[rows, :] = where
        return carry

    lax.fori_loop(0, PLANE, one, 0)


def highway_body(layer, d_ref, *refs):
    blocks = refs[:PLANE]
    w_ref, ba_ref, bb_ref, h_ref, open_ref, ra_ref, hn_ref, hb_ref = refs[PLANE:]
    d = d_ref[0]
    a = ba_ref[layer : layer + 1, :]
    b = bb_ref[layer : layer + 1, :]
    for k in range(PLANE):
        a = a + nn(blocks[k][...], w_ref[d ^ k, 0])
        b = b + nn(blocks[k][...], w_ref[d ^ k, 1])
    opened = jax.nn.sigmoid(b)
    ra = jnp.maximum(a, 0.0)
    mixed = opened * h_ref[...] + (1.0 - opened) * ra
    open_ref[...] = opened
    ra_ref[...] = ra
    hn_ref[...] = mixed
    hb_ref[...] = mixed.astype(bf16)


def highway(layer, dvec, blocks, weights, bias_a, bias_b, hidden):
    words, filters = hidden.shape
    part = words // 4
    row = pl.BlockSpec((part, filters), lambda i: (i, 0))
    return pl.pallas_call(
        functools.partial(highway_body, layer),
        grid=(4,),
        out_shape=[jax.ShapeDtypeStruct((words, filters), t) for t in (f32, f32, f32, bf16)],
        in_specs=[SMEM_SPEC]
        + [row] * PLANE
        + [
            pl.BlockSpec(weights.shape, lambda i: (0, 0, 0, 0)),
            pl.BlockSpec(bias_a.shape, lambda i: (0, 0)),
            pl.BlockSpec(bias_b.shape, lambda i: (0, 0)),
            row,
        ],
        out_specs=[row] * 4,
        name=f"highway{layer}",
        cost_estimate=cost(2 * words * filters * PLANE * 2 * filters, 12e6),
        compiler_params=pltpu.CompilerParams(vmem_limit_bytes=58 * 1024 * 1024),
    )(dvec, *blocks, weights, bias_a, bias_b, hidden)


def project_body(d_ref, h_ref, w_ref, keep_ref, send_ref):
    d = d_ref[0]
    words = keep_ref.shape[1]
    for i in range(PLANE // 2):
        for odd, out in ((0, keep_ref), (1, send_ref)):
            rows = pl.ds(pl.multiple_of((d ^ odd ^ (2 * i)) * words, words), words)
            out[i] = nn(h_ref[rows, :], w_ref[...]).astype(out.dtype)


def unproject_body(words, d_ref, *refs):
    blocks = refs[:PLANE]
    w_ref, h_ref, dh_ref, dw_ref, sum_ref = refs[PLANE:]
    d = d_ref[0]
    total, rest = None, None
    for k in range(PLANE):
        rows = pl.ds(pl.multiple_of((d ^ k) * words, words), words)
        grad = blocks[k][:words, :]
        dh_ref[rows, :] = nt(grad, w_ref[...])
        piece = tn(h_ref[rows, :], grad)
        total = piece if total is None else total + piece
        block = blocks[k][...].astype(f32)
        rest = block if rest is None else rest + block
    dw_ref[...] = total.astype(dw_ref.dtype)
    sum_ref[: words + 16, :] = rest
    sum_ref[words + 16 :, :] = jnp.broadcast_to(over_words(rest[:words]), (16, rest.shape[1]))


def highway_back_body(
    d_ref, dh_ref, open_ref, ra_ref, h_ref, w_ref, ga_ref, gb_ref, dc_ref, sum_ref, keep_ref, send_ref
):
    d = d_ref[0]
    dh = dh_ref[...]
    opened = open_ref[...]
    ra = ra_ref[...]
    closed = 1.0 - opened
    ga = jnp.where(ra > 0.0, dh * closed, 0.0).astype(bf16)
    gb = (dh * (h_ref[...] - ra) * (opened * closed)).astype(bf16)
    ga_ref[...] = ga
    gb_ref[...] = gb
    dc_ref[...] = dh * opened
    filters = ga.shape[1]

    @pl.when(pl.program_id(0) == 0)
    def first():
        sum_ref[...] = jnp.zeros_like(sum_ref)

    sum_ref[:, :filters] += jnp.sum(
        ga.astype(f32).reshape(-1, 8, filters), axis=0
    )
    sum_ref[:, filters:] += jnp.sum(
        gb.astype(f32).reshape(-1, 8, filters), axis=0
    )
    for i in range(PLANE // 2):
        for odd, out in ((1, send_ref), (0, keep_ref)):
            j = d ^ odd ^ (2 * i)
            out[i] = (nt(ga, w_ref[j, 0]) + nt(gb, w_ref[j, 1])).astype(out.dtype)


def highway_back(layer, dvec, d_hidden, opened, ra, hidden, weights):
    words, filters = hidden.shape
    part = words // 4
    row = pl.BlockSpec((part, filters), lambda i: (i, 0))
    half = PLANE // 2
    blocks = pl.BlockSpec((half, part, filters), lambda i: (0, i, 0))
    return pl.pallas_call(
        highway_back_body,
        grid=(4,),
        out_shape=[
            jax.ShapeDtypeStruct((words, filters), bf16),
            jax.ShapeDtypeStruct((words, filters), bf16),
            jax.ShapeDtypeStruct((words, filters), f32),
            jax.ShapeDtypeStruct((8, 2 * filters), f32),
            jax.ShapeDtypeStruct((half, words, filters), f32),
            jax.ShapeDtypeStruct((half, words, filters), bf16),
        ],
        in_specs=[SMEM_SPEC]
        + [row] * 4
        + [pl.BlockSpec(weights.shape, lambda i: (0, 0, 0, 0))],
        out_specs=[row, row, row, pl.BlockSpec((8, 2 * filters), lambda i: (0, 0)), blocks, blocks],
        name=f"highway_back{layer}",
        cost_estimate=cost(2 * words * filters * PLANE * 2 * filters, 20e6),
        compiler_params=pltpu.CompilerParams(vmem_limit_bytes=58 * 1024 * 1024),
    )(dvec, d_hidden, opened, ra, hidden, weights)


def highway_grad_body(d_ref, *refs):
    blocks = refs[:PLANE]
    ga_ref, gb_ref = refs[PLANE : PLANE + 2]
    outs = refs[PLANE + 2 :]
    d = d_ref[0]
    filters = ga_ref.shape[1]
    for k in range(PLANE):
        for side, grad_ref in enumerate((ga_ref, gb_ref)):
            cols = slice(side * filters, (side + 1) * filters)
            piece = tn(blocks[k][...], grad_ref[...]).astype(bf16)
            if len(outs) == 1:
                outs[0][:, d ^ k, :, cols] = piece.reshape(DEPTH, filters // DEPTH, filters)
            else:
                rows = filters // len(outs)
                for i, out_ref in enumerate(outs):
                    out_ref[d ^ k, :, cols] = piece[i * rows : (i + 1) * rows]


def spread_groups(char_len, filters, grad, at, spread_ref, group):
    count = min(GROUP, char_len - GROUP * group)
    for place in range(count):
        hit = at == GROUP * group + place
        spread_ref[:, place * filters : (place + 1) * filters] = jnp.where(hit, grad, 0.0).astype(
            bf16
        )
    return count


def char_back_body(char_len, words, d_ref, h_ref, at_ref, dh_ref, weight_ref, widths_ref, gp_ref, keep_ref, send_ref, taps_ref, spread_ref, chars_ref):
    d = d_ref[0]
    filters = h_ref.shape[1]
    lanes = taps_ref.shape[0] // 2
    held = keep_ref.shape[2]
    fill_taps(d, taps_ref, weight_ref, widths_ref)
    chars_ref[...] = jnp.zeros_like(chars_ref)

    def one(step, carry):
        rows = pl.ds(pl.multiple_of(step * 2 * words, 2 * words), 2 * words)
        grad = jnp.where(h_ref[rows, :] > 0.0, dh_ref[rows, :], 0.0).astype(bf16)
        gp_ref[rows, :] = grad
        grad = grad.astype(f32)
        at = at_ref[rows, :]
        for group in range(-(-char_len // GROUP)):
            count = spread_groups(char_len, filters, grad, at, spread_ref, group)
            piece = nt(spread_ref[:, : count * filters], taps_ref[:, : count * filters])
            chars_ref[rows, group * lanes : (group + 2) * lanes] += piece
        return carry

    lax.fori_loop(0, PLANE // 2, one, 0)
    for i in range(PLANE // 2):
        for odd, out in ((1, send_ref), (0, keep_ref)):
            rows = pl.ds(pl.multiple_of((d ^ odd ^ (2 * i)) * words, words), words)
            out[i] = chars_ref[rows, :held].astype(out.dtype)


def conv_grad_body(char_len, d_ref, x_ref, at_ref, gp_ref, dw_ref, spread_ref, xt_ref):
    filters = gp_ref.shape[1]
    lanes = 128
    depth = dw_ref.shape[0] - 8
    char_dim = lanes // GROUP
    grad = gp_ref[...].astype(f32)
    at = at_ref[...]
    groups = -(-char_len // GROUP)
    dw_ref[...] = jnp.zeros_like(dw_ref)
    for group in range(groups):
        count = spread_groups(char_len, filters, grad, at, spread_ref, group)
        piece = tn(x_ref[:, group * lanes : (group + 2) * lanes], spread_ref[:, : count * filters])
        for place in range(count):
            dw_ref[:depth, :] += piece[
                place * char_dim : place * char_dim + depth,
                place * filters : (place + 1) * filters,
            ]
    total = jnp.sum(grad.reshape(-1, 8, filters), axis=0)
    dw_ref[depth:, :] = jnp.broadcast_to(jnp.sum(total, axis=0, keepdims=True), (8, filters))


def table_grad_body(char_len, d_ref, ids_ref, chars_ref, out_ref):
    words = ids_ref.shape[1]
    lanes = 128
    width = lanes // GROUP
    rows = out_ref.shape[0] * GROUP
    groups = -(-char_len // GROUP)
    entry = lax.broadcasted_iota(jnp.int32, (rows, words), 0)
    lane = lax.broadcasted_iota(jnp.int32, (rows, lanes), 1) // width
    stacked = jnp.concatenate(
        [chars_ref[:, group * lanes : (group + 1) * lanes] for group in range(groups)], axis=0
    ).astype(bf16)
    total = jnp.zeros((rows, lanes), f32)
    for place in range(GROUP):
        pieces = []
        for group in range(groups):
            at = GROUP * group + place
            if at < char_len:
                pieces.append(jnp.where(ids_ref[at : at + 1, :] == entry, 1.0, 0.0).astype(bf16))
            else:
                pieces.append(jnp.zeros((rows, words), bf16))
        found = nn(jnp.concatenate(pieces, axis=1), stacked)
        total = total + jnp.where(lane == place, found, 0.0)
    step = width
    while step < lanes:
        total = total + pltpu.roll(total, step, 1)
        step *= 2
    part = out_ref.shape[0]
    fold = jnp.zeros(out_ref.shape, f32)
    lane = lax.broadcasted_iota(jnp.int32, out_ref.shape, 1) // width
    for place in range(GROUP):
        fold = fold + jnp.where(lane == place, total[place * part : (place + 1) * part], 0.0)
    out_ref[...] = fold


def pack_highway_body(carry_ref, gate_ref, *outs):
    for layer, out_ref in enumerate(outs):
        out_ref[0, 0] = carry_ref[layer]
        out_ref[0, 1] = gate_ref[layer]


def pack_highway(weights):
    layers, rows, columns = weights.shape
    own = columns // (2 * PLANE)
    block = (layers, rows, own)
    return pl.pallas_call(
        pack_highway_body,
        grid=(PLANE,),
        out_shape=[jax.ShapeDtypeStruct((PLANE, 2, rows, own), bf16)] * layers,
        in_specs=[
            pl.BlockSpec(block, lambda j: (0, 0, j)),
            pl.BlockSpec(block, lambda j: (0, 0, PLANE + j)),
        ],
        out_specs=[pl.BlockSpec((1, 2, rows, own), lambda j: (j, 0, 0, 0))] * layers,
        name="pack_highway",
    )(weights, weights)


def pack_encoder_body(qkv_ref, out_ref, inner_ref, outer_ref, packed_ref):
    dim = packed_ref.shape[1]
    at = 0
    for ref in (qkv_ref, out_ref, inner_ref, outer_ref):
        rows = ref.shape[0]
        for start in range(0, ref.shape[1], dim):
            packed_ref[at : at + rows, :] = ref[:, start : start + dim]
            at += rows


def finish_highway_body(count, *refs):
    out_ref = refs[-1]
    half = out_ref.shape[2] // 2
    own = half // PLANE
    low = 0
    for ref in refs[:count]:
        rows = out_ref.shape[1] // count
        for j in range(PLANE):
            for side in range(2):
                at = slice(j * own + side * half, (j + 1) * own + side * half)
                cols = slice(side * own, (side + 1) * own)
                piece = ref[j, :, cols] if len(ref.shape) == 3 else ref[:, j, :, cols]
                out_ref[0, low : low + rows, at] = piece.reshape(rows, own).astype(f32)
        low += rows


def finish_highway(layer, layers, pieces, previous):
    own = pieces[0].shape[-1] // 2
    width = 2 * PLANE * own
    operands = list(pieces)
    specs = [pl.BlockSpec(x.shape, lambda i, n=x.ndim: (0,) * n) for x in pieces]
    aliases = {}
    if previous is not None:
        aliases = {len(operands): 0}
        operands.append(previous)
        specs.append(pl.BlockSpec(memory_space=pl.ANY))
    return pl.pallas_call(
        functools.partial(finish_highway_body, len(pieces)),
        grid=(1,),
        out_shape=jax.ShapeDtypeStruct((layers, own, width), f32),
        in_specs=specs,
        out_specs=pl.BlockSpec((1, own, width), lambda i: (layer, 0, 0)),
        input_output_aliases=aliases,
        name=f"finish_highway{layer}",
        compiler_params=pltpu.CompilerParams(vmem_limit_bytes=58 * 1024 * 1024),
    )(*operands)


def finish_ends_body(d_ref, *refs):
    blocks = refs[:PLANE]
    widths_ref, conv_ref, bias_ref, gates_ref, table_ref, held_ref = refs[PLANE:]
    d = d_ref[0]
    own = blocks[0].shape[1]
    rows = conv_ref.shape[0]
    lanes = table_ref.shape[1]
    char_dim = lanes // GROUP
    tap = lax.broadcasted_iota(jnp.int32, (rows, own), 0) // char_dim
    for k in range(PLANE):
        cols = pl.ds(pl.multiple_of((d ^ k) * own, own), own)
        conv_ref[:, cols] = jnp.where(tap < widths_ref[:, cols], blocks[k][:rows, :], 0.0)
        bias_ref[:, cols] = blocks[k][rows : rows + 8, :]
        gates_ref[:, cols] = blocks[k][rows + 8 : rows + 16, :]
        held_ref[d ^ k] = blocks[k][rows + 16 :, :lanes]
    total = held_ref[0]
    for j in range(1, PLANE):
        total = total + held_ref[j]
    table_ref[...] = total


def finish_encoder_body(d_ref, low_ref, high_ref, *outs):
    dim = low_ref.shape[1]
    at = 0
    for ref in outs:
        count = ref.shape[0]
        for left in range(0, ref.shape[1], dim):
            low = low_ref.shape[0]
            source = low_ref[at : at + count] if at < low else high_ref[at - low : at - low + count]
            ref[:, left : left + dim] = source.astype(f32)
            at += count


def normalize(value):
    mean = jnp.mean(value, axis=-1, keepdims=True)
    centred = value - mean
    spread = jnp.mean(centred * centred, axis=-1, keepdims=True)
    scale = lax.rsqrt(spread + eps_norm)
    return centred * scale, scale


def normalize_back(grad, normal, scale, gain):
    moved = grad * gain
    return (
        moved
        - jnp.mean(moved, axis=-1, keepdims=True)
        - normal * jnp.mean(moved * normal, axis=-1, keepdims=True)
    ) * scale


def over_words(value):
    return jnp.sum(value, axis=0, keepdims=True)


def encoder_body(
    head_count,
    in_parts,
    flag_ref,
    emb_ref,
    e1_ref,
    e2_ref,
    e3_ref,
    small_ref,
    qseg_ref,
    kseg_ref,
    kpad_ref,
    cot_ref,
    w_hbm,
    result_ref,
    d_own_ref,
    send1_ref,
    send2_ref,
    send3_ref,
    embs_ref,
    gq_ref,
    gk_ref,
    gv_ref,
    att_ref,
    gattn_ref,
    first_ref,
    act_ref,
    gup_ref,
    gdown_ref,
    stats_ref,
    w_ref,
    q_ref,
    k_ref,
    v_ref,
    p_ref,
    up_ref,
    gatt_ref,
    sems,
):
    words, dim = emb_ref.shape
    part = dim // PLANE
    wide = act_ref.shape[1] // PLANE
    cuts = [0, 3 * part, 4 * part, (4 + in_parts) * part, (4 + in_parts) * part + wide]
    copies = [
        pltpu.make_async_copy(
            w_hbm.at[:, low:high, :], w_ref.at[:, low:high, :], sems.at[i]
        )
        for i, (low, high) in enumerate(zip(cuts, cuts[1:]))
    ]
    for copy in copies:
        copy.start()
    pair = 2 * HDIM
    scale = HDIM ** (-0.5)

    def square(i):
        return w_ref[:, i * part : (i + 1) * part, :].reshape(dim, dim)

    def small(i):
        return small_ref[i : i + 1, :]

    emb = emb_ref[...]
    emb_b = emb.astype(bf16)
    embs_ref[:words] = emb_b
    for i, ref in enumerate((e1_ref, e2_ref, e3_ref)):
        embs_ref[(i + 1) * words : (i + 2) * words] = ref[...]
    copies[0].wait()
    q_ref[...] = (nn(emb_b, square(0)) + small(1)).astype(bf16)
    k_ref[...] = nn(embs_ref[...], square(1)).astype(bf16)
    v_ref[...] = (nn(embs_ref[...], square(2)) + small(2)).astype(bf16)
    keys = k_ref.shape[0]
    row = lax.broadcasted_iota(jnp.int32, (words, keys), 0)
    column = lax.broadcasted_iota(jnp.int32, (words, keys), 1)
    allowed = (qseg_ref[...] == kseg_ref[...]) & ((kpad_ref[...] == 0) | (row == column))
    low_lane = lax.broadcasted_iota(jnp.int32, (1, pair), 1) < HDIM

    def of_head(value, side):
        keep = low_lane if side == 0 else jnp.logical_not(low_lane)
        return jnp.where(keep, value.astype(f32), 0.0).astype(bf16)

    for at in range(head_count // 2):
        cols = slice(at * pair, (at + 1) * pair)
        outs = []
        for side in range(2):
            scores = nt(of_head(q_ref[:, cols], side), k_ref[:, cols]) * scale
            scores = jnp.where(allowed, scores, masked_score)
            top = jnp.max(scores, axis=-1, keepdims=True)
            raised = jnp.exp(scores - top)
            probs = raised / jnp.sum(raised, axis=-1, keepdims=True)
            p_ref[2 * at + side] = probs
            outs.append(nn(probs.astype(bf16), v_ref[:, cols]))
        att_ref[:, cols] = jnp.where(low_lane, outs[0], outs[1]).astype(bf16)
    copies[1].wait()
    attn_out = nn(att_ref[...], square(3)) + small(3)
    normal1, scale1 = normalize(emb + attn_out)
    first = normal1 * small(6) + small(9)
    first_b = first.astype(bf16)
    first_ref[...] = first_b
    copies[2].wait()
    half_root = math.sqrt(0.5)
    for i in range(in_parts):
        cols = slice(i * dim, (i + 1) * dim)
        up = nn(first_b, square(4 + i)) + small(11 + i)
        up_ref[:, cols] = up
        act_ref[:, cols] = (0.5 * up * (1.0 + lax.erf(up * half_root))).astype(bf16)
    copies[3].wait()
    low = cuts[3]
    outer = w_ref[:, low : low + wide, :].reshape(PLANE * wide, dim)
    second = first + (nn(act_ref[...], outer) + small(4))
    normal2, scale2 = normalize(second)
    result_ref[...] = (normal2 * small(7) + small(10)).astype(bf16)

    grad = cot_ref[...].astype(f32)
    d_second = normalize_back(grad, normal2, scale2, small(7))
    stats_ref[...] = jnp.zeros_like(stats_ref)
    stats_ref[7:8] = over_words(grad * normal2)
    stats_ref[10:11] = over_words(grad)
    gdown = d_second.astype(bf16)
    gdown_ref[...] = gdown
    stats_ref[4:5] = over_words(gdown.astype(f32))
    d_first = d_second
    density = 1.0 / math.sqrt(2.0 * math.pi)
    per = dim // wide
    for i in range(in_parts):
        cols = slice(i * dim, (i + 1) * dim)
        block = w_ref[i * per : (i + 1) * per, low : low + wide, :].reshape(dim, dim)
        up = up_ref[:, cols]
        slope = 0.5 * (1.0 + lax.erf(up * half_root)) + up * (
            density * jnp.exp(-0.5 * up * up)
        )
        gup = (nt(gdown, block) * slope).astype(bf16)
        gup_ref[:, cols] = gup
        stats_ref[11 + i : 12 + i] = over_words(gup.astype(f32))
        d_first = d_first + nt(gup, square(4 + i))
    stats_ref[6:7] = over_words(d_first * normal1)
    stats_ref[9:10] = over_words(d_first)
    d_res = normalize_back(d_first, normal1, scale1, small(6))
    gattn = d_res.astype(bf16)
    gattn_ref[...] = gattn
    stats_ref[3:4] = over_words(gattn.astype(f32))
    gatt_ref[...] = nt(gattn, square(3)).astype(bf16)
    for at in range(head_count // 2):
        cols = slice(at * pair, (at + 1) * pair)
        dq, dk, dv = [], None, None
        for side in range(2):
            gatt = of_head(gatt_ref[:, cols], side)
            probs = p_ref[2 * at + side]
            d_probs = nt(gatt, v_ref[:, cols])
            inner = jnp.sum(probs * d_probs, axis=-1, keepdims=True)
            gscore = (probs * (d_probs - inner)).astype(bf16)
            dq.append(nn(gscore, k_ref[:, cols]))
            more_k = tn(gscore, of_head(q_ref[:, cols], side))
            more_v = tn(probs.astype(bf16), gatt)
            dk = more_k if dk is None else dk + more_k
            dv = more_v if dv is None else dv + more_v
        gq_ref[:, cols] = (jnp.where(low_lane, dq[0], dq[1]) * scale).astype(bf16)
        gk_ref[:, cols] = (dk * scale).astype(bf16)
        gv_ref[:, cols] = dv.astype(bf16)
    stats_ref[1:2] = over_words(gq_ref[...].astype(f32))
    stats_ref[2:3] = over_words(gv_ref[...].astype(f32))
    for i in range(DEPTH):
        rows = slice(i * words, (i + 1) * words)
        piece = nt(gk_ref[rows, :], square(1)) + nt(gv_ref[rows, :], square(2))
        if i == 0:
            d_own_ref[...] = d_res + nt(gq_ref[...], square(0)) + piece
        else:
            (send1_ref, send2_ref, send3_ref)[i - 1][...] = piece.astype(bf16)


def encoder_grad_body(
    flag_ref,
    embs_ref,
    gq_ref,
    gk_ref,
    gv_ref,
    att_ref,
    gattn_ref,
    first_ref,
    act_ref,
    gup_ref,
    gdown_ref,
    stats_ref,
    out_hbm,
    out_ref,
    sems,
):
    words, dim = gq_ref.shape
    part = dim // PLANE
    wide = act_ref.shape[1] // PLANE
    in_parts = gup_ref.shape[1] // dim
    pieces = []

    def put(low, high, value):
        out_ref[:, low:high, :] = value.reshape(PLANE, high - low, dim)

    def send(low, high):
        copy = pltpu.make_async_copy(
            out_ref.at[:, low:high, :], out_hbm.at[:, low:high, :], sems.at[len(pieces)]
        )
        copy.start()
        pieces.append(copy)

    low = (4 + in_parts) * part
    per = dim // wide
    for i in range(in_parts):
        cols = slice(i * dim, (i + 1) * dim)
        out_ref[i * per : (i + 1) * per, low : low + wide, :] = (
            tn(act_ref[:, cols], gdown_ref[...]).astype(bf16).reshape(per, wide, dim)
        )
    tail = jnp.broadcast_to(stats_ref[...].astype(bf16)[None], (PLANE,) + stats_ref.shape)
    out_ref[:, low + wide :, :] = tail
    send(low, out_ref.shape[1])
    for i in range(in_parts):
        cols = slice(i * dim, (i + 1) * dim)
        put((4 + i) * part, (5 + i) * part, tn(first_ref[...], gup_ref[:, cols]).astype(bf16))
    send(4 * part, low)
    put(3 * part, 4 * part, tn(att_ref[...], gattn_ref[...]).astype(bf16))
    put(0, part, tn(embs_ref[:words, :], gq_ref[...]).astype(bf16))
    put(part, 2 * part, tn(embs_ref[...], gk_ref[...]).astype(bf16))
    put(2 * part, 3 * part, tn(embs_ref[...], gv_ref[...]).astype(bf16))
    send(0, 4 * part)
    for copy in pieces:
        copy.wait()


def encoder(flag, embedded, others, small, query_segs, key_segs, key_pads, cotangent, weights):
    words, dim = embedded.shape
    keys = DEPTH * words
    head_count = dim // HDIM
    part = dim // PLANE
    in_parts = 4
    ff_dim = in_parts * dim
    vmem = pl.BlockSpec(memory_space=pltpu.VMEM)
    hbm = pl.BlockSpec(memory_space=pl.ANY)
    shapes = [
        ((words, dim), bf16),
        ((words, dim), f32),
        ((words, dim), bf16),
        ((words, dim), bf16),
        ((words, dim), bf16),
        ((keys, dim), bf16),
        ((words, dim), bf16),
        ((keys, dim), bf16),
        ((keys, dim), bf16),
        ((words, dim), bf16),
        ((words, dim), bf16),
        ((words, dim), bf16),
        ((words, ff_dim), bf16),
        ((words, ff_dim), bf16),
        ((words, dim), bf16),
        ((16, dim), f32),
    ]
    outs = pl.pallas_call(
        functools.partial(encoder_body, head_count, in_parts),
        out_shape=[jax.ShapeDtypeStruct(s, t) for s, t in shapes],
        in_specs=[SMEM_SPEC] + [vmem] * 9 + [hbm],
        out_specs=[vmem] * len(shapes),
        scratch_shapes=[
            VMEM(weights.shape, bf16),
            VMEM((words, dim), bf16),
            VMEM((keys, dim), bf16),
            VMEM((keys, dim), bf16),
            VMEM((head_count, words, keys), f32),
            VMEM((words, ff_dim), f32),
            VMEM((words, dim), bf16),
            pltpu.SemaphoreType.DMA((4,)),
        ],
        name="encoder",
        cost_estimate=cost(16e9, 30e6),
        compiler_params=pltpu.CompilerParams(vmem_limit_bytes=58 * 1024 * 1024),
    )(flag, embedded, *others, small, query_segs, key_segs, key_pads, cotangent, weights)
    result, d_own = outs[:2]
    d_embedded = d_own
    first = None
    for offset in range(1, DEPTH):
        piece = swap(outs[1 + offset], "seq", DEPTH, offset)
        first = piece if first is None else first
        d_embedded = d_embedded + piece.astype(f32)
    saved = [tie(outs[5], first), *outs[6:]]
    rows = (4 + in_parts) * part + ff_dim // PLANE + 16
    grads = pl.pallas_call(
        encoder_grad_body,
        out_shape=jax.ShapeDtypeStruct((PLANE, rows, dim), bf16),
        in_specs=[SMEM_SPEC] + [vmem] * 11,
        out_specs=hbm,
        scratch_shapes=[VMEM((PLANE, rows, dim), bf16), pltpu.SemaphoreType.DMA((3,))],
        name="encoder_grad",
        cost_estimate=cost(6e9, 20e6),
        compiler_params=pltpu.CompilerParams(vmem_limit_bytes=58 * 1024 * 1024),
    )(flag, *saved)
    return result, tie(d_embedded, grads), grads


def round_up(value, multiple):
    return -(-value // multiple) * multiple


def plane_shards(
    char_ids,
    segment_ids,
    pad_mask,
    cotangent,
    char_table,
    conv_weight,
    conv_bias,
    hw_weight,
    hw_bias,
    proj_weight,
    pos_table,
    qkv_weight,
    out_weight,
    ff_in_weight,
    ff_out_weight,
    ff_in_bias,
    d_biases,
    norm_gain,
    norm_shift,
):
    d = lax.axis_index("dp")
    z = lax.axis_index("seq")
    dvec = d.astype(jnp.int32)[None]
    words, char_len = char_ids.shape[1:]
    all_words = PLANE * words
    tap_count, char_dim, filters = conv_weight.shape
    chars = char_table.shape[0]
    own = filters // PLANE
    depth = hw_weight.shape[0]
    model_dim = cotangent.shape[2]
    seq_len = segment_ids.shape[1]
    head_count = model_dim // HDIM
    part = model_dim // PLANE
    ff_dim = ff_out_weight.shape[0] * PLANE
    lanes = GROUP * char_dim
    held = round_up(char_len * char_dim, lanes)
    score_scale = HDIM ** (-0.5)

    ids = char_ids.reshape(words, char_len)
    table_rows = round_up(chars, 128)
    table = jnp.pad(jnp.tile(char_table, (1, GROUP)), ((0, table_rows - chars), (0, 0)))
    (own_x,) = call(
        functools.partial(lookup_body, char_len),
        [((words + EXTRA_ROWS, held), bf16)],
        z.astype(jnp.int32)[None],
        (ids, table, hw_bias, d_biases, norm_gain, norm_shift, ff_in_bias[None, :], pos_table),
        [VMEM((EXTRA_ROWS, held), f32)],
        name="lookup",
    )
    hw_weight, qkv_weight, unused = lax.optimization_barrier((hw_weight, qkv_weight, own_x))
    hw_packed = pack_highway(hw_weight)

    x_blocks = plane_gather(own_x, hw_packed)
    hw_cols = [lax.all_to_all(tie(hw_packed[0], x_blocks[2]), "dp", 0, 0)]

    in_parts = ff_in_weight.shape[1] // model_dim
    weight_rows = (4 + in_parts) * part + ff_dim // PLANE
    packed = pl.pallas_call(
        pack_encoder_body,
        out_shape=jax.ShapeDtypeStruct((weight_rows, model_dim), bf16),
        name="pack_encoder",
    )(qkv_weight, out_weight, ff_in_weight, ff_out_weight)
    widths = filter_widths(filters)
    widths_row = jnp.asarray(widths[None, :], jnp.int32)
    taps = conv_weight.reshape(tap_count * char_dim, filters)
    taps_shape = VMEM((2 * lanes, GROUP * own), bf16)
    hidden0, hidden0_b, top_at, x_all, bias_a, bias_b, extras = call(
        functools.partial(conv_body, char_len, char_len - tap_count + 1, words),
        [
            ((all_words, own), f32),
            ((all_words, own), bf16),
            ((all_words, own), jnp.int32),
            ((all_words, held + lanes), bf16),
            ((16, own), f32),
            ((16, own), f32),
            ((PLANE, EXTRA_ROWS, held), bf16),
        ],
        dvec,
        (*x_blocks, taps, widths_row, conv_bias[None, :]),
        [taps_shape, VMEM((PLANE, 16, 2 * own), f32)],
        name="conv",
        flops=8e9,
    )

    hidden, hidden_b = hidden0, hidden0_b
    saved = []
    for layer in range(depth):
        blocks = plane_gather(hidden_b, (hw_cols[layer],))
        if layer + 1 < depth:
            following, packed = tie((hw_packed[layer + 1], packed), blocks)
            hw_cols.append(lax.all_to_all(following, "dp", 0, 0))
        if layer == 0:
            gathered = lax.all_gather(packed, "dp", axis=0, tiled=False)
        opened, ra, following, following_b = highway(
            layer, dvec, blocks, hw_cols[layer], bias_a, bias_b, hidden
        )
        saved.append((blocks, opened, ra, hidden))
        hidden, hidden_b = following, following_b
    vectors = extras[:, VECTOR_ROW : VECTOR_ROW + 11, :part].astype(f32)
    inner_bias = extras[:, VECTOR_ROW + 11, : ff_dim // PLANE].reshape(in_parts, model_dim)
    small_full = jnp.concatenate(
        [
            vectors.transpose(1, 0, 2).reshape(11, model_dim),
            inner_bias.astype(f32),
            jnp.zeros((16 - 11 - in_parts, model_dim), f32),
        ],
        axis=0,
    )
    per = EXTRA_ROWS - POS_ROW
    pos_full = (
        extras[:, POS_ROW:, : (words // per) * part]
        .reshape(PLANE, per, words // per, part)
        .transpose(2, 1, 0, 3)
        .reshape(words, model_dim)
    )

    half = PLANE // 2
    keep, send = call(
        project_body,
        [((half, words, model_dim), f32), ((half, words, model_dim), bf16)],
        dvec,
        (hidden_b, proj_weight),
        name="project",
    )
    projected = plane_reduce(keep, send) + small_full[0]

    summed = projected + pos_full.astype(f32)
    normal0, scale0 = normalize(summed)
    embedded = normal0 * small_full[5] + small_full[8]
    embedded_b = embedded.astype(bf16)
    others = [swap(embedded_b, "seq", DEPTH, offset) for offset in range(1, DEPTH)]

    def by_offset(row):
        pieces = row.reshape(DEPTH, words)
        return jnp.concatenate(
            [lax.dynamic_index_in_dim(pieces, z ^ offset, 0) for offset in range(DEPTH)], axis=1
        )

    key_segs, key_pads = by_offset(segment_ids), by_offset(pad_mask)
    result, d_embedded, enc_grads = encoder(
        dvec,
        embedded,
        others,
        small_full,
        key_segs[0, :words, None],
        key_segs,
        key_pads,
        cotangent.reshape(words, model_dim),
        gathered,
    )
    enc_slice = lax.psum_scatter(enc_grads, "dp", scatter_dimension=0, tiled=True)[0]
    d_summed = normalize_back(d_embedded, normal0, scale0, small_full[5])
    grad_proj = jnp.concatenate(
        [
            d_summed.astype(bf16),
            over_words(d_embedded * normal0).astype(bf16),
            over_words(d_embedded).astype(bf16),
            jnp.zeros((14, model_dim), bf16),
        ],
        axis=0,
    )

    gp_blocks = plane_gather(grad_proj)
    d_hidden, proj_grad, top_sums = call(
        functools.partial(unproject_body, words),
        [((all_words, own), f32), ((own, model_dim), bf16), ((words + 32, model_dim), f32)],
        dvec,
        (*gp_blocks, proj_weight, hidden_b),
        name="unproject",
    )
    top_own = lax.dynamic_slice_in_dim(top_sums, d * part, part, 1)
    top_own = jnp.pad(top_own, ((0, 0), (0, 128 - part)))
    top_all = lax.dynamic_update_slice_in_dim(
        jnp.zeros((seq_len + 32, 128), f32), top_own[words:], seq_len, 0
    )
    top_all = lax.dynamic_update_slice_in_dim(top_all, top_own[:words], z * words, 0).astype(bf16)
    cut = (4 + in_parts) * part
    gate_parts = {}
    middle = (z == 1) | (z == 2)
    chain = None
    for layer in reversed(range(depth)):
        blocks, opened, ra, hidden = saved[layer]
        ga, gb, d_carry, sums, keep, send = highway_back(
            layer, dvec, d_hidden, opened, ra, hidden, hw_cols[layer]
        )
        parts = plane_parts(keep, send)
        gate_parts[layer] = jnp.sum(sums, axis=0).reshape(2, own)
        after = []
        if layer == 0:
            enc_slice = tie(enc_slice, parts[1])
            chain[1] = chain[1] + tie(steps[1], parts[1])
            steps[1] = line_step(chain[1], 1)
            after = [chain[1]]
        shapes = (
            [((DEPTH, PLANE, own // DEPTH, 2 * own), bf16)]
            if layer == 0
            else [((PLANE, own // 2, 2 * own), bf16)] * 2
        )
        grads = call(
            highway_grad_body,
            shapes,
            dvec,
            (*blocks, tie(ga, parts[1], *after), gb),
            name=f"highway_grad{layer}",
            flops=2 * all_words * filters * 2 * own,
        )
        top_all = tie(top_all, parts[1])
        top_all = top_all + swap(top_all, "seq", DEPTH, 1 if layer else 2)
        if layer == 0:
            quarter = lax.psum_scatter(
                tie(grads[0], enc_slice), "seq", scatter_dimension=0, tiled=False
            )
            quarter = lax.all_to_all(quarter, "dp", 0, 0)
            lowest = lax.all_gather(quarter, "seq", axis=0, tiled=False)
            chain[0] = chain[0] + tie(steps[0], grads[0])
            steps[0] = line_step(chain[0], 2)
            after = [grads[0], top_all, enc_slice, chain[0]]
        else:
            chain = list(grads)
            steps = [line_step(value, 0) for value in chain]
            chain[0] = chain[0] + tie(steps[0], parts[1])
            steps[0] = line_step(chain[0], 1)
            after = [*grads, top_all, chain[0]]
        d_hidden = d_carry + plane_total(parts, after)
    lines = [enc_slice[:cut], jnp.concatenate([enc_slice[cut:], proj_grad], axis=0)]
    moved = [line_step(value, 0) for value in lines]
    d_hidden = tie(d_hidden, *lines)

    grad_pooled, keep, send = call(
        functools.partial(char_back_body, char_len, words),
        [
            ((all_words, own), bf16),
            ((half, words, held), f32),
            ((half, words, held), bf16),
        ],
        dvec,
        (hidden0, top_at, d_hidden, taps, widths_row),
        [
            taps_shape,
            VMEM((2 * words, GROUP * own), bf16),
            VMEM((all_words, held + lanes), f32),
        ],
        name="char_back",
        flops=8e9,
    )
    parts = plane_parts(keep, send)
    chain[1] = chain[1] + tie(steps[1], parts[1])
    steps[1] = line_step(chain[1], 2)
    grad_pooled = tie(grad_pooled, parts[1], chain[1])
    (conv_part,) = call(
        functools.partial(conv_grad_body, char_len),
        [((tap_count * char_dim + 8, own), f32)],
        dvec,
        (x_all, top_at, grad_pooled),
        [VMEM((all_words, GROUP * own), bf16), VMEM((2 * lanes, all_words), bf16)],
        name="conv_grad",
        flops=8e9,
    )
    lines = [value + tie(piece, conv_part) for value, piece in zip(lines, moved)]
    moved = [line_step(value, 1) for value in lines]
    char_grads = plane_total(parts, (conv_part, *lines))
    fold_rows = round_up(-(-chars // GROUP), 8)
    (table_part,) = call(
        functools.partial(table_grad_body, char_len),
        [((fold_rows, lanes), f32)],
        dvec,
        (ids.T, char_grads),
        name="table_grad",
        flops=2e9,
    )
    gate_rows = jnp.concatenate([gate_parts[layer] for layer in range(depth)], axis=0)
    ends = jnp.concatenate(
        [
            conv_part,
            jnp.pad(gate_rows, ((0, 8 - 2 * depth), (0, 0))),
            jnp.pad(table_part, ((0, 0), (0, own - lanes))),
        ],
        axis=0,
    )
    ends = ends + swap(ends, "seq", DEPTH, 1)
    ends = ends + swap(ends, "seq", DEPTH, 2)
    end_blocks = plane_gather(ends)
    conv_rows = tap_count * char_dim
    conv_total, conv_bias_total, gate_sums, table_total = call(
        finish_ends_body,
        [
            ((conv_rows, filters), f32),
            ((8, filters), f32),
            ((8, filters), f32),
            ((fold_rows, lanes), f32),
        ],
        dvec,
        (*end_blocks, widths_row),
        [VMEM((PLANE, fold_rows, lanes), f32)],
        name="finish_ends",
    )
    conv_total = conv_total.reshape(tap_count, char_dim, filters)
    conv_bias_total = conv_bias_total[0]
    table_total = (
        table_total.reshape(fold_rows, GROUP, char_dim)
        .transpose(1, 0, 2)
        .reshape(GROUP * fold_rows, char_dim)[:chars]
    )

    lines = [value + tie(piece, ends) for value, piece in zip(lines, moved)]
    moved = [line_step(value, 2) for value in lines]
    enc_total = [jnp.where(middle, value, piece) for value, piece in zip(lines, moved)]
    proj_total = enc_total[1][-own:]
    top_total = top_all[:, :part].astype(f32)
    pos_total = top_total[:seq_len]
    gain0, shift0, bias0 = top_total[seq_len], top_total[seq_len + 1], top_total[seq_len + 16]
    proj_total = proj_total.astype(f32)
    qkv_total, out_total, inner_total, outer_total, small_total = call(
        finish_encoder_body,
        [
            ((part, 3 * model_dim), f32),
            ((part, model_dim), f32),
            ((part, ff_dim), f32),
            ((ff_dim // PLANE, model_dim), f32),
            ((16, model_dim), f32),
        ],
        dvec,
        enc_total,
        name="finish_encoder",
    )
    own_small = lax.dynamic_slice_in_dim(small_total, d * part, part, 1)
    bias_total = jnp.concatenate([bias0[None], own_small[1:5]], axis=0)
    gain_total = jnp.concatenate([gain0[None], own_small[6:8]], axis=0)
    shift_total = jnp.concatenate([shift0[None], own_small[9:11]], axis=0)
    inner_bias_total = lax.dynamic_slice_in_dim(
        small_total[11 : 11 + in_parts].reshape(-1), d * (ff_dim // PLANE), ff_dim // PLANE, 0
    )

    chain = [
        jnp.where(middle, value, tie(piece, table_part)) for value, piece in zip(chain, steps)
    ]
    pieces = [lax.all_to_all(value, "dp", 0, 0) for value in chain]
    hw_total = finish_highway(1, depth, pieces, None)
    hw_total = finish_highway(0, depth, [lowest], hw_total)
    hw_bias_totals = []
    for layer in range(depth):
        row = gate_sums[2 * layer : 2 * layer + 2].reshape(-1)
        hw_bias_totals.append(lax.dynamic_slice_in_dim(row, d * 2 * own, 2 * own, 0))

    output = result.reshape(1, words, model_dim)
    return (
        output,
        table_total,
        conv_total,
        conv_bias_total,
        hw_total,
        jnp.stack(hw_bias_totals),
        proj_total,
        pos_total,
        qkv_total,
        out_total,
        inner_total,
        outer_total,
        inner_bias_total,
        bias_total,
        gain_total,
        shift_total,
    )


def solution(mesh):
    placed = (
        P("dp", "seq", None),
        P("dp", None),
        P("dp", None),
        P("dp", "seq", None),
        P(),
        P(),
        P(),
        P(None, "dp", None),
        P(None, "dp"),
        P("dp", None),
        P(None, "dp"),
        P("dp", None),
        P("dp", None),
        P("dp", None),
        P("dp", None),
        P("dp"),
        P(None, "dp"),
        P(None, "dp"),
        P(None, "dp"),
    )
    plane, depth = mesh.shape["dp"], mesh.shape["seq"]
    step = plane_shards if (plane, depth) == (PLANE, DEPTH) else shards
    return jax.shard_map(
        step,
        mesh=mesh,
        in_specs=placed,
        out_specs=(
            P("dp", "seq", None),
            P(),
            P(),
            P(),
            P(None, "dp", None),
            P(None, "dp"),
            P("dp", None),
            P(None, "dp"),
            P("dp", None),
            P("dp", None),
            P("dp", None),
            P("dp", None),
            P("dp"),
            P(None, "dp"),
            P(None, "dp"),
            P(None, "dp"),
        ),
        check_vma=False,
    )
```

```python
import functools
import math

import jax
import jax.numpy as jnp
import numpy as np
from jax import lax
from jax.experimental import pallas as pl
from jax.experimental.pallas import tpu as pltpu
from jax.sharding import PartitionSpec as P

HDIM = 64


eps_norm = 1e-12
masked_score = -1e30
width_shares = (1, 1, 2, 4, 8, 16, 32)


def filter_widths(filters):
    per_share = filters // 64
    return np.repeat(
        np.arange(1, len(width_shares) + 1),
        [per_share * share_count for share_count in width_shares],
    )


def layer_norm(inputs, gain_row, shift_row):
    centred = inputs - jnp.mean(inputs, axis=-1, keepdims=True)
    spread = jnp.mean(centred * centred, axis=-1, keepdims=True)
    return centred * lax.rsqrt(spread + eps_norm) * gain_row + shift_row


def highway_mix(gate_values, carried):
    filters = carried.shape[-1]
    opened = jax.nn.sigmoid(gate_values[:, filters:])
    return opened * carried + (1.0 - opened) * jax.nn.relu(gate_values[:, :filters])


def gelu_exact(inputs):
    return jax.nn.gelu(inputs, approximate=False)


def product(left_side, right_side):
    return jnp.dot(left_side, right_side, preferred_element_type=jnp.float32)


def product_tn(left_side, right_side):
    return lax.dot_general(
        left_side, right_side, (((0,), (0,)), ((), ())), preferred_element_type=jnp.float32
    )


def product_nt(left_side, right_side):
    return lax.dot_general(
        left_side, right_side, (((1,), (1,)), ((), ())), preferred_element_type=jnp.float32
    )


def char_windows(word_ids, char_rows, tap_count):
    word_count, char_len = word_ids.shape
    char_count = char_rows.shape[0]
    onehot = (
        word_ids.reshape(-1)[:, None] == jnp.arange(char_count, dtype=jnp.int32)[None, :]
    ).astype(jnp.bfloat16)
    vectors = product(onehot, char_rows).astype(jnp.bfloat16).reshape(word_count, char_len, -1)
    padded = jnp.pad(vectors, ((0, 0), (0, tap_count - 1), (0, 0)))
    char_taps = jnp.stack(
        [padded[:, tap_index : tap_index + char_len, :] for tap_index in range(tap_count)], axis=2
    )
    return (onehot, char_taps.reshape(word_count * char_len, -1))


def shards(
    char_ids,
    segment_ids,
    pad_mask,
    cotangent,
    char_table,
    conv_weight,
    conv_bias,
    hw_weight,
    hw_bias,
    proj_weight,
    pos_table,
    qkv_weight,
    out_weight,
    ff_in_weight,
    ff_out_weight,
    ff_in_bias,
    d_biases,
    norm_gain,
    norm_shift,
):
    (
        highway_full,
        highway_bias,
        proj_full,
        pos_full,
        qkv_full,
        out_full,
        inner_full,
        outer_full,
        inner_bias,
        bias_full,
        gain_full,
        shift_full,
    ) = (
        lax.all_gather(hw_weight, "dp", axis=1, tiled=True),
        lax.all_gather(hw_bias, "dp", axis=1, tiled=True),
        lax.all_gather(proj_weight, "dp", axis=0, tiled=True),
        lax.all_gather(pos_table, "dp", axis=1, tiled=True),
        lax.all_gather(qkv_weight, "dp", axis=0, tiled=True),
        lax.all_gather(out_weight, "dp", axis=0, tiled=True),
        lax.all_gather(ff_in_weight, "dp", axis=0, tiled=True),
        lax.all_gather(ff_out_weight, "dp", axis=0, tiled=True),
        lax.all_gather(ff_in_bias, "dp", axis=0, tiled=True),
        lax.all_gather(d_biases, "dp", axis=1, tiled=True),
        lax.all_gather(norm_gain, "dp", axis=1, tiled=True),
        lax.all_gather(norm_shift, "dp", axis=1, tiled=True),
    )
    seqs_here, local_len, char_len = char_ids.shape
    tap_count, char_dim, filters = conv_weight.shape
    model_dim = cotangent.shape[2]
    seq_len = segment_ids.shape[1]
    head_count = model_dim // HDIM
    highway_depth = highway_full.shape[0]
    word_count = seqs_here * local_len
    score_scale = HDIM ** (-0.5)
    bias_rows = bias_full.astype(jnp.float32)
    gain_rows = gain_full.astype(jnp.float32)
    shift_rows = shift_full.astype(jnp.float32)
    widths = filter_widths(filters)
    tap_mask = np.arange(tap_count)[:, None] < widths[None, :]
    masked_kernel = (conv_weight * jnp.asarray(tap_mask, jnp.bfloat16)[:, None, :]).reshape(
        tap_count * char_dim, filters
    )
    valid_place = jnp.asarray(np.arange(char_len)[:, None] <= char_len - widths[None, :])
    word_block = math.gcd(word_count, 32)
    block_count = word_count // word_block
    id_blocks = char_ids.reshape(block_count, word_block, char_len)

    def embed_forward(block_ids):
        unused, char_taps = char_windows(block_ids, char_table, tap_count)
        conv_out = (product(char_taps, masked_kernel) + conv_bias.astype(jnp.float32)).reshape(
            word_block, char_len, filters
        )
        conv_out = jnp.where(valid_place[None], conv_out, masked_score)
        return (jnp.max(conv_out, axis=1), jnp.argmax(conv_out, axis=1))

    pooled, top_place = lax.map(embed_forward, id_blocks)
    pooled = pooled.reshape(word_count, filters)
    hidden = jax.nn.relu(pooled)
    carried_list = []
    gates_list = []
    for highway_layer in range(highway_depth):
        carried_list.append(hidden)
        gate_values = product(
            hidden.astype(jnp.bfloat16), highway_full[highway_layer]
        ) + highway_bias[highway_layer].astype(jnp.float32)
        gates_list.append(gate_values)
        hidden = highway_mix(gate_values, hidden)
    top_hidden = hidden.astype(jnp.bfloat16)
    projected = product(top_hidden, proj_full) + bias_rows[0]
    row_start = lax.axis_index("seq") * local_len
    pos_rows = lax.dynamic_slice_in_dim(pos_full, row_start, local_len, 0).astype(jnp.float32)
    summed = (projected.reshape(seqs_here, local_len, model_dim) + pos_rows[None]).reshape(
        word_count, model_dim
    )
    embedded = layer_norm(summed, gain_rows[0], shift_rows[0])
    embedded_b = embedded.astype(jnp.bfloat16)
    qkv_shift = jnp.concatenate([bias_rows[1], jnp.zeros_like(bias_rows[1]), bias_rows[2]])
    qkv = (product(embedded_b, qkv_full) + qkv_shift).astype(jnp.bfloat16)
    queries = qkv[:, :model_dim].reshape(seqs_here, local_len, head_count, HDIM)
    keys_local = qkv[:, model_dim : 2 * model_dim].reshape(seqs_here, local_len, model_dim)
    values_local = qkv[:, 2 * model_dim :].reshape(seqs_here, local_len, model_dim)
    keys_full, values_full = (
        lax.all_gather(keys_local, "seq", axis=1, tiled=True),
        lax.all_gather(values_local, "seq", axis=1, tiled=True),
    )
    query_segs = lax.dynamic_slice_in_dim(segment_ids, row_start, local_len, 1)
    query_pos = row_start + jnp.arange(local_len, dtype=jnp.int32)
    same_segment = query_segs[:, :, None] == segment_ids[:, None, :]
    open_key = (pad_mask[:, None, :] == 0) | (
        query_pos[:, None] == jnp.arange(seq_len, dtype=jnp.int32)[None, :]
    )[None]
    allowed = (same_segment & open_key)[:, None]

    def score_of(key_rows):
        raw_scores = (
            jnp.einsum(
                "sqhd,skhd->shqk",
                queries,
                key_rows.reshape(seqs_here, seq_len, head_count, HDIM),
                preferred_element_type=jnp.float32,
            )
            * score_scale
        )
        return jnp.where(allowed, raw_scores, masked_score)

    scores = score_of(keys_full)
    row_top = jnp.max(scores, axis=-1, keepdims=True)
    exp_scores = jnp.exp(scores - row_top)
    denominator = jnp.sum(exp_scores, axis=-1, keepdims=True)
    attn_probs = (exp_scores / denominator).astype(jnp.bfloat16)
    log_total = row_top + jnp.log(denominator)
    attended = (
        jnp.einsum(
            "shqk,skhd->sqhd",
            attn_probs,
            values_full.reshape(seqs_here, seq_len, head_count, HDIM),
            preferred_element_type=jnp.float32,
        )
        .reshape(word_count, model_dim)
        .astype(jnp.bfloat16)
    )
    attn_out = product(attended, out_full) + bias_rows[3]
    first_input = embedded + attn_out
    first_norm = layer_norm(first_input, gain_rows[1], shift_rows[1])
    first_b = first_norm.astype(jnp.bfloat16)
    ffn_up = product(first_b, inner_full) + inner_bias.astype(jnp.float32)
    ffn_act = gelu_exact(ffn_up).astype(jnp.bfloat16)
    ffn_down = product(ffn_act, outer_full) + bias_rows[4]
    second = first_norm + ffn_down
    result = layer_norm(second, gain_rows[2], shift_rows[2])
    grad_out = cotangent.reshape(word_count, model_dim).astype(jnp.float32)
    unused, norm_back = jax.vjp(layer_norm, second, gain_rows[2], shift_rows[2])
    d_second, gain_grad2, shift_grad2 = norm_back(grad_out)
    grad_down = d_second.astype(jnp.bfloat16)
    outer_grad = product_tn(ffn_act, grad_down)
    bias_grad4 = jnp.sum(grad_down.astype(jnp.float32), axis=0)
    unused, gelu_back = jax.vjp(gelu_exact, ffn_up)
    grad_up = gelu_back(product_nt(grad_down, outer_full))[0].astype(jnp.bfloat16)
    inner_grad = product_tn(first_b, grad_up)
    inner_bias_grad = jnp.sum(grad_up.astype(jnp.float32), axis=0)
    d_first = d_second + product_nt(grad_up, inner_full)
    unused, norm_back = jax.vjp(layer_norm, first_input, gain_rows[1], shift_rows[1])
    d_res, gain_grad1, shift_grad1 = norm_back(d_first)
    grad_attn = d_res.astype(jnp.bfloat16)
    out_grad = product_tn(attended, grad_attn)
    bias_grad3 = jnp.sum(grad_attn.astype(jnp.float32), axis=0)
    grad_attended = (
        product_nt(grad_attn, out_full)
        .astype(jnp.bfloat16)
        .reshape(seqs_here, local_len, head_count, HDIM)
    )
    keys_back, values_back = (keys_full, values_full)
    probs_again = jnp.exp(score_of(keys_back) - log_total)
    probs_again_b = probs_again.astype(jnp.bfloat16)
    key_heads = keys_back.reshape(seqs_here, seq_len, head_count, HDIM)
    value_heads = values_back.reshape(seqs_here, seq_len, head_count, HDIM)
    d_probs = jnp.einsum(
        "sqhd,skhd->shqk", grad_attended, value_heads, preferred_element_type=jnp.float32
    )
    grad_scores = (
        probs_again * (d_probs - jnp.sum(probs_again * d_probs, axis=-1, keepdims=True))
    ).astype(jnp.bfloat16)
    d_queries = (
        jnp.einsum("shqk,skhd->sqhd", grad_scores, key_heads, preferred_element_type=jnp.float32)
        * score_scale
    )
    d_keys_all = (
        jnp.einsum("shqk,sqhd->skhd", grad_scores, queries, preferred_element_type=jnp.float32)
        * score_scale
    )
    d_values_all = jnp.einsum(
        "shqk,sqhd->skhd", probs_again_b, grad_attended, preferred_element_type=jnp.float32
    )
    d_keys, d_values = (
        lax.psum_scatter(
            d_keys_all.reshape(seqs_here, seq_len, model_dim).astype(jnp.bfloat16),
            "seq",
            scatter_dimension=1,
            tiled=True,
        ).astype(jnp.float32),
        lax.psum_scatter(
            d_values_all.reshape(seqs_here, seq_len, model_dim).astype(jnp.bfloat16),
            "seq",
            scatter_dimension=1,
            tiled=True,
        ).astype(jnp.float32),
    )
    grad_qkv = jnp.concatenate(
        [
            d_queries.reshape(word_count, model_dim),
            d_keys.reshape(word_count, model_dim),
            d_values.reshape(word_count, model_dim),
        ],
        axis=1,
    ).astype(jnp.bfloat16)
    qkv_grad = product_tn(embedded_b, grad_qkv)
    bias_grad1 = jnp.sum(grad_qkv[:, :model_dim].astype(jnp.float32), axis=0)
    bias_grad2 = jnp.sum(grad_qkv[:, 2 * model_dim :].astype(jnp.float32), axis=0)
    d_embedded = d_res + product_nt(grad_qkv, qkv_full)
    unused, norm_back = jax.vjp(layer_norm, summed, gain_rows[0], shift_rows[0])
    d_summed, gain_grad0, shift_grad0 = norm_back(d_embedded)
    pos_local = jnp.sum(d_summed.reshape(seqs_here, local_len, model_dim), axis=0)
    pos_grad = lax.dynamic_update_slice_in_dim(
        jnp.zeros((seq_len, model_dim), jnp.float32), pos_local, row_start, 0
    )
    grad_proj = d_summed.astype(jnp.bfloat16)
    proj_grad = product_tn(top_hidden, grad_proj)
    bias_grad0 = jnp.sum(grad_proj.astype(jnp.float32), axis=0)
    d_hidden = product_nt(grad_proj, proj_full)
    kernel_grads = [None] * highway_depth
    shift_grads = [None] * highway_depth
    for highway_layer in reversed(range(highway_depth)):
        carried = carried_list[highway_layer]
        unused, mix_back = jax.vjp(highway_mix, gates_list[highway_layer], carried)
        d_gates, d_carried = mix_back(d_hidden)
        grad_gates = d_gates.astype(jnp.bfloat16)
        kernel_grads[highway_layer] = product_tn(carried.astype(jnp.bfloat16), grad_gates)
        shift_grads[highway_layer] = jnp.sum(grad_gates.astype(jnp.float32), axis=0)
        d_hidden = d_carried + product_nt(grad_gates, highway_full[highway_layer])
    grad_pooled = jnp.where(pooled > 0, d_hidden, 0.0).astype(jnp.bfloat16)

    def embed_backward(running, inputs):
        weight_sum, bias_sum, table_sum = running
        block_ids, place_block, grad_block = inputs
        onehot, char_taps = char_windows(block_ids, char_table, tap_count)
        grad_conv = jnp.where(
            jnp.arange(char_len, dtype=jnp.int32)[None, :, None] == place_block[:, None, :],
            grad_block[:, None, :],
            jnp.zeros((), jnp.bfloat16),
        ).reshape(word_block * char_len, filters)
        weight_sum = weight_sum + product_tn(char_taps, grad_conv)
        bias_sum = bias_sum + jnp.sum(grad_block.astype(jnp.float32), axis=0)
        d_taps = product_nt(grad_conv, masked_kernel).reshape(
            word_block, char_len, tap_count, char_dim
        )
        spread = jnp.zeros((word_block, char_len + tap_count - 1, char_dim), jnp.float32)
        for tap_index in range(tap_count):
            spread = spread.at[:, tap_index : tap_index + char_len].add(d_taps[:, :, tap_index])
        grad_chars = (
            spread[:, :char_len].reshape(word_block * char_len, char_dim).astype(jnp.bfloat16)
        )
        table_sum = table_sum + product_tn(onehot, grad_chars)
        return ((weight_sum, bias_sum, table_sum), None)

    start_sums = (
        jnp.zeros((tap_count * char_dim, filters), jnp.float32),
        jnp.zeros((filters,), jnp.float32),
        jnp.zeros(char_table.shape, jnp.float32),
    )
    conv_sums, unused = lax.scan(
        embed_backward,
        start_sums,
        (id_blocks, top_place, grad_pooled.reshape(block_count, word_block, filters)),
    )
    conv_weight_grad = (
        conv_sums[0] * jnp.asarray(np.repeat(tap_mask, char_dim, axis=0), jnp.float32)
    ).reshape(tap_count, char_dim, filters)
    table_total, conv_total, conv_bias_total = lax.psum(
        (conv_sums[2], conv_weight_grad, conv_sums[1]), ("dp", "seq")
    )
    weight_grads = (
        jnp.stack(kernel_grads),
        jnp.stack(shift_grads),
        proj_grad,
        pos_grad,
        qkv_grad,
        out_grad,
        inner_grad,
        outer_grad,
        inner_bias_grad,
        jnp.stack([bias_grad0, bias_grad1, bias_grad2, bias_grad3, bias_grad4]),
        jnp.stack([gain_grad0, gain_grad1, gain_grad2]),
        jnp.stack([shift_grad0, shift_grad1, shift_grad2]),
    )
    sliced = (
        lax.psum_scatter(weight_grads[0], "dp", scatter_dimension=1, tiled=True),
        lax.psum_scatter(weight_grads[1], "dp", scatter_dimension=1, tiled=True),
        lax.psum_scatter(weight_grads[2], "dp", scatter_dimension=0, tiled=True),
        lax.psum_scatter(weight_grads[3], "dp", scatter_dimension=1, tiled=True),
        lax.psum_scatter(weight_grads[4], "dp", scatter_dimension=0, tiled=True),
        lax.psum_scatter(weight_grads[5], "dp", scatter_dimension=0, tiled=True),
        lax.psum_scatter(weight_grads[6], "dp", scatter_dimension=0, tiled=True),
        lax.psum_scatter(weight_grads[7], "dp", scatter_dimension=0, tiled=True),
        lax.psum_scatter(weight_grads[8], "dp", scatter_dimension=0, tiled=True),
        lax.psum_scatter(weight_grads[9], "dp", scatter_dimension=1, tiled=True),
        lax.psum_scatter(weight_grads[10], "dp", scatter_dimension=1, tiled=True),
        lax.psum_scatter(weight_grads[11], "dp", scatter_dimension=1, tiled=True),
    )
    summed_grads = (
        lax.psum(sliced[0].astype(jnp.bfloat16), "seq").astype(jnp.float32),
        lax.psum(sliced[1].astype(jnp.bfloat16), "seq").astype(jnp.float32),
        lax.psum(sliced[2].astype(jnp.bfloat16), "seq").astype(jnp.float32),
        lax.psum(sliced[3].astype(jnp.bfloat16), "seq").astype(jnp.float32),
        lax.psum(sliced[4].astype(jnp.bfloat16), "seq").astype(jnp.float32),
        lax.psum(sliced[5].astype(jnp.bfloat16), "seq").astype(jnp.float32),
        lax.psum(sliced[6].astype(jnp.bfloat16), "seq").astype(jnp.float32),
        lax.psum(sliced[7].astype(jnp.bfloat16), "seq").astype(jnp.float32),
        lax.psum(sliced[8].astype(jnp.bfloat16), "seq").astype(jnp.float32),
        lax.psum(sliced[9].astype(jnp.bfloat16), "seq").astype(jnp.float32),
        lax.psum(sliced[10].astype(jnp.bfloat16), "seq").astype(jnp.float32),
        lax.psum(sliced[11].astype(jnp.bfloat16), "seq").astype(jnp.float32),
    )
    output = result.astype(jnp.bfloat16).reshape(seqs_here, local_len, model_dim)
    return (output, table_total, conv_total, conv_bias_total) + tuple(summed_grads)


PLANE = 8
DEPTH = 4
CORE_PARTNER = 1
GROUP = 8

f32 = jnp.float32
bf16 = jnp.bfloat16


def swap(value, axis_name, size, offset):
    return lax.ppermute(value, axis_name, [(at, at ^ offset) for at in range(size)])


def plane_swap(value, offset):
    return swap(value, "dp", PLANE, offset)


def plane_gather(block, before=()):
    even = [block] + [plane_swap(block, offset) for offset in (2, 4, 6)]
    if before:
        even[1] = tie(even[1], *before)
    odd = [plane_swap(piece, CORE_PARTNER) for piece in even]
    return [piece for pair in zip(even, odd) for piece in pair]


def tie(value, *after):
    return lax.optimization_barrier((value, *after))[0]


def plane_parts(keep, send):
    arrived = plane_swap(send, CORE_PARTNER)
    own = keep[0].astype(f32) + arrived[0].astype(f32)
    return [own] + [
        (keep[i].astype(f32) + arrived[i].astype(f32)).astype(bf16) for i in range(1, PLANE // 2)
    ]


def plane_others(parts):
    return [plane_swap(part, 2 * i) for i, part in enumerate(parts[1:], 1)]


def plane_total(parts, after=(), others=None):
    total = tie(parts[0], *after)
    for piece in others or plane_others(parts):
        total = total + piece.astype(f32)
    return total


def plane_reduce(keep, send):
    return plane_total(plane_parts(keep, send))


LINE_STEPS = ([(0, 1), (3, 2)], [(1, 2), (2, 1)], [(1, 0), (2, 3)])


def line_step(value, step):
    return lax.ppermute(value, "seq", LINE_STEPS[step])


def nn(left_side, right_side):
    return jnp.dot(left_side, right_side, preferred_element_type=f32)


def nt(left_side, right_side):
    return lax.dot_general(
        left_side, right_side, (((1,), (1,)), ((), ())), preferred_element_type=f32
    )


def tn(left_side, right_side):
    return lax.dot_general(
        left_side, right_side, (((0,), (0,)), ((), ())), preferred_element_type=f32
    )


VMEM = pltpu.VMEM
SMEM_SPEC = pl.BlockSpec(memory_space=pltpu.SMEM)


def whole(count):
    return [pl.BlockSpec(memory_space=pltpu.VMEM)] * count


def cost(flops, moved):
    return pl.CostEstimate(flops=int(flops), transcendentals=0, bytes_accessed=int(moved))


def call(body, out_shapes, scalar, operands, scratch=(), name=None, flops=0):
    return pl.pallas_call(
        body,
        out_shape=[jax.ShapeDtypeStruct(s, t) for s, t in out_shapes],
        in_specs=[SMEM_SPEC] + whole(len(operands)),
        out_specs=whole(len(out_shapes)),
        scratch_shapes=list(scratch),
        name=name,
        cost_estimate=cost(
            flops,
            sum(x.size * x.dtype.itemsize for x in operands)
            + sum(math.prod(s) * jnp.dtype(t).itemsize for s, t in out_shapes),
        ),
        compiler_params=pltpu.CompilerParams(vmem_limit_bytes=58 * 1024 * 1024),
    )(scalar, *operands)


EXTRA_ROWS = 32
VECTOR_ROW = 2
POS_ROW = 16


def lookup_body(
    char_len,
    z_ref,
    ids_ref,
    table_ref,
    gate_ref,
    biases_ref,
    gain_ref,
    shift_ref,
    inner_ref,
    pos_ref,
    x_ref,
    extra_ref,
):
    words = ids_ref.shape[0]
    rows, lanes = table_ref.shape
    width = lanes // GROUP
    groups = x_ref.shape[1] // lanes
    lane = lax.broadcasted_iota(jnp.int32, (rows, lanes), 1) // width
    entry = lax.broadcasted_iota(jnp.int32, (words, rows), 1)
    total = jnp.zeros((groups * words, lanes), f32)
    for place in range(GROUP):
        pieces = []
        for group in range(groups):
            at = GROUP * group + place
            if at < char_len:
                hit = ids_ref[:, at : at + 1] == entry
                pieces.append(jnp.where(hit, 1.0, 0.0).astype(bf16))
            else:
                pieces.append(jnp.zeros((words, rows), bf16))
        own = jnp.where(lane == place, table_ref[...].astype(f32), 0.0).astype(bf16)
        total = total + nn(jnp.concatenate(pieces, axis=0), own)
    for group in range(groups):
        x_ref[:words, group * lanes : (group + 1) * lanes] = total[
            group * words : (group + 1) * words
        ].astype(bf16)
    extra_ref[...] = jnp.zeros_like(extra_ref)
    at = 0
    for ref in (gate_ref, biases_ref, gain_ref, shift_ref, inner_ref):
        extra_ref[at : at + ref.shape[0], : ref.shape[1]] = ref[...].astype(f32)
        at += ref.shape[0]
    per = EXTRA_ROWS - POS_ROW
    part = pos_ref.shape[1]
    for i in range(words // per):
        rows = pl.ds(pl.multiple_of(z_ref[0] * words + i * per, per), per)
        extra_ref[POS_ROW:, i * part : (i + 1) * part] = pos_ref[rows, :].astype(f32)
    x_ref[words:, :] = extra_ref[...].astype(bf16)


def fill_taps(d, taps_ref, weight_ref, widths_ref):
    depth = weight_ref.shape[0]
    filters = weight_ref.shape[1] // PLANE
    char_dim = taps_ref.shape[0] // (2 * GROUP)
    cols = pl.ds(pl.multiple_of(d * filters, filters), filters)
    tap = lax.broadcasted_iota(jnp.int32, (depth, filters), 0) // char_dim
    own = jnp.where(tap < widths_ref[:, cols], weight_ref[:, cols].astype(f32), 0.0).astype(bf16)
    taps_ref[...] = jnp.zeros_like(taps_ref)
    for place in range(GROUP):
        taps_ref[
            place * char_dim : place * char_dim + depth, place * filters : (place + 1) * filters
        ] = own


def conv_body(char_len, first_masked, words, d_ref, *refs):
    blocks = refs[:PLANE]
    (weight_ref, widths_ref, bias_ref, h_ref, hb_ref, at_ref, x_ref, ba_ref, bb_ref, all_extra_ref) = refs[
        PLANE : PLANE + 10
    ]
    taps_ref, extra_ref = refs[PLANE + 10 :]
    d = d_ref[0]
    filters = h_ref.shape[1]
    held = blocks[0].shape[1]
    lanes = taps_ref.shape[0] // 2
    fill_taps(d, taps_ref, weight_ref, widths_ref)
    cols = pl.ds(pl.multiple_of(d * filters, filters), filters)
    bias = bias_ref[:, cols].astype(f32)
    for k in range(PLANE):
        rows = pl.ds(pl.multiple_of((d ^ k) * words, words), words)
        x_ref[rows, :held] = blocks[k][:words, :]
        x_ref[rows, held:] = jnp.zeros((words, x_ref.shape[1] - held), bf16)
        extra_ref[d ^ k] = blocks[k][words : words + 16, : 2 * filters].astype(f32)
        all_extra_ref[d ^ k] = blocks[k][words:, :]
    for half, out in ((0, ba_ref), (PLANE // 2, bb_ref)):
        source = extra_ref[half + d // 2]
        out[...] = jnp.where(d % 2 == 0, source[:, :filters], source[:, filters:])
    last = char_len - widths_ref[:, cols]

    def one(step, carry):
        rows = pl.ds(pl.multiple_of(step * words, words), words)
        best = None
        for group in range(-(-char_len // GROUP)):
            count = min(GROUP, char_len - GROUP * group)
            values = nn(
                x_ref[rows, group * lanes : (group + 2) * lanes], taps_ref[:, : count * filters]
            )
            for place in range(count):
                at = GROUP * group + place
                value = values[:, place * filters : (place + 1) * filters]
                if at >= first_masked:
                    value = jnp.where(at <= last, value, masked_score)
                if best is None:
                    best, where = value, jnp.zeros(value.shape, jnp.int32)
                else:
                    where = jnp.where(value > best, at, where)
                    best = jnp.maximum(value, best)
        pooled = jnp.maximum(best + bias, 0.0)
        h_ref[rows, :] = pooled
        hb_ref[rows, :] = pooled.astype(bf16)
        at_ref[rows, :] = where
        return carry

    lax.fori_loop(0, PLANE, one, 0)


def highway_body(layer, d_ref, *refs):
    blocks = refs[:PLANE]
    w_ref, ba_ref, bb_ref, h_ref, open_ref, ra_ref, hn_ref, hb_ref = refs[PLANE:]
    d = d_ref[0]
    a = ba_ref[layer : layer + 1, :]
    b = bb_ref[layer : layer + 1, :]
    for k in range(PLANE):
        a = a + nn(blocks[k][...], w_ref[d ^ k, 0])
        b = b + nn(blocks[k][...], w_ref[d ^ k, 1])
    opened = jax.nn.sigmoid(b)
    ra = jnp.maximum(a, 0.0)
    mixed = opened * h_ref[...] + (1.0 - opened) * ra
    open_ref[...] = opened
    ra_ref[...] = ra
    hn_ref[...] = mixed
    hb_ref[...] = mixed.astype(bf16)


def highway(layer, dvec, blocks, weights, bias_a, bias_b, hidden):
    words, filters = hidden.shape
    part = words // 4
    row = pl.BlockSpec((part, filters), lambda i: (i, 0))
    return pl.pallas_call(
        functools.partial(highway_body, layer),
        grid=(4,),
        out_shape=[jax.ShapeDtypeStruct((words, filters), t) for t in (f32, f32, f32, bf16)],
        in_specs=[SMEM_SPEC]
        + [row] * PLANE
        + [
            pl.BlockSpec(weights.shape, lambda i: (0, 0, 0, 0)),
            pl.BlockSpec(bias_a.shape, lambda i: (0, 0)),
            pl.BlockSpec(bias_b.shape, lambda i: (0, 0)),
            row,
        ],
        out_specs=[row] * 4,
        name=f"highway{layer}",
        cost_estimate=cost(2 * words * filters * PLANE * 2 * filters, 12e6),
        compiler_params=pltpu.CompilerParams(vmem_limit_bytes=58 * 1024 * 1024),
    )(dvec, *blocks, weights, bias_a, bias_b, hidden)


def project_body(d_ref, h_ref, w_ref, keep_ref, send_ref):
    d = d_ref[0]
    words = keep_ref.shape[1]
    for i in range(PLANE // 2):
        for odd, out in ((0, keep_ref), (1, send_ref)):
            rows = pl.ds(pl.multiple_of((d ^ odd ^ (2 * i)) * words, words), words)
            out[i] = nn(h_ref[rows, :], w_ref[...]).astype(out.dtype)


def unproject_body(words, d_ref, *refs):
    blocks = refs[:PLANE]
    w_ref, h_ref, dh_ref, dw_ref, sum_ref = refs[PLANE:]
    d = d_ref[0]
    total, rest = None, None
    for k in range(PLANE):
        rows = pl.ds(pl.multiple_of((d ^ k) * words, words), words)
        grad = blocks[k][:words, :]
        dh_ref[rows, :] = nt(grad, w_ref[...])
        piece = tn(h_ref[rows, :], grad)
        total = piece if total is None else total + piece
        block = blocks[k][...].astype(f32)
        rest = block if rest is None else rest + block
    dw_ref[...] = total.astype(dw_ref.dtype)
    sum_ref[: words + 16, :] = rest
    sum_ref[words + 16 :, :] = jnp.broadcast_to(over_words(rest[:words]), (16, rest.shape[1]))


def highway_back_body(
    d_ref, dh_ref, open_ref, ra_ref, h_ref, w_ref, ga_ref, gb_ref, dc_ref, sum_ref, keep_ref, send_ref
):
    d = d_ref[0]
    dh = dh_ref[...]
    opened = open_ref[...]
    ra = ra_ref[...]
    closed = 1.0 - opened
    ga = jnp.where(ra > 0.0, dh * closed, 0.0).astype(bf16)
    gb = (dh * (h_ref[...] - ra) * (opened * closed)).astype(bf16)
    ga_ref[...] = ga
    gb_ref[...] = gb
    dc_ref[...] = dh * opened
    filters = ga.shape[1]

    @pl.when(pl.program_id(0) == 0)
    def first():
        sum_ref[...] = jnp.zeros_like(sum_ref)

    sum_ref[:, :filters] += jnp.sum(
        ga.astype(f32).reshape(-1, 8, filters), axis=0
    )
    sum_ref[:, filters:] += jnp.sum(
        gb.astype(f32).reshape(-1, 8, filters), axis=0
    )
    for i in range(PLANE // 2):
        for odd, out in ((1, send_ref), (0, keep_ref)):
            j = d ^ odd ^ (2 * i)
            out[i] = (nt(ga, w_ref[j, 0]) + nt(gb, w_ref[j, 1])).astype(out.dtype)


def highway_back(layer, dvec, d_hidden, opened, ra, hidden, weights):
    words, filters = hidden.shape
    part = words // 4
    row = pl.BlockSpec((part, filters), lambda i: (i, 0))
    half = PLANE // 2
    blocks = pl.BlockSpec((half, part, filters), lambda i: (0, i, 0))
    return pl.pallas_call(
        highway_back_body,
        grid=(4,),
        out_shape=[
            jax.ShapeDtypeStruct((words, filters), bf16),
            jax.ShapeDtypeStruct((words, filters), bf16),
            jax.ShapeDtypeStruct((words, filters), f32),
            jax.ShapeDtypeStruct((8, 2 * filters), f32),
            jax.ShapeDtypeStruct((half, words, filters), f32),
            jax.ShapeDtypeStruct((half, words, filters), bf16),
        ],
        in_specs=[SMEM_SPEC]
        + [row] * 4
        + [pl.BlockSpec(weights.shape, lambda i: (0, 0, 0, 0))],
        out_specs=[row, row, row, pl.BlockSpec((8, 2 * filters), lambda i: (0, 0)), blocks, blocks],
        name=f"highway_back{layer}",
        cost_estimate=cost(2 * words * filters * PLANE * 2 * filters, 20e6),
        compiler_params=pltpu.CompilerParams(vmem_limit_bytes=58 * 1024 * 1024),
    )(dvec, d_hidden, opened, ra, hidden, weights)


def highway_grad_body(d_ref, *refs):
    blocks = refs[:PLANE]
    ga_ref, gb_ref = refs[PLANE : PLANE + 2]
    outs = refs[PLANE + 2 :]
    d = d_ref[0]
    filters = ga_ref.shape[1]
    for k in range(PLANE):
        for side, grad_ref in enumerate((ga_ref, gb_ref)):
            cols = slice(side * filters, (side + 1) * filters)
            piece = tn(blocks[k][...], grad_ref[...]).astype(bf16)
            if len(outs) == 1:
                outs[0][:, d ^ k, :, cols] = piece.reshape(DEPTH, filters // DEPTH, filters)
            else:
                rows = filters // len(outs)
                for i, out_ref in enumerate(outs):
                    out_ref[d ^ k, :, cols] = piece[i * rows : (i + 1) * rows]


def spread_groups(char_len, filters, grad, at, spread_ref, group):
    count = min(GROUP, char_len - GROUP * group)
    for place in range(count):
        hit = at == GROUP * group + place
        spread_ref[:, place * filters : (place + 1) * filters] = jnp.where(hit, grad, 0.0).astype(
            bf16
        )
    return count


def char_back_body(char_len, words, d_ref, h_ref, at_ref, dh_ref, weight_ref, widths_ref, gp_ref, keep_ref, send_ref, taps_ref, spread_ref, chars_ref):
    d = d_ref[0]
    filters = h_ref.shape[1]
    lanes = taps_ref.shape[0] // 2
    held = keep_ref.shape[2]
    fill_taps(d, taps_ref, weight_ref, widths_ref)
    chars_ref[...] = jnp.zeros_like(chars_ref)

    def one(step, carry):
        rows = pl.ds(pl.multiple_of(step * 2 * words, 2 * words), 2 * words)
        grad = jnp.where(h_ref[rows, :] > 0.0, dh_ref[rows, :], 0.0).astype(bf16)
        gp_ref[rows, :] = grad
        grad = grad.astype(f32)
        at = at_ref[rows, :]
        for group in range(-(-char_len // GROUP)):
            count = spread_groups(char_len, filters, grad, at, spread_ref, group)
            piece = nt(spread_ref[:, : count * filters], taps_ref[:, : count * filters])
            chars_ref[rows, group * lanes : (group + 2) * lanes] += piece
        return carry

    lax.fori_loop(0, PLANE // 2, one, 0)
    for i in range(PLANE // 2):
        for odd, out in ((1, send_ref), (0, keep_ref)):
            rows = pl.ds(pl.multiple_of((d ^ odd ^ (2 * i)) * words, words), words)
            out[i] = chars_ref[rows, :held].astype(out.dtype)


def conv_grad_body(char_len, d_ref, x_ref, at_ref, gp_ref, dw_ref, spread_ref, xt_ref):
    filters = gp_ref.shape[1]
    lanes = 128
    depth = dw_ref.shape[0] - 8
    char_dim = lanes // GROUP
    grad = gp_ref[...].astype(f32)
    at = at_ref[...]
    groups = -(-char_len // GROUP)
    dw_ref[...] = jnp.zeros_like(dw_ref)
    for group in range(groups):
        count = spread_groups(char_len, filters, grad, at, spread_ref, group)
        piece = tn(x_ref[:, group * lanes : (group + 2) * lanes], spread_ref[:, : count * filters])
        for place in range(count):
            dw_ref[:depth, :] += piece[
                place * char_dim : place * char_dim + depth,
                place * filters : (place + 1) * filters,
            ]
    total = jnp.sum(grad.reshape(-1, 8, filters), axis=0)
    dw_ref[depth:, :] = jnp.broadcast_to(jnp.sum(total, axis=0, keepdims=True), (8, filters))


def table_grad_body(char_len, d_ref, ids_ref, chars_ref, out_ref):
    words = ids_ref.shape[1]
    lanes = 128
    width = lanes // GROUP
    rows = out_ref.shape[0] * GROUP
    groups = -(-char_len // GROUP)
    entry = lax.broadcasted_iota(jnp.int32, (rows, words), 0)
    lane = lax.broadcasted_iota(jnp.int32, (rows, lanes), 1) // width
    stacked = jnp.concatenate(
        [chars_ref[:, group * lanes : (group + 1) * lanes] for group in range(groups)], axis=0
    ).astype(bf16)
    total = jnp.zeros((rows, lanes), f32)
    for place in range(GROUP):
        pieces = []
        for group in range(groups):
            at = GROUP * group + place
            if at < char_len:
                pieces.append(jnp.where(ids_ref[at : at + 1, :] == entry, 1.0, 0.0).astype(bf16))
            else:
                pieces.append(jnp.zeros((rows, words), bf16))
        found = nn(jnp.concatenate(pieces, axis=1), stacked)
        total = total + jnp.where(lane == place, found, 0.0)
    step = width
    while step < lanes:
        total = total + pltpu.roll(total, step, 1)
        step *= 2
    part = out_ref.shape[0]
    fold = jnp.zeros(out_ref.shape, f32)
    lane = lax.broadcasted_iota(jnp.int32, out_ref.shape, 1) // width
    for place in range(GROUP):
        fold = fold + jnp.where(lane == place, total[place * part : (place + 1) * part], 0.0)
    out_ref[...] = fold


def pack_highway_body(carry_ref, gate_ref, *outs):
    for layer, out_ref in enumerate(outs):
        out_ref[0, 0] = carry_ref[layer]
        out_ref[0, 1] = gate_ref[layer]


def pack_highway(weights):
    layers, rows, columns = weights.shape
    own = columns // (2 * PLANE)
    block = (layers, rows, own)
    return pl.pallas_call(
        pack_highway_body,
        grid=(PLANE,),
        out_shape=[jax.ShapeDtypeStruct((PLANE, 2, rows, own), bf16)] * layers,
        in_specs=[
            pl.BlockSpec(block, lambda j: (0, 0, j)),
            pl.BlockSpec(block, lambda j: (0, 0, PLANE + j)),
        ],
        out_specs=[pl.BlockSpec((1, 2, rows, own), lambda j: (j, 0, 0, 0))] * layers,
        name="pack_highway",
    )(weights, weights)


def pack_encoder_body(qkv_ref, out_ref, inner_ref, outer_ref, packed_ref):
    dim = packed_ref.shape[1]
    at = 0
    for ref in (qkv_ref, out_ref, inner_ref, outer_ref):
        rows = ref.shape[0]
        for start in range(0, ref.shape[1], dim):
            packed_ref[at : at + rows, :] = ref[:, start : start + dim]
            at += rows


def finish_highway_body(count, *refs):
    out_ref = refs[-1]
    half = out_ref.shape[2] // 2
    own = half // PLANE
    low = 0
    for ref in refs[:count]:
        rows = out_ref.shape[1] // count
        for j in range(PLANE):
            for side in range(2):
                at = slice(j * own + side * half, (j + 1) * own + side * half)
                cols = slice(side * own, (side + 1) * own)
                piece = ref[j, :, cols] if len(ref.shape) == 3 else ref[:, j, :, cols]
                out_ref[0, low : low + rows, at] = piece.reshape(rows, own).astype(f32)
        low += rows


def finish_highway(layer, layers, pieces, previous):
    own = pieces[0].shape[-1] // 2
    width = 2 * PLANE * own
    operands = list(pieces)
    specs = [pl.BlockSpec(x.shape, lambda i, n=x.ndim: (0,) * n) for x in pieces]
    aliases = {}
    if previous is not None:
        aliases = {len(operands): 0}
        operands.append(previous)
        specs.append(pl.BlockSpec(memory_space=pl.ANY))
    return pl.pallas_call(
        functools.partial(finish_highway_body, len(pieces)),
        grid=(1,),
        out_shape=jax.ShapeDtypeStruct((layers, own, width), f32),
        in_specs=specs,
        out_specs=pl.BlockSpec((1, own, width), lambda i: (layer, 0, 0)),
        input_output_aliases=aliases,
        name=f"finish_highway{layer}",
        compiler_params=pltpu.CompilerParams(vmem_limit_bytes=58 * 1024 * 1024),
    )(*operands)


def finish_ends_body(d_ref, *refs):
    blocks = refs[:PLANE]
    widths_ref, conv_ref, bias_ref, gates_ref, table_ref, held_ref = refs[PLANE:]
    d = d_ref[0]
    own = blocks[0].shape[1]
    rows = conv_ref.shape[0]
    lanes = table_ref.shape[1]
    char_dim = lanes // GROUP
    tap = lax.broadcasted_iota(jnp.int32, (rows, own), 0) // char_dim
    for k in range(PLANE):
        cols = pl.ds(pl.multiple_of((d ^ k) * own, own), own)
        conv_ref[:, cols] = jnp.where(tap < widths_ref[:, cols], blocks[k][:rows, :], 0.0)
        bias_ref[:, cols] = blocks[k][rows : rows + 8, :]
        gates_ref[:, cols] = blocks[k][rows + 8 : rows + 16, :]
        held_ref[d ^ k] = blocks[k][rows + 16 :, :lanes]
    total = held_ref[0]
    for j in range(1, PLANE):
        total = total + held_ref[j]
    table_ref[...] = total


def finish_encoder_body(middle_ref, whole_ref, third_ref, *outs):
    middle = middle_ref[0] == 1
    dim = whole_ref.shape[1]
    at = 0
    for ref in outs:
        count = ref.shape[0]
        for left in range(0, ref.shape[1], dim):
            rows = slice(at, at + count)
            ref[:, left : left + dim] = jnp.where(
                middle, whole_ref[rows].astype(f32), third_ref[rows].astype(f32)
            )
            at += count


def corner(value):
    return value.reshape((-1,) + value.shape[-2:])[0, :16, :128]


def normalize(value):
    mean = jnp.mean(value, axis=-1, keepdims=True)
    centred = value - mean
    spread = jnp.mean(centred * centred, axis=-1, keepdims=True)
    scale = lax.rsqrt(spread + eps_norm)
    return centred * scale, scale


def normalize_back(grad, normal, scale, gain):
    moved = grad * gain
    return (
        moved
        - jnp.mean(moved, axis=-1, keepdims=True)
        - normal * jnp.mean(moved * normal, axis=-1, keepdims=True)
    ) * scale


def over_words(value):
    return jnp.sum(value, axis=0, keepdims=True)


def encoder_body(
    head_count,
    in_parts,
    flag_ref,
    emb_ref,
    e1_ref,
    e2_ref,
    e3_ref,
    small_ref,
    qseg_ref,
    kseg_ref,
    kpad_ref,
    cot_ref,
    w_hbm,
    result_ref,
    d_own_ref,
    send1_ref,
    send2_ref,
    send3_ref,
    embs_ref,
    gq_ref,
    gk_ref,
    gv_ref,
    att_ref,
    gattn_ref,
    first_ref,
    act_ref,
    gup_ref,
    gdown_ref,
    stats_ref,
    w_ref,
    q_ref,
    k_ref,
    v_ref,
    p_ref,
    up_ref,
    gatt_ref,
    sems,
):
    words, dim = emb_ref.shape
    part = dim // PLANE
    wide = act_ref.shape[1] // PLANE
    cuts = [0, 3 * part, 4 * part, (4 + in_parts) * part, (4 + in_parts) * part + wide]
    copies = [
        pltpu.make_async_copy(
            w_hbm.at[:, low:high, :], w_ref.at[:, low:high, :], sems.at[i]
        )
        for i, (low, high) in enumerate(zip(cuts, cuts[1:]))
    ]
    for copy in copies:
        copy.start()
    pair = 2 * HDIM
    scale = HDIM ** (-0.5)

    def square(i):
        return w_ref[:, i * part : (i + 1) * part, :].reshape(dim, dim)

    def small(i):
        return small_ref[i : i + 1, :]

    emb = emb_ref[...]
    emb_b = emb.astype(bf16)
    embs_ref[:words] = emb_b
    for i, ref in enumerate((e1_ref, e2_ref, e3_ref)):
        embs_ref[(i + 1) * words : (i + 2) * words] = ref[...]
    copies[0].wait()
    q_ref[...] = (nn(emb_b, square(0)) + small(1)).astype(bf16)
    k_ref[...] = nn(embs_ref[...], square(1)).astype(bf16)
    v_ref[...] = (nn(embs_ref[...], square(2)) + small(2)).astype(bf16)
    keys = k_ref.shape[0]
    row = lax.broadcasted_iota(jnp.int32, (words, keys), 0)
    column = lax.broadcasted_iota(jnp.int32, (words, keys), 1)
    allowed = (qseg_ref[...] == kseg_ref[...]) & ((kpad_ref[...] == 0) | (row == column))
    low_lane = lax.broadcasted_iota(jnp.int32, (1, pair), 1) < HDIM

    def of_head(value, side):
        keep = low_lane if side == 0 else jnp.logical_not(low_lane)
        return jnp.where(keep, value.astype(f32), 0.0).astype(bf16)

    for at in range(head_count // 2):
        cols = slice(at * pair, (at + 1) * pair)
        outs = []
        for side in range(2):
            scores = nt(of_head(q_ref[:, cols], side), k_ref[:, cols]) * scale
            scores = jnp.where(allowed, scores, masked_score)
            top = jnp.max(scores, axis=-1, keepdims=True)
            raised = jnp.exp(scores - top)
            probs = raised / jnp.sum(raised, axis=-1, keepdims=True)
            p_ref[2 * at + side] = probs
            outs.append(nn(probs.astype(bf16), v_ref[:, cols]))
        att_ref[:, cols] = jnp.where(low_lane, outs[0], outs[1]).astype(bf16)
    copies[1].wait()
    attn_out = nn(att_ref[...], square(3)) + small(3)
    normal1, scale1 = normalize(emb + attn_out)
    first = normal1 * small(6) + small(9)
    first_b = first.astype(bf16)
    first_ref[...] = first_b
    copies[2].wait()
    half_root = math.sqrt(0.5)
    for i in range(in_parts):
        cols = slice(i * dim, (i + 1) * dim)
        up = nn(first_b, square(4 + i)) + small(11 + i)
        up_ref[:, cols] = up
        act_ref[:, cols] = (0.5 * up * (1.0 + lax.erf(up * half_root))).astype(bf16)
    copies[3].wait()
    low = cuts[3]
    outer = w_ref[:, low : low + wide, :].reshape(PLANE * wide, dim)
    second = first + (nn(act_ref[...], outer) + small(4))
    normal2, scale2 = normalize(second)
    result_ref[...] = (normal2 * small(7) + small(10)).astype(bf16)

    grad = cot_ref[...].astype(f32)
    d_second = normalize_back(grad, normal2, scale2, small(7))
    stats_ref[...] = jnp.zeros_like(stats_ref)
    stats_ref[7:8] = over_words(grad * normal2)
    stats_ref[10:11] = over_words(grad)
    gdown = d_second.astype(bf16)
    gdown_ref[...] = gdown
    stats_ref[4:5] = over_words(gdown.astype(f32))
    d_first = d_second
    density = 1.0 / math.sqrt(2.0 * math.pi)
    per = dim // wide
    for i in range(in_parts):
        cols = slice(i * dim, (i + 1) * dim)
        block = w_ref[i * per : (i + 1) * per, low : low + wide, :].reshape(dim, dim)
        up = up_ref[:, cols]
        slope = 0.5 * (1.0 + lax.erf(up * half_root)) + up * (
            density * jnp.exp(-0.5 * up * up)
        )
        gup = (nt(gdown, block) * slope).astype(bf16)
        gup_ref[:, cols] = gup
        stats_ref[11 + i : 12 + i] = over_words(gup.astype(f32))
        d_first = d_first + nt(gup, square(4 + i))
    stats_ref[6:7] = over_words(d_first * normal1)
    stats_ref[9:10] = over_words(d_first)
    d_res = normalize_back(d_first, normal1, scale1, small(6))
    gattn = d_res.astype(bf16)
    gattn_ref[...] = gattn
    stats_ref[3:4] = over_words(gattn.astype(f32))
    gatt_ref[...] = nt(gattn, square(3)).astype(bf16)
    for at in range(head_count // 2):
        cols = slice(at * pair, (at + 1) * pair)
        dq, dk, dv = [], None, None
        for side in range(2):
            gatt = of_head(gatt_ref[:, cols], side)
            probs = p_ref[2 * at + side]
            d_probs = nt(gatt, v_ref[:, cols])
            inner = jnp.sum(probs * d_probs, axis=-1, keepdims=True)
            gscore = (probs * (d_probs - inner)).astype(bf16)
            dq.append(nn(gscore, k_ref[:, cols]))
            more_k = tn(gscore, of_head(q_ref[:, cols], side))
            more_v = tn(probs.astype(bf16), gatt)
            dk = more_k if dk is None else dk + more_k
            dv = more_v if dv is None else dv + more_v
        gq_ref[:, cols] = (jnp.where(low_lane, dq[0], dq[1]) * scale).astype(bf16)
        gk_ref[:, cols] = (dk * scale).astype(bf16)
        gv_ref[:, cols] = dv.astype(bf16)
    stats_ref[1:2] = over_words(gq_ref[...].astype(f32))
    stats_ref[2:3] = over_words(gv_ref[...].astype(f32))
    for i in range(DEPTH):
        rows = slice(i * words, (i + 1) * words)
        piece = nt(gk_ref[rows, :], square(1)) + nt(gv_ref[rows, :], square(2))
        if i == 0:
            d_own_ref[...] = d_res + nt(gq_ref[...], square(0)) + piece
        else:
            (send1_ref, send2_ref, send3_ref)[i - 1][...] = piece.astype(bf16)


def encoder_grad_body(
    flag_ref,
    embs_ref,
    gq_ref,
    gk_ref,
    gv_ref,
    att_ref,
    gattn_ref,
    first_ref,
    act_ref,
    gup_ref,
    gdown_ref,
    stats_ref,
    out_hbm,
    out_ref,
    sems,
):
    words, dim = gq_ref.shape
    part = dim // PLANE
    wide = act_ref.shape[1] // PLANE
    in_parts = gup_ref.shape[1] // dim
    pieces = []

    def put(low, high, value):
        out_ref[:, low:high, :] = value.reshape(PLANE, high - low, dim)

    def send(low, high):
        copy = pltpu.make_async_copy(
            out_ref.at[:, low:high, :], out_hbm.at[:, low:high, :], sems.at[len(pieces)]
        )
        copy.start()
        pieces.append(copy)

    low = (4 + in_parts) * part
    per = dim // wide
    for i in range(in_parts):
        cols = slice(i * dim, (i + 1) * dim)
        out_ref[i * per : (i + 1) * per, low : low + wide, :] = (
            tn(act_ref[:, cols], gdown_ref[...]).astype(bf16).reshape(per, wide, dim)
        )
    tail = jnp.broadcast_to(stats_ref[...].astype(bf16)[None], (PLANE,) + stats_ref.shape)
    out_ref[:, low + wide :, :] = tail
    send(low, out_ref.shape[1])
    for i in range(in_parts):
        cols = slice(i * dim, (i + 1) * dim)
        put((4 + i) * part, (5 + i) * part, tn(first_ref[...], gup_ref[:, cols]).astype(bf16))
    send(4 * part, low)
    put(3 * part, 4 * part, tn(att_ref[...], gattn_ref[...]).astype(bf16))
    put(0, part, tn(embs_ref[:words, :], gq_ref[...]).astype(bf16))
    put(part, 2 * part, tn(embs_ref[...], gk_ref[...]).astype(bf16))
    put(2 * part, 3 * part, tn(embs_ref[...], gv_ref[...]).astype(bf16))
    send(0, 4 * part)
    for copy in pieces:
        copy.wait()


def encoder(flag, embedded, others, small, query_segs, key_segs, key_pads, cotangent, weights):
    words, dim = embedded.shape
    keys = DEPTH * words
    head_count = dim // HDIM
    part = dim // PLANE
    in_parts = 4
    ff_dim = in_parts * dim
    vmem = pl.BlockSpec(memory_space=pltpu.VMEM)
    hbm = pl.BlockSpec(memory_space=pl.ANY)
    shapes = [
        ((words, dim), bf16),
        ((words, dim), f32),
        ((words, dim), bf16),
        ((words, dim), bf16),
        ((words, dim), bf16),
        ((keys, dim), bf16),
        ((words, dim), bf16),
        ((keys, dim), bf16),
        ((keys, dim), bf16),
        ((words, dim), bf16),
        ((words, dim), bf16),
        ((words, dim), bf16),
        ((words, ff_dim), bf16),
        ((words, ff_dim), bf16),
        ((words, dim), bf16),
        ((16, dim), f32),
    ]
    outs = pl.pallas_call(
        functools.partial(encoder_body, head_count, in_parts),
        out_shape=[jax.ShapeDtypeStruct(s, t) for s, t in shapes],
        in_specs=[SMEM_SPEC] + [vmem] * 9 + [hbm],
        out_specs=[vmem] * len(shapes),
        scratch_shapes=[
            VMEM(weights.shape, bf16),
            VMEM((words, dim), bf16),
            VMEM((keys, dim), bf16),
            VMEM((keys, dim), bf16),
            VMEM((head_count, words, keys), f32),
            VMEM((words, ff_dim), f32),
            VMEM((words, dim), bf16),
            pltpu.SemaphoreType.DMA((4,)),
        ],
        name="encoder",
        cost_estimate=cost(16e9, 30e6),
        compiler_params=pltpu.CompilerParams(vmem_limit_bytes=58 * 1024 * 1024),
    )(flag, embedded, *others, small, query_segs, key_segs, key_pads, cotangent, weights)
    result, d_own = outs[:2]
    d_embedded = d_own
    first = None
    for offset in range(1, DEPTH):
        piece = swap(outs[1 + offset], "seq", DEPTH, offset)
        first = piece if first is None else first
        d_embedded = d_embedded + piece.astype(f32)
    saved = [tie(outs[5], first), *outs[6:]]
    rows = (4 + in_parts) * part + ff_dim // PLANE + 16
    grads = pl.pallas_call(
        encoder_grad_body,
        out_shape=jax.ShapeDtypeStruct((PLANE, rows, dim), bf16),
        in_specs=[SMEM_SPEC] + [vmem] * 11,
        out_specs=hbm,
        scratch_shapes=[VMEM((PLANE, rows, dim), bf16), pltpu.SemaphoreType.DMA((3,))],
        name="encoder_grad",
        cost_estimate=cost(6e9, 20e6),
        compiler_params=pltpu.CompilerParams(vmem_limit_bytes=58 * 1024 * 1024),
    )(flag, *saved)
    return result, tie(d_embedded, grads), grads


def round_up(value, multiple):
    return -(-value // multiple) * multiple


def plane_shards(
    char_ids,
    segment_ids,
    pad_mask,
    cotangent,
    char_table,
    conv_weight,
    conv_bias,
    hw_weight,
    hw_bias,
    proj_weight,
    pos_table,
    qkv_weight,
    out_weight,
    ff_in_weight,
    ff_out_weight,
    ff_in_bias,
    d_biases,
    norm_gain,
    norm_shift,
):
    d = lax.axis_index("dp")
    z = lax.axis_index("seq")
    dvec = d.astype(jnp.int32)[None]
    words, char_len = char_ids.shape[1:]
    all_words = PLANE * words
    tap_count, char_dim, filters = conv_weight.shape
    chars = char_table.shape[0]
    own = filters // PLANE
    depth = hw_weight.shape[0]
    model_dim = cotangent.shape[2]
    seq_len = segment_ids.shape[1]
    head_count = model_dim // HDIM
    part = model_dim // PLANE
    ff_dim = ff_out_weight.shape[0] * PLANE
    lanes = GROUP * char_dim
    held = round_up(char_len * char_dim, lanes)
    score_scale = HDIM ** (-0.5)

    ids = char_ids.reshape(words, char_len)
    table_rows = round_up(chars, 128)
    table = jnp.pad(jnp.tile(char_table, (1, GROUP)), ((0, table_rows - chars), (0, 0)))
    (own_x,) = call(
        functools.partial(lookup_body, char_len),
        [((words + EXTRA_ROWS, held), bf16)],
        z.astype(jnp.int32)[None],
        (ids, table, hw_bias, d_biases, norm_gain, norm_shift, ff_in_bias[None, :], pos_table),
        [VMEM((EXTRA_ROWS, held), f32)],
        name="lookup",
    )
    hw_weight, qkv_weight, unused = lax.optimization_barrier((hw_weight, qkv_weight, own_x))
    hw_packed = pack_highway(hw_weight)

    x_blocks = plane_gather(own_x, hw_packed)
    hw_cols = [lax.all_to_all(tie(hw_packed[0], x_blocks[2]), "dp", 0, 0)]

    in_parts = ff_in_weight.shape[1] // model_dim
    weight_rows = (4 + in_parts) * part + ff_dim // PLANE
    packed = pl.pallas_call(
        pack_encoder_body,
        out_shape=jax.ShapeDtypeStruct((weight_rows, model_dim), bf16),
        name="pack_encoder",
    )(qkv_weight, out_weight, ff_in_weight, ff_out_weight)
    widths = filter_widths(filters)
    widths_row = jnp.asarray(widths[None, :], jnp.int32)
    taps = conv_weight.reshape(tap_count * char_dim, filters)
    taps_shape = VMEM((2 * lanes, GROUP * own), bf16)
    hidden0, hidden0_b, top_at, x_all, bias_a, bias_b, extras = call(
        functools.partial(conv_body, char_len, char_len - tap_count + 1, words),
        [
            ((all_words, own), f32),
            ((all_words, own), bf16),
            ((all_words, own), jnp.int32),
            ((all_words, held + lanes), bf16),
            ((16, own), f32),
            ((16, own), f32),
            ((PLANE, EXTRA_ROWS, held), bf16),
        ],
        dvec,
        (*x_blocks, taps, widths_row, conv_bias[None, :]),
        [taps_shape, VMEM((PLANE, 16, 2 * own), f32)],
        name="conv",
        flops=8e9,
    )

    hidden, hidden_b = hidden0, hidden0_b
    saved = []
    for layer in range(depth):
        blocks = plane_gather(hidden_b, (hw_cols[layer],))
        if layer + 1 < depth:
            following, packed = tie((hw_packed[layer + 1], packed), blocks)
            hw_cols.append(lax.all_to_all(following, "dp", 0, 0))
        if layer == 0:
            gathered = lax.all_gather(packed, "dp", axis=0, tiled=False)
        opened, ra, following, following_b = highway(
            layer, dvec, blocks, hw_cols[layer], bias_a, bias_b, hidden
        )
        saved.append((blocks, opened, ra, hidden))
        hidden, hidden_b = following, following_b
    vectors = extras[:, VECTOR_ROW : VECTOR_ROW + 11, :part].astype(f32)
    inner_bias = extras[:, VECTOR_ROW + 11, : ff_dim // PLANE].reshape(in_parts, model_dim)
    small_full = jnp.concatenate(
        [
            vectors.transpose(1, 0, 2).reshape(11, model_dim),
            inner_bias.astype(f32),
            jnp.zeros((16 - 11 - in_parts, model_dim), f32),
        ],
        axis=0,
    )
    per = EXTRA_ROWS - POS_ROW
    pos_full = (
        extras[:, POS_ROW:, : (words // per) * part]
        .reshape(PLANE, per, words // per, part)
        .transpose(2, 1, 0, 3)
        .reshape(words, model_dim)
    )

    half = PLANE // 2
    keep, send = call(
        project_body,
        [((half, words, model_dim), f32), ((half, words, model_dim), bf16)],
        dvec,
        (hidden_b, proj_weight),
        name="project",
    )
    projected = plane_reduce(keep, send) + small_full[0]

    summed = projected + pos_full.astype(f32)
    normal0, scale0 = normalize(summed)
    embedded = normal0 * small_full[5] + small_full[8]
    embedded_b = embedded.astype(bf16)
    others = [swap(embedded_b, "seq", DEPTH, offset) for offset in range(1, DEPTH)]

    def by_offset(row):
        pieces = row.reshape(DEPTH, words)
        return jnp.concatenate(
            [lax.dynamic_index_in_dim(pieces, z ^ offset, 0) for offset in range(DEPTH)], axis=1
        )

    key_segs, key_pads = by_offset(segment_ids), by_offset(pad_mask)
    result, d_embedded, enc_grads = encoder(
        dvec,
        embedded,
        others,
        small_full,
        key_segs[0, :words, None],
        key_segs,
        key_pads,
        cotangent.reshape(words, model_dim),
        gathered,
    )
    enc_slice = lax.psum_scatter(enc_grads, "dp", scatter_dimension=0, tiled=True)[0]
    d_summed = normalize_back(d_embedded, normal0, scale0, small_full[5])
    grad_proj = jnp.concatenate(
        [
            d_summed.astype(bf16),
            over_words(d_embedded * normal0).astype(bf16),
            over_words(d_embedded).astype(bf16),
            jnp.zeros((14, model_dim), bf16),
        ],
        axis=0,
    )

    gp_blocks = plane_gather(grad_proj)
    d_hidden, proj_grad, top_sums = call(
        functools.partial(unproject_body, words),
        [((all_words, own), f32), ((own, model_dim), bf16), ((words + 32, model_dim), f32)],
        dvec,
        (*gp_blocks, proj_weight, hidden_b),
        name="unproject",
    )
    top_own = lax.dynamic_slice_in_dim(top_sums, d * part, part, 1)
    top_own = jnp.pad(top_own, ((0, 0), (0, 128 - part)))
    wide_rows = round_up(round_up(seq_len + 32, model_dim // 128) // (model_dim // 128), 16)
    top_all = lax.dynamic_update_slice_in_dim(
        jnp.zeros((wide_rows * (model_dim // 128), 128), f32), top_own[words:], seq_len, 0
    )
    top_all = lax.dynamic_update_slice_in_dim(top_all, top_own[:words], z * words, 0).astype(bf16)
    top_all = jnp.concatenate(jnp.split(top_all, model_dim // 128), axis=1)
    cut = (4 + in_parts) * part
    gate_parts = {}
    middle = (z == 1) | (z == 2)
    chain = None
    for layer in reversed(range(depth)):
        blocks, opened, ra, hidden = saved[layer]
        ga, gb, d_carry, sums, keep, send = highway_back(
            layer, dvec, d_hidden, opened, ra, hidden, hw_cols[layer]
        )
        parts = plane_parts(keep, send)
        gate_parts[layer] = jnp.sum(sums, axis=0).reshape(2, own)
        others = plane_others(parts)
        if layer == 0:
            enc_slice = tie(enc_slice, parts[1])
            chain[1] = chain[1] + tie(steps[1], others[0])
            steps[1] = line_step(chain[1], 1)
        shapes = (
            [((DEPTH, PLANE, own // DEPTH, 2 * own), bf16)]
            if layer == 0
            else [((PLANE, own // 2, 2 * own), bf16)] * 2
        )
        grads = call(
            highway_grad_body,
            shapes,
            dvec,
            (*blocks, tie(ga, parts[1]), gb),
            name=f"highway_grad{layer}",
            flops=2 * all_words * filters * 2 * own,
        )
        if layer == 0:
            quarter = lax.psum_scatter(
                tie(grads[0], enc_slice), "seq", scatter_dimension=0, tiled=False
            )
            quarter = lax.all_to_all(quarter, "dp", 0, 0)
            lowest = lax.all_gather(quarter, "seq", axis=0, tiled=False)
            chain[0] = chain[0] + tie(steps[0], grads[0], others[0])
            steps[0] = line_step(chain[0], 2)
            after = [grads[0], enc_slice, *chain]
        else:
            chain = list(grads)
            steps = [line_step(value, 0) for value in chain]
            chain[0] = chain[0] + tie(steps[0], parts[1])
            steps[0] = line_step(chain[0], 1)
            after = [*grads, chain[0]]
        d_hidden = d_carry + plane_total(parts, after, others)
    lines = [enc_slice[:cut], jnp.concatenate([enc_slice[cut:], proj_grad, top_all], axis=0)]
    moved = [line_step(value, 0) for value in lines]
    d_hidden = tie(d_hidden, *lines)

    grad_pooled, keep, send = call(
        functools.partial(char_back_body, char_len, words),
        [
            ((all_words, own), bf16),
            ((half, words, held), f32),
            ((half, words, held), bf16),
        ],
        dvec,
        (hidden0, top_at, d_hidden, taps, widths_row),
        [
            taps_shape,
            VMEM((2 * words, GROUP * own), bf16),
            VMEM((all_words, held + lanes), f32),
        ],
        name="char_back",
        flops=8e9,
    )
    parts = plane_parts(keep, send)
    chain[1] = chain[1] + tie(steps[1], parts[1])
    steps[1] = line_step(chain[1], 2)
    grad_pooled = tie(grad_pooled, parts[1], chain[1])
    (conv_part,) = call(
        functools.partial(conv_grad_body, char_len),
        [((tap_count * char_dim + 8, own), f32)],
        dvec,
        (x_all, top_at, grad_pooled),
        [VMEM((all_words, GROUP * own), bf16), VMEM((2 * lanes, all_words), bf16)],
        name="conv_grad",
        flops=8e9,
    )
    lines = [value + tie(piece, conv_part) for value, piece in zip(lines, moved)]
    moved = [line_step(value, 1) for value in lines]
    char_grads = plane_total(parts, (conv_part, *lines))
    fold_rows = round_up(-(-chars // GROUP), 8)
    (table_part,) = call(
        functools.partial(table_grad_body, char_len),
        [((fold_rows, lanes), f32)],
        dvec,
        (ids.T, char_grads),
        name="table_grad",
        flops=2e9,
    )
    gate_rows = jnp.concatenate([gate_parts[layer] for layer in range(depth)], axis=0)
    ends = jnp.concatenate(
        [
            conv_part,
            jnp.pad(gate_rows, ((0, 8 - 2 * depth), (0, 0))),
            jnp.pad(table_part, ((0, 0), (0, own - lanes))),
        ],
        axis=0,
    )
    ends = ends + swap(ends, "seq", DEPTH, 1)
    ends = ends + swap(ends, "seq", DEPTH, 2)
    end_blocks = plane_gather(ends)
    conv_rows = tap_count * char_dim
    conv_total, conv_bias_total, gate_sums, table_total = call(
        finish_ends_body,
        [
            ((conv_rows, filters), f32),
            ((8, filters), f32),
            ((8, filters), f32),
            ((fold_rows, lanes), f32),
        ],
        dvec,
        (*end_blocks, widths_row),
        [VMEM((PLANE, fold_rows, lanes), f32)],
        name="finish_ends",
    )
    conv_total = conv_total.reshape(tap_count, char_dim, filters)
    conv_bias_total = conv_bias_total[0]
    table_total = (
        table_total.reshape(fold_rows, GROUP, char_dim)
        .transpose(1, 0, 2)
        .reshape(GROUP * fold_rows, char_dim)[:chars]
    )

    lines = [value + tie(piece, ends) for value, piece in zip(lines, moved)]
    moved = [line_step(value, 2) for value in lines]
    middle_flag = middle.astype(jnp.int32)[None]
    outer_total, small_total, proj_total, top_total = call(
        finish_encoder_body,
        [
            ((ff_dim // PLANE, model_dim), f32),
            ((16, model_dim), f32),
            ((own, model_dim), f32),
            ((wide_rows, model_dim), f32),
        ],
        middle_flag,
        (lines[1], moved[1]),
        name="finish_high",
    )
    top_total = jnp.concatenate(jnp.split(top_total, model_dim // 128, axis=1))[:, :part]
    pos_total = top_total[:seq_len]
    gain0, shift0, bias0 = top_total[seq_len], top_total[seq_len + 1], top_total[seq_len + 16]
    own_small = lax.dynamic_slice_in_dim(small_total, d * part, part, 1)
    bias_total = jnp.concatenate([bias0[None], own_small[1:5]], axis=0)
    gain_total = jnp.concatenate([gain0[None], own_small[6:8]], axis=0)
    shift_total = jnp.concatenate([shift0[None], own_small[9:11]], axis=0)
    inner_bias_total = lax.dynamic_slice_in_dim(
        small_total[11 : 11 + in_parts].reshape(-1), d * (ff_dim // PLANE), ff_dim // PLANE, 0
    )

    chain = [
        jnp.where(middle, value, tie(piece, table_part)) for value, piece in zip(chain, steps)
    ]
    pieces = [lax.all_to_all(value, "dp", 0, 0) for value in chain]
    hw_total = finish_highway(1, depth, pieces, None)
    hw_total = finish_highway(0, depth, [lowest], hw_total)
    qkv_total, out_total, inner_total = call(
        finish_encoder_body,
        [((part, 3 * model_dim), f32), ((part, model_dim), f32), ((part, ff_dim), f32)],
        middle_flag,
        (lines[0], tie(moved[0], corner(hw_total), outer_total[:8, :128])),
        name="finish_low",
    )
    hw_bias_totals = []
    for layer in range(depth):
        row = gate_sums[2 * layer : 2 * layer + 2].reshape(-1)
        hw_bias_totals.append(lax.dynamic_slice_in_dim(row, d * 2 * own, 2 * own, 0))

    output = result.reshape(1, words, model_dim)
    return (
        output,
        table_total,
        conv_total,
        conv_bias_total,
        hw_total,
        jnp.stack(hw_bias_totals),
        proj_total,
        pos_total,
        qkv_total,
        out_total,
        inner_total,
        outer_total,
        inner_bias_total,
        bias_total,
        gain_total,
        shift_total,
    )


def solution(mesh):
    placed = (
        P("dp", "seq", None),
        P("dp", None),
        P("dp", None),
        P("dp", "seq", None),
        P(),
        P(),
        P(),
        P(None, "dp", None),
        P(None, "dp"),
        P("dp", None),
        P(None, "dp"),
        P("dp", None),
        P("dp", None),
        P("dp", None),
        P("dp", None),
        P("dp"),
        P(None, "dp"),
        P(None, "dp"),
        P(None, "dp"),
    )
    plane, depth = mesh.shape["dp"], mesh.shape["seq"]
    step = plane_shards if (plane, depth) == (PLANE, DEPTH) else shards
    return jax.shard_map(
        step,
        mesh=mesh,
        in_specs=placed,
        out_specs=(
            P("dp", "seq", None),
            P(),
            P(),
            P(),
            P(None, "dp", None),
            P(None, "dp"),
            P("dp", None),
            P(None, "dp"),
            P("dp", None),
            P("dp", None),
            P("dp", None),
            P("dp", None),
            P("dp"),
            P(None, "dp"),
            P(None, "dp"),
            P(None, "dp"),
        ),
        check_vma=False,
    )
```
